256 devices in a mesh: lon: 8 (over x, y_lo), lat: 8 (over z), lev: 4 (over y_hi, core).
Axes of the slice: x: 4, y: 4 (y_hi: 2, y_lo: 2; y = y_hi * 2 + y_lo), z: 8, core: 2. Of those that a mesh axis runs over, the one named last changes fastest.
Arguments:
- tokens_in: bfloat16 [4, 128, 128, 512], P('lev', 'lat', 'lon'), may hold values from -6 to 6
- cotangent: bfloat16 [4, 128, 128, 512], P('lev', 'lat', 'lon'), may hold values from -6 to 6
- qkv_weight: bfloat16 [512, 1536], replicated, may hold values from -5 to 5
- out_weight: bfloat16 [512, 512], replicated, may hold values from -0.25 to 0.25
- norm_gain: float32 [512], replicated, may hold values from 0.5 to 1.5
- ocean_mask: int32 [4, 128, 128], P('lev', 'lat', 'lon'), may hold values from 0 to 1, as said below
Outputs:
- layer_out: bfloat16 [4, 128, 128, 512], P('lev', 'lat', 'lon')
- input_grad: bfloat16 [4, 128, 128, 512], P('lev', 'lat', 'lon')
- qkv_grad: float32 [512, 1536], P('lev')
- out_grad: float32 [512, 512], P('lev')
- gain_grad: float32 [512], P('lev')
The draws below stay inside these ranges and needn't reach their ends.
Inputs may be any that keep to these rules, and one draw needn't show every extreme that they name: `ocean_mask`: at each level group, at most 3 of the windows of one device hold an ocean patch, and some device holds exactly 3 such windows.
All inputs are finite; a program needn't handle non-finite values.
Results may differ from the reference program's by a relative error of at most 0.017.
The reference program's roundings to bfloat16 on the way (of `hidden`, `projected`, `probabilities_low`, `mixed_out`, `grad_branch`, `grad_mixed`, `grad_scores` and `grad_qkv`) count: a program that leaves them out, or rounds other values in their place, can miss the bound.
Values may be sent and summed in bfloat16 or wider, within the bound.
A program may use at most 128 MiB of HBM per device.

```python
import jax
import jax.numpy as jnp
from jax import lax

D = 512
HEADS = 8
WIN = 8
WLAT = 2
WLON = 2
LEVG = 4
NLAT_P = 128
NLON_P = 128
OCEAN_MAX = 3


def draw_qkv_weight(key, part):
    values_out = jnp.clip(jax.random.normal(key, (D, 3 * D), jnp.float32), -5.0, 5.0) * D ** (-0.5)
    return values_out.astype(jnp.bfloat16)


def draw_ocean_mask(key, part):
    lat_tiles = NLAT_P // (WLAT * WIN)
    lon_tiles = NLON_P // (WLON * WIN)
    tile_count = LEVG * lat_tiles * lon_tiles
    window_count = WLAT * WLON
    keys_all = jax.random.split(key, 5)
    order_bits = jax.random.randint(keys_all[0], (tile_count, window_count), 0, 2 ** 30)
    ranking = jnp.argsort(jnp.argsort(order_bits, axis=1, stable=True), axis=1, stable=True)
    counts = jax.random.randint(keys_all[1], (tile_count,), max(1, OCEAN_MAX // 2), OCEAN_MAX + 1)
    fullest = jax.random.randint(keys_all[2], (), 0, tile_count)
    counts = jnp.where(jnp.arange(tile_count) == fullest, OCEAN_MAX, counts)
    alive_flag = ranking < counts[:, None]
    patches = jax.random.randint(keys_all[3], (tile_count, window_count, WIN * WIN), 0, 5) < 3
    forced = jax.random.randint(keys_all[4], (tile_count, window_count), 0, WIN * WIN)
    patches = patches | (jnp.arange(WIN * WIN)[None, None, :] == forced[..., None])
    ocean = (patches & alive_flag[..., None]).astype(jnp.int32)
    ocean = ocean.reshape(LEVG, lat_tiles, lon_tiles, WLAT, WLON, WIN, WIN)
    ocean = jnp.transpose(ocean, (0, 1, 3, 5, 2, 4, 6))
    return ocean.reshape(LEVG, NLAT_P, NLON_P)


def shard_levels(own_key, dims, cuts, low, high):
    def one(axis_at, parts):
        steps = jax.random.uniform(jax.random.fold_in(jax.random.fold_in(own_key, 6), axis_at), (parts,), jnp.float32, low / len(cuts), high / len(cuts))
        return jnp.repeat(jnp.exp(steps), dims[axis_at] // parts).reshape((-1,) + (1,) * (len(dims) - axis_at - 1))

    loudness = one(*cuts[0])
    for cut in cuts[1:]:
        loudness = loudness * one(*cut)
    return loudness


def bell_draw(rng, extent, scale, most, cuts=(), kind=jnp.bfloat16):
    factor_of = shard_levels(rng, extent, cuts, -0.22, 0.18) if cuts else 1.0
    array = jax.random.normal(rng, extent, jnp.float32) * scale * factor_of
    return jnp.minimum(jnp.maximum(array, -most), most).astype(kind)


def setup_inputs(seed: int = 0) -> dict:
    keys = jax.random.split(jax.random.key(seed), 7)
    return {
        "tokens_in": bell_draw(keys[0], (LEVG, NLAT_P, NLON_P, D), 1.0, 6.0, ((0, 4), (1, 8), (2, 8))),
        "cotangent": bell_draw(keys[1], (LEVG, NLAT_P, NLON_P, D), 1.0, 6.0, ((0, 4), (1, 8), (2, 8))),
        "qkv_weight": draw_qkv_weight(jax.random.fold_in(keys[6], 71), 0),
        "out_weight": bell_draw(keys[3], (D, D), D ** -0.5, 0.25),
        "norm_gain": jnp.clip(1.0 + 0.1 * jax.random.normal(keys[4], (D,), jnp.float32), 0.5, 1.5),
        "ocean_mask": draw_ocean_mask(jax.random.fold_in(keys[6], 71), 0),
    }


def norm_rows(values_in):
    center = values_in - lax.optimization_barrier(jnp.mean(values_in, axis=-1, keepdims=True))
    spread = lax.optimization_barrier(jnp.mean(center * center, axis=-1, keepdims=True))
    scaling = lax.rsqrt(spread + 1e-05)
    return (center * scaling, scaling)

def to_windows(grid_in, lat_windows, lon_windows, window_side):
    channels = grid_in.shape[-1]
    blocks = grid_in.reshape(lat_windows, window_side, lon_windows, window_side, channels)
    return jnp.transpose(blocks, (0, 2, 1, 3, 4)).reshape(lat_windows * lon_windows, window_side * window_side, channels)

def from_windows(blocks, lat_windows, lon_windows, window_side):
    channels = blocks.shape[-1]
    grid_out = blocks.reshape(lat_windows, lon_windows, window_side, window_side, channels)
    return jnp.transpose(grid_out, (0, 2, 1, 3, 4)).reshape(lat_windows * window_side, lon_windows * window_side, channels)

def neighbours(padded, lat_windows, lon_windows, window_side):
    pieces = []
    for lat_step in range(3):
        for lon_step in range(3):
            section = padded[lat_step * window_side:(lat_step + lat_windows) * window_side, lon_step * window_side:(lon_step + lon_windows) * window_side]
            pieces.append(to_windows(section, lat_windows, lon_windows, window_side))
    return jnp.concatenate(pieces, axis=1)

def spread_back(gathered, lat_windows, lon_windows, window_side):
    channels = gathered.shape[-1]
    window_area = window_side * window_side
    totals = jnp.zeros(((lat_windows + 2) * window_side, (lon_windows + 2) * window_side, channels), jnp.float32)
    for lat_step in range(3):
        for lon_step in range(3):
            slot_index = lat_step * 3 + lon_step
            section = from_windows(gathered[:, slot_index * window_area:(slot_index + 1) * window_area], lat_windows, lon_windows, window_side)
            totals = totals.at[lat_step * window_side:(lat_step + lat_windows) * window_side, lon_step * window_side:(lon_step + lon_windows) * window_side].add(section)
    return totals

def split_heads(array_in, head_count):
    return array_in.reshape(array_in.shape[0], array_in.shape[1], head_count, array_in.shape[2] // head_count).astype(jnp.float32)

def attend_forward(queries, key_rows, value_rows, key_mask, alive_flag, head_count):
    features = queries.shape[-1]
    inv_root = (features // head_count) ** (-0.5)
    scores = jnp.einsum('wqhd,wkhd->whqk', split_heads(queries, head_count), split_heads(key_rows, head_count)) * inv_root
    scores = scores + (key_mask[:, None, None, :] - 1.0) * 1000000000.0
    row_top = lax.optimization_barrier(jnp.max(scores, axis=-1, keepdims=True))
    weights = jnp.exp(scores - row_top)
    probabilities = weights / lax.optimization_barrier(jnp.sum(weights, axis=-1, keepdims=True))
    probabilities_low = probabilities.astype(jnp.bfloat16)
    mixed_out = jnp.einsum('whqk,wkhd->wqhd', probabilities_low.astype(jnp.float32), split_heads(value_rows, head_count))
    mixed_out = mixed_out.reshape(queries.shape) * alive_flag[:, None, None]
    return (mixed_out.astype(jnp.bfloat16), probabilities)

def attend_backward(queries, key_rows, value_rows, probabilities, mixed_out, grad_mixed, head_count):
    features = queries.shape[-1]
    inv_root = (features // head_count) ** (-0.5)
    grad_heads = split_heads(grad_mixed, head_count)
    query_heads = split_heads(queries, head_count)
    grad_probs = jnp.einsum('wqhd,wkhd->whqk', grad_heads, split_heads(value_rows, head_count))
    delta_rows = jnp.einsum('wqhd,wqhd->whq', grad_heads, split_heads(mixed_out, head_count))
    grad_scores = (probabilities * (grad_probs - delta_rows[..., None]) * inv_root).astype(jnp.bfloat16).astype(jnp.float32)
    grad_query = jnp.einsum('whqk,wkhd->wqhd', grad_scores, split_heads(key_rows, head_count)).reshape(queries.shape)
    key_shape = (key_rows.shape[0], key_rows.shape[1], features)
    grad_key = jnp.einsum('whqk,wqhd->wkhd', grad_scores, query_heads).reshape(key_shape)
    grad_value = jnp.einsum('whqk,wqhd->wkhd', probabilities.astype(jnp.bfloat16).astype(jnp.float32), grad_heads).reshape(key_shape)
    return (grad_query, jnp.concatenate([grad_key, grad_value], axis=-1))

def pad_grid(grid_in):
    wrapped = jnp.concatenate([grid_in[:, NLON_P - WIN:], grid_in, grid_in[:, :WIN]], axis=1)
    border = jnp.zeros((WIN,) + wrapped.shape[1:], wrapped.dtype)
    return jnp.concatenate([border, wrapped, border], axis=0)

def level_pass(level_tokens, level_cotangent, level_mask, qkv_weight, out_weight, norm_gain):
    lat_windows = NLAT_P // WIN
    lon_windows = NLON_P // WIN
    flat_in = level_tokens.reshape(-1, D).astype(jnp.float32)
    normed, scaling = norm_rows(flat_in)
    hidden = (normed * norm_gain).astype(jnp.bfloat16)
    projected = jnp.dot(hidden, qkv_weight, preferred_element_type=jnp.float32).astype(jnp.bfloat16)
    queries = projected[:, :D].reshape(NLAT_P, NLON_P, D)
    key_vals = projected[:, D:].reshape(NLAT_P, NLON_P, 2 * D)
    ocean = level_mask.astype(jnp.float32)
    padded = pad_grid(key_vals)
    padded_mask = pad_grid(ocean[..., None])
    grad_branch = level_cotangent * ocean[..., None].astype(jnp.bfloat16)
    grad_flat = grad_branch.reshape(-1, D)
    grad_mixed = jnp.dot(grad_flat, out_weight.T, preferred_element_type=jnp.float32).astype(jnp.bfloat16).reshape(NLAT_P, NLON_P, D)

    def row_step(grad_pad, row_index):
        start = (row_index * WIN).astype(jnp.int32)
        slab = lax.dynamic_slice_in_dim(padded, start, 3 * WIN, 0)
        slab_mask = lax.dynamic_slice_in_dim(padded_mask, start, 3 * WIN, 0)
        near = neighbours(slab, 1, lon_windows, WIN)
        near_mask = neighbours(slab_mask, 1, lon_windows, WIN)[..., 0]
        query_rows = to_windows(lax.dynamic_slice_in_dim(queries, start, WIN, 0), 1, lon_windows, WIN)
        ocean_rows = to_windows(lax.dynamic_slice_in_dim(ocean[..., None], start, WIN, 0), 1, lon_windows, WIN)[..., 0]
        alive_flag = lax.optimization_barrier(jnp.max(ocean_rows, axis=1))
        grad_rows = to_windows(lax.dynamic_slice_in_dim(grad_mixed, start, WIN, 0), 1, lon_windows, WIN)
        mixed_out, probabilities = attend_forward(query_rows, near[..., :D], near[..., D:], near_mask, alive_flag, HEADS)
        grad_query, grad_near = attend_backward(query_rows, near[..., :D], near[..., D:], probabilities, mixed_out, grad_rows, HEADS)
        spread = spread_back(grad_near, 1, lon_windows, WIN)
        current = lax.dynamic_slice_in_dim(grad_pad, start, 3 * WIN, 0)
        grad_pad = lax.dynamic_update_slice_in_dim(grad_pad, current + spread, start, 0)
        return (grad_pad, (from_windows(mixed_out, 1, lon_windows, WIN), from_windows(grad_query, 1, lon_windows, WIN)))
    start_pad = jnp.zeros((NLAT_P + 2 * WIN, NLON_P + 2 * WIN, 2 * D), jnp.float32)
    grad_pad, (mixed_rows, query_rows) = lax.scan(row_step, start_pad, jnp.arange(lat_windows, dtype=jnp.int32))
    mixed_flat = mixed_rows.reshape(-1, D)
    grad_query = query_rows.reshape(-1, D)
    inner_rows = grad_pad[WIN:WIN + NLAT_P]
    grad_kv = inner_rows[:, WIN:WIN + NLON_P]
    grad_kv = grad_kv.at[:, :WIN].add(inner_rows[:, WIN + NLON_P:])
    grad_kv = grad_kv.at[:, NLON_P - WIN:].add(inner_rows[:, :WIN])
    branch = jnp.dot(mixed_flat, out_weight, preferred_element_type=jnp.float32)
    layer_out = (flat_in + ocean.reshape(-1, 1) * branch).astype(jnp.bfloat16)
    out_grad = jnp.dot(mixed_flat.T, grad_flat, preferred_element_type=jnp.float32)
    grad_qkv = jnp.concatenate([grad_query.astype(jnp.bfloat16), grad_kv.reshape(-1, 2 * D).astype(jnp.bfloat16)], axis=1)
    grad_hidden = jnp.dot(grad_qkv, qkv_weight.T, preferred_element_type=jnp.float32)
    qkv_grad = jnp.dot(hidden.T, grad_qkv, preferred_element_type=jnp.float32)
    gain_grad = lax.optimization_barrier(jnp.sum(grad_hidden * normed, axis=0))
    scaled = grad_hidden * norm_gain
    correction = scaled - lax.optimization_barrier(jnp.mean(scaled, axis=-1, keepdims=True)) - normed * lax.optimization_barrier(jnp.mean(scaled * normed, axis=-1, keepdims=True))
    input_grad = (level_cotangent.reshape(-1, D).astype(jnp.float32) + scaling * correction).astype(jnp.bfloat16)
    return (layer_out.reshape(NLAT_P, NLON_P, D), input_grad.reshape(NLAT_P, NLON_P, D), qkv_grad, out_grad, gain_grad)

def reference(tokens_in, cotangent, qkv_weight, out_weight, norm_gain, ocean_mask):

    def one_level(inputs):
        return level_pass(inputs[0], inputs[1], inputs[2], qkv_weight, out_weight, norm_gain)
    layer_out, input_grad, qkv_grads, out_grads, gain_grads = lax.map(one_level, (tokens_in, cotangent, ocean_mask))
    return (layer_out, input_grad, lax.optimization_barrier(jnp.sum(qkv_grads, axis=0)), lax.optimization_barrier(jnp.sum(out_grads, axis=0)), lax.optimization_barrier(jnp.sum(gain_grads, axis=0)))
```

```python
import jax
import jax.numpy as jnp
from jax import lax
from jax.experimental import pallas as pl
from jax.experimental.pallas import tpu as pltpu
from jax.sharding import PartitionSpec as P

MESH = pl.DeviceIdType.MESH
HEADS = 8
WIN = 8


def with_halo(block, sides, width, periodic):
    for axis, dim in sides:
        count = lax.axis_size(axis)
        forward = [(i, i + 1) for i in range(count - 1)]
        if periodic:
            forward.append((count - 1, 0))
        backward = [(target, source) for source, target in forward]
        low = lax.ppermute(
            lax.slice_in_dim(block, block.shape[dim] - width, None, axis=dim), axis, forward
        )
        high = lax.ppermute(lax.slice_in_dim(block, 0, width, axis=dim), axis, backward)
        block = jnp.concatenate([low, block, high], axis=dim)
    return block


def norm_rows(values_in):
    center = values_in - jnp.mean(values_in, axis=-1, keepdims=True)
    spread = jnp.mean(center * center, axis=-1, keepdims=True)
    scaling = lax.rsqrt(spread + 1e-05)
    return (center * scaling, scaling)


def to_windows(grid_in, lat_windows, lon_windows, window_side):
    channels = grid_in.shape[-1]
    blocks = grid_in.reshape(lat_windows, window_side, lon_windows, window_side, channels)
    return jnp.transpose(blocks, (0, 2, 1, 3, 4)).reshape(
        lat_windows * lon_windows, window_side * window_side, channels
    )


def from_windows(blocks, lat_windows, lon_windows, window_side):
    channels = blocks.shape[-1]
    grid_out = blocks.reshape(lat_windows, lon_windows, window_side, window_side, channels)
    return jnp.transpose(grid_out, (0, 2, 1, 3, 4)).reshape(
        lat_windows * window_side, lon_windows * window_side, channels
    )


def neighbours(padded, lat_windows, lon_windows, window_side):
    pieces = []
    for lat_step in range(3):
        for lon_step in range(3):
            section = padded[
                lat_step * window_side : (lat_step + lat_windows) * window_side,
                lon_step * window_side : (lon_step + lon_windows) * window_side,
            ]
            pieces.append(to_windows(section, lat_windows, lon_windows, window_side))
    return jnp.concatenate(pieces, axis=1)


def spread_back(gathered, lat_windows, lon_windows, window_side):
    channels = gathered.shape[-1]
    window_area = window_side * window_side
    totals = jnp.zeros(
        ((lat_windows + 2) * window_side, (lon_windows + 2) * window_side, channels), jnp.float32
    )
    for lat_step in range(3):
        for lon_step in range(3):
            slot_index = lat_step * 3 + lon_step
            section = from_windows(
                gathered[:, slot_index * window_area : (slot_index + 1) * window_area],
                lat_windows,
                lon_windows,
                window_side,
            )
            totals = totals.at[
                lat_step * window_side : (lat_step + lat_windows) * window_side,
                lon_step * window_side : (lon_step + lon_windows) * window_side,
            ].add(section)
    return totals


def split_heads(array_in, head_count):
    return array_in.reshape(
        array_in.shape[0], array_in.shape[1], head_count, array_in.shape[2] // head_count
    )


def attend_forward(queries, key_rows, value_rows, key_mask, alive_flag, head_count):
    features = queries.shape[-1]
    inv_root = (features // head_count) ** (-0.5)
    scores = (
        jnp.einsum(
            "wqhd,wkhd->whqk",
            split_heads(queries, head_count),
            split_heads(key_rows, head_count),
            preferred_element_type=jnp.float32,
        )
        * inv_root
    )
    scores = scores + (key_mask[:, None, None, :] - 1.0) * 1000000000.0
    row_top = jnp.max(scores, axis=-1, keepdims=True)
    weights = jnp.exp(scores - row_top)
    probabilities = weights / jnp.sum(weights, axis=-1, keepdims=True)
    probabilities_low = probabilities.astype(jnp.bfloat16)
    mixed_out = jnp.einsum(
        "whqk,wkhd->wqhd",
        probabilities_low,
        split_heads(value_rows, head_count),
        preferred_element_type=jnp.float32,
    )
    mixed_out = mixed_out.reshape(queries.shape) * alive_flag[:, None, None]
    return (mixed_out.astype(jnp.bfloat16), probabilities)


def attend_backward(
    queries, key_rows, value_rows, probabilities, mixed_out, grad_mixed, head_count
):
    features = queries.shape[-1]
    inv_root = (features // head_count) ** (-0.5)
    grad_heads = split_heads(grad_mixed, head_count)
    query_heads = split_heads(queries, head_count)
    grad_probs = jnp.einsum(
        "wqhd,wkhd->whqk",
        grad_heads,
        split_heads(value_rows, head_count),
        preferred_element_type=jnp.float32,
    )
    delta_rows = jnp.einsum(
        "wqhd,wqhd->whq",
        grad_heads,
        split_heads(mixed_out, head_count),
        preferred_element_type=jnp.float32,
    )
    grad_scores = (probabilities * (grad_probs - delta_rows[..., None]) * inv_root).astype(
        jnp.bfloat16
    )
    grad_query = jnp.einsum(
        "whqk,wkhd->wqhd",
        grad_scores,
        split_heads(key_rows, head_count),
        preferred_element_type=jnp.float32,
    ).reshape(queries.shape)
    key_shape = (key_rows.shape[0], key_rows.shape[1], features)
    grad_key = jnp.einsum(
        "whqk,wqhd->wkhd", grad_scores, query_heads, preferred_element_type=jnp.float32
    ).reshape(key_shape)
    grad_value = jnp.einsum(
        "whqk,wqhd->wkhd",
        probabilities.astype(jnp.bfloat16),
        grad_heads,
        preferred_element_type=jnp.float32,
    ).reshape(key_shape)
    return (grad_query, jnp.concatenate([grad_key, grad_value], axis=-1))


def fold_lat(grad_pad, window_side):
    inner_rows = grad_pad.shape[0] - 2 * window_side
    filler = jnp.zeros((inner_rows - 2 * window_side,) + grad_pad.shape[1:], jnp.float32)
    folded = jnp.concatenate(
        [grad_pad[:window_side], filler, grad_pad[inner_rows + window_side :]], axis=0
    )
    arrived = with_halo(folded, (("lat", 0),), window_side, False)
    middle = grad_pad[window_side : inner_rows + window_side]
    middle = middle.at[:window_side].add(arrived[:window_side])
    return middle.at[inner_rows - window_side :].add(arrived[inner_rows + window_side :])


def fold_lon(grad_pad, window_side):
    inner_cols = grad_pad.shape[1] - 2 * window_side
    filler = jnp.zeros(
        (grad_pad.shape[0], inner_cols - 2 * window_side, grad_pad.shape[2]), jnp.float32
    )
    folded = jnp.concatenate(
        [grad_pad[:, :window_side], filler, grad_pad[:, inner_cols + window_side :]], axis=1
    )
    arrived = with_halo(folded, (("lon", 1),), window_side, True)
    middle = grad_pad[:, window_side : inner_cols + window_side]
    middle = middle.at[:, :window_side].add(arrived[:, :window_side])
    return middle.at[:, inner_cols - window_side :].add(arrived[:, inner_cols + window_side :])


def reduce_kernel(wg_ref, out_ref, r1, a1, r2, a2, r3, a3, g4, g5,
                  s1, v1, s2, v2, s3, v3, s4, v4, s5, v5):
    lon = lax.axis_index("lon")
    lat = lax.axis_index("lat")
    lev = lax.axis_index("lev")
    hi = lev // 2
    core = lev % 2
    here = hi * 8 + lon
    barrier = pltpu.get_barrier_semaphore()

    def plane_peer(step):
        there = (here + step) % 16
        return there // 8, there % 8

    def greet_plane(step, carry):
        peer_hi, peer_lon = plane_peer(step)
        pl.semaphore_signal(
            barrier, inc=1, device_id=(peer_lon, lat, peer_hi * 2 + core), device_id_type=MESH
        )
        return carry

    def greet_lat(step, carry):
        pl.semaphore_signal(
            barrier, inc=1, device_id=(lon, (lat + step) % 8, lev), device_id_type=MESH
        )
        return carry

    pl.semaphore_signal(
        barrier, inc=1, device_id=(lon, lat, hi * 2 + 1 - core), device_id_type=MESH
    )
    lax.fori_loop(1, 16, greet_plane, 0)
    lax.fori_loop(1, 8, greet_lat, 0)
    pl.semaphore_wait(barrier, 23)

    def pair_copy(part):
        return pltpu.make_async_remote_copy(
            src_ref=wg_ref.at[part * 2 + 1 - core],
            dst_ref=r1.at[part],
            send_sem=s1.at[part],
            recv_sem=v1.at[part],
            device_id=(lon, lat, hi * 2 + 1 - core),
            device_id_type=MESH,
        )

    for part in range(2):
        pair_copy(part).start()
    for part in range(2):
        pair_copy(part).wait()

        def add_pair(piece, carry):
            rows = pl.ds(pl.multiple_of(piece * 16, 16), 16)
            total = wg_ref[part * 2 + core, rows, :].astype(jnp.float32) + r1[
                part, rows, :
            ].astype(jnp.float32)
            a1[part * 8 + piece] = total.astype(jnp.bfloat16)
            return carry

        lax.fori_loop(0, 8, add_pair, 0)

    def plane_copy(step):
        peer_hi, peer_lon = plane_peer(step)
        return pltpu.make_async_remote_copy(
            src_ref=a1.at[peer_hi * 8 + peer_lon],
            dst_ref=r2.at[step - 1],
            send_sem=s2.at[step - 1],
            recv_sem=v2.at[step - 1],
            device_id=(peer_lon, lat, peer_hi * 2 + core),
            device_id_type=MESH,
        )

    def begin(copy):
        def one(step, carry):
            copy(step).start()
            return carry

        return one

    def finish(copy):
        def one(step, carry):
            copy(step).wait()
            return carry

        return one

    lax.fori_loop(1, 16, begin(plane_copy), 0)
    lax.fori_loop(1, 16, finish(plane_copy), 0)
    for part in range(8):
        cols = slice(part * 256, (part + 1) * 256)
        total = a1[here, :, cols].astype(jnp.float32)
        for step in range(15):
            total = total + r2[step, :, cols].astype(jnp.float32)
        a2[part] = total.astype(jnp.bfloat16)

    def lat_copy(step):
        peer = (lat + step) % 8
        return pltpu.make_async_remote_copy(
            src_ref=a2.at[peer],
            dst_ref=r3.at[step - 1],
            send_sem=s3.at[step - 1],
            recv_sem=v3.at[step - 1],
            device_id=(lon, peer, lev),
            device_id_type=MESH,
        )

    lax.fori_loop(1, 8, begin(lat_copy), 0)
    lax.fori_loop(1, 8, finish(lat_copy), 0)
    total = a2[lat].astype(jnp.float32)
    for step in range(7):
        total = total + r3[step].astype(jnp.float32)
    a3[...] = total.astype(jnp.bfloat16)
    g4[lat] = a3[...]

    def lat_gather(step):
        return pltpu.make_async_remote_copy(
            src_ref=a3,
            dst_ref=g4.at[lat],
            send_sem=s4.at[step - 1],
            recv_sem=v4.at[step - 1],
            device_id=(lon, (lat + step) % 8, lev),
            device_id_type=MESH,
        )

    lax.fori_loop(1, 8, begin(lat_gather), 0)
    lax.fori_loop(1, 8, finish(lat_gather), 0)
    g5[lon] = g4[...]

    def lon_gather(step):
        return pltpu.make_async_remote_copy(
            src_ref=g4,
            dst_ref=g5.at[lon],
            send_sem=s5.at[step - 1],
            recv_sem=v5.at[step - 1],
            device_id=((lon + step) % 8, lat, lev),
            device_id_type=MESH,
        )

    lax.fori_loop(1, 8, begin(lon_gather), 0)
    lax.fori_loop(1, 8, finish(lon_gather), 0)
    for row in range(8):
        for col in range(8):
            out_ref[row * 16 : (row + 1) * 16, col * 256 : (col + 1) * 256] = g5[row, col].astype(
                jnp.float32
            )


def reduce_weights(wg):
    dma = pltpu.SemaphoreType.DMA
    low = jnp.bfloat16
    return pl.pallas_call(
        reduce_kernel,
        out_shape=jax.ShapeDtypeStruct((128, 2048), jnp.float32),
        in_specs=[pl.BlockSpec(memory_space=pltpu.VMEM)],
        out_specs=pl.BlockSpec(memory_space=pltpu.VMEM),
        scratch_shapes=[
            pltpu.VMEM((2, 128, 2048), low),
            pltpu.VMEM((16, 16, 2048), low),
            pltpu.VMEM((15, 16, 2048), low),
            pltpu.VMEM((8, 16, 256), low),
            pltpu.VMEM((7, 16, 256), low),
            pltpu.VMEM((16, 256), low),
            pltpu.VMEM((8, 16, 256), low),
            pltpu.VMEM((8, 8, 16, 256), low),
            dma((2,)), dma((2,)), dma((15,)), dma((15,)), dma((7,)), dma((7,)),
            dma((7,)), dma((7,)), dma((7,)), dma((7,)),
        ],
        compiler_params=pltpu.CompilerParams(
            collective_id=1, has_side_effects=True, vmem_limit_bytes=40 << 20
        ),
    )(wg)


def on_device(tokens_in, cotangent, qkv_weight, out_weight, norm_gain, ocean_mask):
    lat_rows = tokens_in.shape[1]
    lon_cols = tokens_in.shape[2]
    features = tokens_in.shape[3]
    window_side = WIN
    lat_windows = lat_rows // window_side
    lon_windows = lon_cols // window_side
    flat_in = tokens_in.reshape(-1, features).astype(jnp.float32)
    normed, scaling = norm_rows(flat_in)
    hidden = (normed * norm_gain).astype(jnp.bfloat16)
    ocean = ocean_mask[0].astype(jnp.float32)
    ocean_low = ocean.astype(jnp.bfloat16)
    projected = jnp.dot(hidden, qkv_weight, preferred_element_type=jnp.float32).astype(jnp.bfloat16)
    queries = projected[:, :features]
    payload = projected[:, features:].reshape(lat_rows, lon_cols, 2 * features)
    padded, padded_mask = (
        with_halo(payload, (("lat", 0), ("lon", 1)), window_side, True),
        with_halo(ocean_low, (("lat", 0), ("lon", 1)), window_side, True),
    )
    lat_place = lax.axis_index("lat")
    lat_count = lax.axis_size("lat")
    row_ids = jnp.arange(lat_rows + 2 * window_side)
    keep_rows = jnp.where(
        row_ids < window_side,
        lat_place > 0,
        jnp.where(row_ids >= lat_rows + window_side, lat_place < lat_count - 1, True),
    )
    keep_low = keep_rows.astype(jnp.bfloat16)
    padded = padded * keep_low[:, None, None]
    padded_mask = padded_mask * keep_low[:, None]
    near = neighbours(padded, lat_windows, lon_windows, window_side)
    near_mask = neighbours(padded_mask[..., None], lat_windows, lon_windows, window_side)[
        ..., 0
    ].astype(jnp.float32)
    query_windows = to_windows(
        queries.reshape(lat_rows, lon_cols, features), lat_windows, lon_windows, window_side
    )
    ocean_windows = to_windows(ocean[..., None], lat_windows, lon_windows, window_side)[..., 0]
    alive_flag = jnp.max(ocean_windows, axis=1)
    grad_branch = (cotangent[0] * ocean_low[..., None]).reshape(-1, features)
    grad_mixed = jnp.einsum(
        "te,de->td", grad_branch, out_weight, preferred_element_type=jnp.float32
    ).astype(jnp.bfloat16)
    grad_windows = to_windows(
        grad_mixed.reshape(lat_rows, lon_cols, features), lat_windows, lon_windows, window_side
    )
    key_rows = near[..., :features]
    value_rows = near[..., features:]
    mixed_windows, probabilities = attend_forward(
        query_windows, key_rows, value_rows, near_mask, alive_flag, HEADS
    )
    grad_query, grad_near = attend_backward(
        query_windows, key_rows, value_rows, probabilities, mixed_windows, grad_windows, HEADS
    )
    mixed_flat = from_windows(mixed_windows, lat_windows, lon_windows, window_side).reshape(
        -1, features
    )
    branch = jnp.dot(mixed_flat, out_weight, preferred_element_type=jnp.float32)
    layer_out = (
        (flat_in + ocean.reshape(-1, 1) * branch).astype(jnp.bfloat16).reshape(tokens_in.shape)
    )
    out_grad_local = jnp.einsum(
        "td,te->de", mixed_flat, grad_branch, preferred_element_type=jnp.float32
    )
    grad_pad = spread_back(grad_near, lat_windows, lon_windows, window_side)
    grad_kv = fold_lon(fold_lat(grad_pad, window_side), window_side)
    grad_query_flat = from_windows(grad_query, lat_windows, lon_windows, window_side).reshape(
        -1, features
    )
    grad_qkv = jnp.concatenate(
        [
            grad_query_flat.astype(jnp.bfloat16),
            grad_kv.reshape(-1, 2 * features).astype(jnp.bfloat16),
        ],
        axis=1,
    )
    grad_hidden = jnp.einsum("tc,dc->td", grad_qkv, qkv_weight, preferred_element_type=jnp.float32)
    qkv_grad_local = jnp.einsum("td,tc->dc", hidden, grad_qkv, preferred_element_type=jnp.float32)
    scaled = grad_hidden * norm_gain
    correction = (
        scaled
        - jnp.mean(scaled, axis=-1, keepdims=True)
        - normed * jnp.mean(scaled * normed, axis=-1, keepdims=True)
    )
    input_grad = (
        (cotangent.reshape(-1, features).astype(jnp.float32) + scaling * correction)
        .astype(jnp.bfloat16)
        .reshape(tokens_in.shape)
    )
    wg = jnp.concatenate([qkv_grad_local, out_grad_local], axis=1).astype(jnp.bfloat16)
    shared = reduce_weights(wg.reshape(4, features // 4, 4 * features))
    qkv_grad = shared[:, : 3 * features]
    out_grad = shared[:, 3 * features :]
    first = lax.axis_index("lev") * (features // 4)
    weight_rows = lax.dynamic_slice_in_dim(qkv_weight, first, features // 4, 0)
    gain_rows = lax.dynamic_slice_in_dim(norm_gain, first, features // 4, 0)
    gain_grad = jnp.sum(weight_rows.astype(jnp.float32) * qkv_grad, axis=1) / gain_rows
    return (layer_out, input_grad, qkv_grad, out_grad, gain_grad)


def solution(mesh):
    placed = (
        P("lev", "lat", "lon", None),
        P("lev", "lat", "lon", None),
        P(),
        P(),
        P(),
        P("lev", "lat", "lon"),
    )
    return jax.shard_map(
        on_device,
        mesh=mesh,
        in_specs=placed,
        out_specs=(
            P("lev", "lat", "lon", None),
            P("lev", "lat", "lon", None),
            P("lev", None),
            P("lev", None),
            P("lev"),
        ),
        check_vma=False,
    )
```

```python
import jax
import jax.numpy as jnp
from jax import lax
from jax.experimental import pallas as pl
from jax.experimental.pallas import tpu as pltpu
from jax.sharding import PartitionSpec as P

MESH = pl.DeviceIdType.MESH


def halo_kernel(tokens_ref, mask_ref, ext_ref, near_ref, own_sem, s_lon, v_lon, s_lat, v_lat, s_rel, v_rel, s_m, v_m):
    lon = lax.axis_index("lon")
    lat = lax.axis_index("lat")
    lev = lax.axis_index("lev")
    west = ((lon + 7) % 8, lat, lev)
    east = ((lon + 1) % 8, lat, lev)
    north = (lon, (lat + 7) % 8, lev)
    south = (lon, (lat + 1) % 8, lev)
    barrier = pltpu.get_barrier_semaphore()
    for peer in (west, east, north, south):
        pl.semaphore_signal(barrier, inc=1, device_id=peer, device_id_type=MESH)

    def window(row, col):
        return tokens_ref.at[0, row * 8 : row * 8 + 8, col * 8 : col * 8 + 8, :]

    own = []
    for row in range(2):
        for col in range(2):
            own.append(
                pltpu.make_async_copy(
                    window(row, col), ext_ref.at[1 + row, 1 + col], own_sem.at[row * 2 + col]
                )
            )
            own[-1].start()
    mask_copy = pltpu.make_async_copy(mask_ref, near_ref.at[1, 1], own_sem.at[4])
    mask_copy.start()
    pl.semaphore_wait(barrier, 4)

    def remote(src, dst, send, recv, peer):
        copy = pltpu.make_async_remote_copy(
            src_ref=src, dst_ref=dst, send_sem=send, recv_sem=recv, device_id=peer,
            device_id_type=MESH,
        )
        copy.start()
        return copy

    mask_lon = [
        remote(mask_ref, near_ref.at[1, 2], s_m.at[0], v_m.at[0], west),
        remote(mask_ref, near_ref.at[1, 0], s_m.at[1], v_m.at[1], east),
    ]
    to_lon = []
    for row in range(2):
        to_lon.append(
            remote(window(row, 0), ext_ref.at[1 + row, 3], s_lon.at[row, 0], v_lon.at[row, 0], west)
        )
        to_lon.append(
            remote(window(row, 1), ext_ref.at[1 + row, 0], s_lon.at[row, 1], v_lon.at[row, 1], east)
        )
    to_lat = []
    for col in range(2):
        to_lat.append(
            remote(window(0, col), ext_ref.at[3, 1 + col], s_lat.at[0, col], v_lat.at[0, col], north)
        )
        to_lat.append(
            remote(window(1, col), ext_ref.at[0, 1 + col], s_lat.at[1, col], v_lat.at[1, col], south)
        )
    mask_copy.wait()
    for copy in mask_lon:
        copy.wait()
    mask_lat = [
        remote(near_ref.at[1], near_ref.at[2], s_m.at[2], v_m.at[2], north),
        remote(near_ref.at[1], near_ref.at[0], s_m.at[3], v_m.at[3], south),
    ]
    relayed = []
    for row, line, peer in ((0, 3, north), (1, 0, south)):
        for side, col in ((0, 3), (1, 0)):
            to_lon[row * 2 + side].wait()
            relayed.append(
                remote(
                    ext_ref.at[1 + row, col], ext_ref.at[line, col],
                    s_rel.at[row, side], v_rel.at[row, side], peer,
                )
            )
    for copy in own + to_lat + mask_lat + relayed:
        copy.wait()


def halo(tokens_in, mask_rows):
    dma = pltpu.SemaphoreType.DMA
    return pl.pallas_call(
        halo_kernel,
        out_shape=(
            jax.ShapeDtypeStruct((4, 4, 8, 8, 512), jnp.bfloat16),
            jax.ShapeDtypeStruct((3, 3, 8, 128), jnp.float32),
        ),
        in_specs=[pl.BlockSpec(memory_space=pl.ANY), pl.BlockSpec(memory_space=pltpu.VMEM)],
        out_specs=(
            pl.BlockSpec(memory_space=pltpu.VMEM),
            pl.BlockSpec(memory_space=pltpu.VMEM),
        ),
        scratch_shapes=[
            dma((5,)), dma((2, 2)), dma((2, 2)), dma((2, 2)), dma((2, 2)),
            dma((2, 2)), dma((2, 2)), dma((4,)), dma((4,)),
        ],
        compiler_params=pltpu.CompilerParams(
            collective_id=0, has_side_effects=True, vmem_limit_bytes=16 << 20
        ),
    )(tokens_in, mask_rows)


def dot_nn(left, right):
    return lax.dot_general(
        left, right, (((1,), (0,)), ((), ())), preferred_element_type=jnp.float32
    )


def dot_nt(left, right):
    return lax.dot_general(
        left, right, (((1,), (1,)), ((), ())), preferred_element_type=jnp.float32
    )


def dot_tn(left, right):
    return lax.dot_general(
        left, right, (((0,), (0,)), ((), ())), preferred_element_type=jnp.float32
    )


def norm_rows(values_in):
    center = values_in - jnp.mean(values_in, axis=-1, keepdims=True)
    spread = jnp.mean(center * center, axis=-1, keepdims=True)
    scaling = lax.rsqrt(spread + 1e-05)
    return (center * scaling, scaling)


def attend_kernel(
    ext_ref, near_ref, cot_ref, wqkv_ref, wout_ref, gain_ref,
    layer_ref, back_ref, own_ref, gq_ref, wg_ref,
    hid, kv, gkv, qs, gb, dout, mixed, pscr, dscr, rows_scr, bias,
):
    low = jnp.bfloat16
    full = jnp.float32
    lat = lax.axis_index("lat")
    has_north = jnp.where(lat > 0, 1.0, 0.0).astype(full)
    has_south = jnp.where(lat < 7, 1.0, 0.0).astype(full)
    gain = gain_ref[...]
    place = ((0, 1), (1, 0), (1, 1), (2, 0))
    for row in range(4):
        tile_row, in_row = place[row]
        for col in range(4):
            tile_col, in_col = place[col]
            line = near_ref[tile_row, tile_col, in_row * 2 + in_col : in_row * 2 + in_col + 1, :]
            if row == 0:
                line = line * has_north
            if row == 3:
                line = line * has_south
            rows_scr[row * 4 + col : row * 4 + col + 1, :] = line
    columns = jnp.transpose(jnp.concatenate([rows_scr[...]] * 8, axis=0))
    oceans = []
    for index in range(16):
        column = columns[:64, index : index + 1]
        wide = jnp.broadcast_to(column, (64, 128))
        bias[index * 64 : index * 64 + 64, :] = (wide - 1.0) * 1000000000.0
        if index in (5, 6, 9, 10):
            oceans.append(wide)
    for row in range(4):
        span = slice(row * 256, row * 256 + 256)
        normed, _ = norm_rows(ext_ref[row].astype(full).reshape(256, 512))
        hid[span, :] = (normed * gain).astype(low)
        kv[span, :] = dot_nn(hid[span, :], wqkv_ref[:, 512:]).astype(low)
        gkv[span, :] = jnp.zeros((256, 1024), full)
    for row in range(2):
        own_rows = slice(row * 256 + 320, row * 256 + 448)
        qs[row * 128 : row * 128 + 128, :] = (
            dot_nn(hid[own_rows, :], wqkv_ref[:, :512]) * 0.125
        ).astype(low)
        band = cot_ref[0, row * 8 : row * 8 + 8].astype(full)
        for col in range(2):
            at = (row * 2 + col) * 64
            piece = band[:, col * 8 : col * 8 + 8, :].reshape(64, 512)
            flags = jnp.concatenate([oceans[row * 2 + col]] * 4, axis=1)
            gb[at : at + 64, :] = (piece * flags).astype(low)
    dout[...] = dot_nt(gb[...], wout_ref[...]).astype(low)
    block_row = lax.broadcasted_iota(jnp.int32, (256, 256), 0) // 64
    block_col = lax.broadcasted_iota(jnp.int32, (256, 256), 1) // 64
    diag = jnp.where(block_row == block_col, 1.0, 0.0).astype(full)
    diag_low = diag.astype(low)

    def fold(square):
        kept = square * diag
        return (kept[:64] + kept[64:128]) + (kept[128:192] + kept[192:])

    for index in range(4):
        row, col = index // 2, index % 2
        at = slice(index * 64, index * 64 + 64)
        alive = jnp.max(oceans[index])
        spare = 192 if col == 0 else 0
        for part in range(3):
            pscr[part * 256 + spare : part * 256 + spare + 64, :] = jnp.zeros((64, 256), low)
            dscr[part * 256 + spare : part * 256 + spare + 64, :] = jnp.zeros((64, 256), low)
        spans = [
            slice((row + part) * 256 + col * 64, (row + part) * 256 + col * 64 + 192)
            for part in range(3)
        ]
        kept_spans = [
            slice(part * 256 + col * 64, part * 256 + col * 64 + 192) for part in range(3)
        ]
        slab = slice(row * 256, row * 256 + 768)
        for group in range(2):
            lanes = slice(group * 256, group * 256 + 256)
            value_lanes = slice(512 + group * 256, 512 + group * 256 + 256)
            qbd = jnp.concatenate([qs[at, lanes]] * 4, axis=0) * diag_low
            dbd = jnp.concatenate([dout[at, lanes]] * 4, axis=0) * diag_low
            scores = [
                dot_nt(kv[span, lanes], qbd) + jnp.concatenate([bias[span, :]] * 2, axis=1)
                for span in spans
            ]
            top = jnp.maximum(
                jnp.maximum(
                    jnp.max(scores[0], axis=0, keepdims=True),
                    jnp.max(scores[1], axis=0, keepdims=True),
                ),
                jnp.max(scores[2], axis=0, keepdims=True),
            )
            weights = [jnp.exp(part - top) for part in scores]
            total = (
                jnp.sum(weights[0], axis=0, keepdims=True)
                + jnp.sum(weights[1], axis=0, keepdims=True)
                + jnp.sum(weights[2], axis=0, keepdims=True)
            )
            inverse = 1.0 / total
            probs = [part * inverse for part in weights]
            for part in range(3):
                pscr[kept_spans[part], :] = probs[part].astype(low)
            out = fold(dot_tn(pscr[...], kv[slab, value_lanes]))
            mixed[at, lanes] = (out * alive).astype(low)
            gprobs = [dot_nt(kv[span, value_lanes], dbd) for span in spans]
            delta = (
                jnp.sum(probs[0] * gprobs[0], axis=0, keepdims=True)
                + jnp.sum(probs[1] * gprobs[1], axis=0, keepdims=True)
                + jnp.sum(probs[2] * gprobs[2], axis=0, keepdims=True)
            )
            for part in range(3):
                dscr[kept_spans[part], :] = (probs[part] * (gprobs[part] - delta)).astype(low)
            gq_ref[at, lanes] = (fold(dot_tn(dscr[...], kv[slab, lanes])) * 0.125).astype(low)
            for part in range(3):
                gkv[spans[part], lanes] += dot_nn(dscr[kept_spans[part], :], qbd)
                gkv[spans[part], value_lanes] += dot_nn(pscr[kept_spans[part], :], dbd)
    branch = dot_nn(mixed[...], wout_ref[...])
    for row in range(2):
        pieces = []
        for col in range(2):
            index = row * 2 + col
            flags = jnp.concatenate([oceans[index]] * 4, axis=1)
            here = ext_ref[1 + row, 1 + col].astype(full).reshape(64, 512)
            result = here + flags * branch[index * 64 : index * 64 + 64]
            pieces.append(result.reshape(8, 8, 512))
        layer_ref[0, row * 8 : row * 8 + 8] = jnp.concatenate(pieces, axis=1).astype(low)
    for row in range(4):
        for col in range(4):
            base = (row * 4 + col) * 64
            block = gkv[base : base + 64, :]
            back_ref[row, col] = block.astype(low)
            if row in (1, 2) and col in (1, 2):
                own_ref[(row - 1) * 2 + col - 1] = block
    wg_ref[:, :512] = (
        dot_tn(hid[320:448, :], gq_ref[:128, :]) + dot_tn(hid[576:704, :], gq_ref[128:, :])
    ).astype(low)
    wg_ref[:, 512:1536] = dot_tn(hid[...], back_ref[...].reshape(1024, 1024)).astype(low)
    wg_ref[:, 1536:] = dot_tn(mixed[...], gb[...]).astype(low)


def attend(ext, near, cotangent, qkv_weight, out_weight, gain):
    low, full = jnp.bfloat16, jnp.float32
    vmem = pl.BlockSpec(memory_space=pltpu.VMEM)
    return pl.pallas_call(
        attend_kernel,
        out_shape=(
            jax.ShapeDtypeStruct((1, 16, 16, 512), low),
            jax.ShapeDtypeStruct((4, 4, 64, 1024), low),
            jax.ShapeDtypeStruct((4, 64, 1024), full),
            jax.ShapeDtypeStruct((256, 512), low),
            jax.ShapeDtypeStruct((512, 2048), low),
        ),
        in_specs=[vmem] * 6,
        out_specs=(vmem,) * 5,
        scratch_shapes=[
            pltpu.VMEM((1024, 512), low),
            pltpu.VMEM((1024, 1024), low),
            pltpu.VMEM((1024, 1024), full),
            pltpu.VMEM((256, 512), low),
            pltpu.VMEM((256, 512), low),
            pltpu.VMEM((256, 512), low),
            pltpu.VMEM((256, 512), low),
            pltpu.VMEM((768, 256), low),
            pltpu.VMEM((768, 256), low),
            pltpu.VMEM((16, 128), full),
            pltpu.VMEM((1024, 128), full),
        ],
        compiler_params=pltpu.CompilerParams(vmem_limit_bytes=48 << 20),
    )(ext, near, cotangent, qkv_weight, out_weight, gain)


def input_kernel(tokens_ref, cot_ref, gq_ref, gkv_ref, wqkv_ref, gain_ref, out_ref):
    full = jnp.float32
    gain = gain_ref[...]
    grad_hidden = dot_nt(gq_ref[...], wqkv_ref[:, :512]) + dot_nt(
        gkv_ref[...].reshape(256, 1024), wqkv_ref[:, 512:]
    )
    for row in range(2):
        tokens = tokens_ref[0, row * 8 : row * 8 + 8].astype(full)
        cot = cot_ref[0, row * 8 : row * 8 + 8].astype(full)
        pieces = []
        for col in range(2):
            cols = slice(col * 8, col * 8 + 8)
            at = (row * 2 + col) * 64
            normed, scaling = norm_rows(tokens[:, cols, :].reshape(64, 512))
            scaled = grad_hidden[at : at + 64] * gain
            correction = (
                scaled
                - jnp.mean(scaled, axis=-1, keepdims=True)
                - normed * jnp.mean(scaled * normed, axis=-1, keepdims=True)
            )
            result = cot[:, cols, :].reshape(64, 512) + scaling * correction
            pieces.append(result.reshape(8, 8, 512))
        out_ref[0, row * 8 : row * 8 + 8] = jnp.concatenate(pieces, axis=1).astype(jnp.bfloat16)


def input_gradient(tokens_in, cotangent, gq, gkv, qkv_weight, gain):
    vmem = pl.BlockSpec(memory_space=pltpu.VMEM)
    return pl.pallas_call(
        input_kernel,
        out_shape=jax.ShapeDtypeStruct((1, 16, 16, 512), jnp.bfloat16),
        in_specs=[vmem] * 6,
        out_specs=vmem,
        compiler_params=pltpu.CompilerParams(vmem_limit_bytes=24 << 20),
    )(tokens_in, cotangent, gq, gkv, qkv_weight, gain)


def share_kernel(
    wg_ref, back_ref, own_ref, sum_ref, gkv_ref,
    r1, a1, r2, a2, r3, a3, g4, g5, from_north, from_south, from_west, from_east,
    to_west, to_east,
    s1, v1, s2, v2, s3, v3, s4, v4, s5, v5, s_lat, v_lat, s_lon, v_lon,
):
    low = jnp.bfloat16
    full = jnp.float32
    lon = lax.axis_index("lon")
    lat = lax.axis_index("lat")
    lev = lax.axis_index("lev")
    hi = lev // 2
    core = lev % 2
    here = hi * 8 + lon
    barrier = pltpu.get_barrier_semaphore()

    def plane_peer(step):
        there = (here + step) % 16
        return there // 8, there % 8

    def greet_plane(step, carry):
        peer_hi, peer_lon = plane_peer(step)
        pl.semaphore_signal(
            barrier, inc=1, device_id=(peer_lon, lat, peer_hi * 2 + core), device_id_type=MESH
        )
        return carry

    def greet_lat(step, carry):
        pl.semaphore_signal(
            barrier, inc=1, device_id=(lon, (lat + step) % 8, lev), device_id_type=MESH
        )
        return carry

    pl.semaphore_signal(
        barrier, inc=1, device_id=(lon, lat, hi * 2 + 1 - core), device_id_type=MESH
    )
    lax.fori_loop(1, 16, greet_plane, 0)
    lax.fori_loop(1, 8, greet_lat, 0)
    pl.semaphore_wait(barrier, 23)

    def remote(src, dst, send, recv, peer):
        return pltpu.make_async_remote_copy(
            src_ref=src, dst_ref=dst, send_sem=send, recv_sem=recv, device_id=peer,
            device_id_type=MESH,
        )

    def begin(copy):
        def one(step, carry):
            copy(step).start()
            return carry

        return one

    def finish(copy):
        def one(step, carry):
            copy(step).wait()
            return carry

        return one

    def pair_copy(part):
        return remote(
            wg_ref.at[part * 2 + 1 - core], r1.at[part], s1.at[part], v1.at[part],
            (lon, lat, hi * 2 + 1 - core),
        )

    def plane_copy(step):
        peer_hi, peer_lon = plane_peer(step)
        return remote(
            a1.at[peer_hi * 8 + peer_lon], r2.at[step - 1], s2.at[step - 1], v2.at[step - 1],
            (peer_lon, lat, peer_hi * 2 + core),
        )

    def lat_copy(step):
        peer = (lat + step) % 8
        return remote(
            a2.at[peer], r3.at[step - 1], s3.at[step - 1], v3.at[step - 1], (lon, peer, lev)
        )

    def lat_gather(step):
        return remote(
            a3, g4.at[lat], s4.at[step - 1], v4.at[step - 1], (lon, (lat + step) % 8, lev)
        )

    def lon_gather(step):
        return remote(
            g4, g5.at[lon], s5.at[step - 1], v5.at[step - 1], ((lon + step) % 8, lat, lev)
        )

    north = (lon, (lat + 7) % 8, lev)
    south = (lon, (lat + 1) % 8, lev)
    west = ((lon + 7) % 8, lat, lev)
    east = ((lon + 1) % 8, lat, lev)
    corners = []
    edges = []
    for line, target, peer, side in ((0, from_south, north, 0), (3, from_north, south, 1)):
        for col in (0, 3):
            corners.append(
                remote(
                    back_ref.at[line, col], target.at[col],
                    s_lat.at[side, col], v_lat.at[side, col], peer,
                )
            )
        edges.append(
            remote(
                back_ref.at[line, pl.ds(1, 2)], target.at[pl.ds(1, 2)],
                s_lat.at[side, 1], v_lat.at[side, 1], peer,
            )
        )
    pairs = [pair_copy(part) for part in range(2)]
    for copy in pairs:
        copy.start()
    for copy in corners:
        copy.start()
    for part in range(2):
        pairs[part].wait()

        def add_pair(piece, carry):
            rows = pl.ds(pl.multiple_of(piece * 16, 16), 16)
            total = wg_ref[part * 2 + core, rows, :].astype(full) + r1[part, rows, :].astype(full)
            a1[part * 8 + piece] = total.astype(low)
            return carry

        lax.fori_loop(0, 8, add_pair, 0)
    lax.fori_loop(1, 16, begin(plane_copy), 0)
    for copy in edges:
        copy.start()
    for copy in corners:
        copy.wait()
    sources = (from_north, from_south)

    def add_corner(piece, carry):
        rows = pl.ds(pl.multiple_of(piece * 16, 16), 16)
        for row in range(2):
            to_west[row, rows, :] = (
                back_ref[1 + row, 0, rows, :].astype(full)
                + sources[row][0, rows, :].astype(full)
            ).astype(low)
            to_east[row, rows, :] = (
                back_ref[1 + row, 3, rows, :].astype(full)
                + sources[row][3, rows, :].astype(full)
            ).astype(low)
        return carry

    lax.fori_loop(0, 4, add_corner, 0)
    sides = [
        remote(to_west, from_east, s_lon.at[0], v_lon.at[0], west),
        remote(to_east, from_west, s_lon.at[1], v_lon.at[1], east),
    ]
    for copy in sides:
        copy.start()
    lax.fori_loop(1, 16, finish(plane_copy), 0)
    for part in range(8):
        cols = slice(part * 256, (part + 1) * 256)
        total = a1[here, :, cols].astype(full)
        for step in range(15):
            total = total + r2[step, :, cols].astype(full)
        a2[part] = total
    lax.fori_loop(1, 8, begin(lat_copy), 0)
    lax.fori_loop(1, 8, finish(lat_copy), 0)
    total = a2[lat]
    for step in range(7):
        total = total + r3[step]
    a3[...] = total.astype(low)
    g4[lat] = a3[...]
    lax.fori_loop(1, 8, begin(lat_gather), 0)
    lax.fori_loop(1, 8, finish(lat_gather), 0)
    g5[lon] = g4[...]
    lax.fori_loop(1, 8, begin(lon_gather), 0)
    for copy in edges + sides:
        copy.wait()

    def add_own(piece, carry):
        rows = pl.ds(pl.multiple_of(piece * 16, 16), 16)
        for row in range(2):
            for col in range(2):
                index = row * 2 + col
                side = (from_west, from_east)[col]
                gkv_ref[index, rows, :] = (
                    own_ref[index, rows, :]
                    + sources[row][1 + col, rows, :].astype(full)
                    + side[row, rows, :].astype(full)
                ).astype(low)
        return carry

    lax.fori_loop(0, 4, add_own, 0)
    lax.fori_loop(1, 8, finish(lon_gather), 0)
    for row in range(8):
        for col in range(8):
            sum_ref[row * 16 : (row + 1) * 16, col * 256 : (col + 1) * 256] = g5[row, col].astype(
                full
            )


def share(wg, back, own):
    dma = pltpu.SemaphoreType.DMA
    low, full = jnp.bfloat16, jnp.float32
    vmem = pl.BlockSpec(memory_space=pltpu.VMEM)
    return pl.pallas_call(
        share_kernel,
        out_shape=(
            jax.ShapeDtypeStruct((128, 2048), full),
            jax.ShapeDtypeStruct((4, 64, 1024), low),
        ),
        in_specs=[vmem] * 3,
        out_specs=(vmem, vmem),
        scratch_shapes=[
            pltpu.VMEM((2, 128, 2048), low),
            pltpu.VMEM((16, 16, 2048), low),
            pltpu.VMEM((15, 16, 2048), low),
            pltpu.VMEM((8, 16, 256), full),
            pltpu.VMEM((7, 16, 256), full),
            pltpu.VMEM((16, 256), low),
            pltpu.VMEM((8, 16, 256), low),
            pltpu.VMEM((8, 8, 16, 256), low),
            pltpu.VMEM((4, 64, 1024), low),
            pltpu.VMEM((4, 64, 1024), low),
            pltpu.VMEM((2, 64, 1024), low),
            pltpu.VMEM((2, 64, 1024), low),
            pltpu.VMEM((2, 64, 1024), low),
            pltpu.VMEM((2, 64, 1024), low),
            dma((2,)), dma((2,)), dma((15,)), dma((15,)), dma((7,)), dma((7,)),
            dma((7,)), dma((7,)), dma((7,)), dma((7,)),
            dma((2, 4)), dma((2, 4)), dma((2,)), dma((2,)),
        ],
        compiler_params=pltpu.CompilerParams(
            collective_id=1, has_side_effects=True, vmem_limit_bytes=40 << 20
        ),
    )(wg, back, own)


def on_device(tokens_in, cotangent, qkv_weight, out_weight, norm_gain, ocean_mask):
    features = tokens_in.shape[3]
    ocean = ocean_mask[0].astype(jnp.float32).reshape(2, 8, 2, 8)
    mask_rows = jnp.pad(jnp.transpose(ocean, (0, 2, 1, 3)).reshape(4, 64), ((0, 4), (0, 64)))
    ext, near = halo(tokens_in, mask_rows)
    gain = norm_gain.reshape(1, features)
    layer_out, back, own, gq, wg = attend(ext, near, cotangent, qkv_weight, out_weight, gain)
    shared, gkv = share(wg.reshape(4, features // 4, 4 * features), back, own)
    input_grad = input_gradient(tokens_in, cotangent, gq, gkv, qkv_weight, gain)
    qkv_grad = shared[:, : 3 * features]
    out_grad = shared[:, 3 * features :]
    first = lax.axis_index("lev") * (features // 4)
    weight_rows = lax.dynamic_slice_in_dim(qkv_weight, first, features // 4, 0)
    gain_rows = lax.dynamic_slice_in_dim(norm_gain, first, features // 4, 0)
    gain_grad = jnp.sum(weight_rows.astype(jnp.float32) * qkv_grad, axis=1) / gain_rows
    return (layer_out, input_grad, qkv_grad, out_grad, gain_grad)


def solution(mesh):
    placed = (
        P("lev", "lat", "lon", None),
        P("lev", "lat", "lon", None),
        P(),
        P(),
        P(),
        P("lev", "lat", "lon"),
    )
    return jax.shard_map(
        on_device,
        mesh=mesh,
        in_specs=placed,
        out_specs=(
            P("lev", "lat", "lon", None),
            P("lev", "lat", "lon", None),
            P("lev", None),
            P("lev", None),
            P("lev"),
        ),
        check_vma=False,
    )
```

```python
import jax
import jax.numpy as jnp
from jax import lax
from jax.experimental import pallas as pl
from jax.experimental.pallas import tpu as pltpu
from jax.sharding import PartitionSpec as P

MESH = pl.DeviceIdType.MESH
LOW = jnp.bfloat16
FULL = jnp.float32
WIDTHS = (768, 512, 768)


def dot_nn(left, right):
    return lax.dot_general(
        left, right, (((1,), (0,)), ((), ())), preferred_element_type=jnp.float32
    )


def dot_nt(left, right):
    return lax.dot_general(
        left, right, (((1,), (1,)), ((), ())), preferred_element_type=jnp.float32
    )


def dot_tn(left, right):
    return lax.dot_general(
        left, right, (((0,), (0,)), ((), ())), preferred_element_type=jnp.float32
    )


def norm_rows(values_in):
    center = values_in - jnp.mean(values_in, axis=-1, keepdims=True)
    spread = jnp.mean(center * center, axis=-1, keepdims=True)
    scaling = lax.rsqrt(spread + 1e-05)
    return (center * scaling, scaling)


def layer_kernel(
    tokens_ref, cot_ref, wqkv_ref, wout_ref, gain_ref, mask_ref,
    layer_ref, grad_ref, sum_a, sum_c, sum_b,
    ext, near, cots, wq, wo, hid, kv, gkv, back, qs, gb, dout, mixed, gq, pscr, dscr, bias,
    wg_a, wg_c, wg_b, r1_a, r1_c, r1_b, a1_a, a1_c, a1_b, r2_a, r2_c, r2_b,
    a2_a, a2_c, a2_b, r3_a, r3_c, r3_b,
    from_north, from_south, from_west, from_east, to_west, to_east,
    local_sem, s_lon, v_lon, s_lat, v_lat, s_rel, v_rel, s_m, v_m,
    s_pair, v_pair, s_plane, v_plane, s_z, v_z, s_all, v_all, s_gz, v_gz, s_gx, v_gx,
):
    lon = lax.axis_index("lon")
    lat = lax.axis_index("lat")
    lev = lax.axis_index("lev")
    hi = lev // 2
    core = lev % 2
    here = hi * 8 + lon
    west = ((lon + 7) % 8, lat, lev)
    east = ((lon + 1) % 8, lat, lev)
    north = (lon, (lat + 7) % 8, lev)
    south = (lon, (lat + 1) % 8, lev)
    partner = (lon, lat, hi * 2 + 1 - core)

    def plane_peer(step):
        there = (here + step) % 16
        return there // 8, there % 8

    def window(row, col):
        return tokens_ref.at[0, row * 8 : row * 8 + 8, col * 8 : col * 8 + 8, :]

    def local(src, dst, slot):
        copy = pltpu.make_async_copy(src, dst, local_sem.at[slot])
        copy.start()
        return copy

    def remote(src, dst, send, recv, peer):
        return pltpu.make_async_remote_copy(
            src_ref=src, dst_ref=dst, send_sem=send, recv_sem=recv, device_id=peer,
            device_id_type=MESH,
        )

    def begin(copy):
        def one(step, carry):
            copy(step).start()
            return carry

        return one

    def finish(copy):
        def one(step, carry):
            copy(step).wait()
            return carry

        return one

    mask_copy = local(mask_ref.at[0], near.at[1, 1], 0)
    own = [
        local(window(row, col), ext.at[1 + row, 1 + col], 1 + row * 2 + col)
        for row in range(2)
        for col in range(2)
    ]
    wq_copy = local(wqkv_ref, wq, 5)
    cot_copy = local(cot_ref.at[0], cots, 6)
    wo_copy = local(wout_ref, wo, 7)

    barrier = pltpu.get_barrier_semaphore()

    def greet(peer):
        pl.semaphore_signal(barrier, inc=1, device_id=peer, device_id_type=MESH)

    def greet_plane(step, carry):
        peer_hi, peer_lon = plane_peer(step)
        greet((peer_lon, lat, peer_hi * 2 + core))
        return carry

    def greet_lat(step, carry):
        greet((lon, (lat + step) % 8, lev))
        return carry

    greet(partner)
    lax.fori_loop(1, 16, greet_plane, 0)
    lax.fori_loop(1, 8, greet_lat, 0)
    mask_copy.wait()
    pl.semaphore_wait(barrier, 23)

    mask_lon = [
        remote(near.at[1, 1], near.at[1, 2], s_m.at[0], v_m.at[0], west),
        remote(near.at[1, 1], near.at[1, 0], s_m.at[1], v_m.at[1], east),
    ]
    to_lon = []
    to_lat = []
    for row in range(2):
        to_lon.append(
            remote(window(row, 0), ext.at[1 + row, 3], s_lon.at[row, 0], v_lon.at[row, 0], west)
        )
        to_lon.append(
            remote(window(row, 1), ext.at[1 + row, 0], s_lon.at[row, 1], v_lon.at[row, 1], east)
        )
    for col in range(2):
        to_lat.append(
            remote(window(0, col), ext.at[3, 1 + col], s_lat.at[0, col], v_lat.at[0, col], north)
        )
        to_lat.append(
            remote(window(1, col), ext.at[0, 1 + col], s_lat.at[1, col], v_lat.at[1, col], south)
        )
    for copy in mask_lon + to_lon + to_lat:
        copy.start()

    gain = gain_ref[...]

    def normalise(row, col):
        normed, _ = norm_rows(ext[row, col].astype(FULL).reshape(64, 512))
        at = (row * 4 + col) * 64
        hid[at : at + 64, :] = (normed * gain).astype(LOW)

    def project(spots):
        for row, col in spots:
            normalise(row, col)
        rows = jnp.concatenate(
            [hid[(row * 4 + col) * 64 : (row * 4 + col) * 64 + 64, :] for row, col in spots], axis=0
        )
        for group in range(2):
            for part in range(2):
                first = 512 + part * 512 + group * 256
                result = dot_nn(rows, wq[:, first : first + 256]).astype(LOW)
                for index, (row, col) in enumerate(spots):
                    at = (row * 4 + col) * 64
                    kv[group, at : at + 64, part * 256 : part * 256 + 256] = result[
                        index * 64 : index * 64 + 64
                    ]
        return rows

    token_of = lax.broadcasted_iota(jnp.int32, (128, 16), 0)
    lane_of = lax.broadcasted_iota(jnp.int32, (128, 16), 1)
    repeat_rows = jnp.where(token_of // 8 == lane_of, 1.0, 0.0).astype(LOW)
    picks = [jnp.where(lane_of == token_of % 8 + 8 * side, 1.0, 0.0) for side in range(2)]
    has_north = jnp.where(lat > 0, 1.0, 0.0).astype(FULL)
    has_south = jnp.where(lat < 7, 1.0, 0.0).astype(FULL)

    def mask_columns(tile_row, tile_col):
        tall = dot_nn(repeat_rows, near[tile_row, tile_col].astype(FULL).astype(LOW))
        return [
            jnp.broadcast_to(jnp.sum(tall * pick, axis=1, keepdims=True), (128, 128))
            for pick in picks
        ]

    for copy in own:
        copy.wait()
    oceans = [None] * 4
    centre = mask_columns(1, 1)
    for row in range(2):
        for col in range(2):
            oceans[row * 2 + col] = centre[col][row * 64 : row * 64 + 64]
    wq_copy.wait()
    rows = project(((1, 1), (1, 2), (2, 1), (2, 2)))
    qs[...] = (dot_nn(rows, wq[:, :512]) * 0.125).astype(LOW)
    for copy in mask_lon:
        copy.wait()
    mask_lat = [
        remote(near.at[1], near.at[2], s_m.at[2], v_m.at[2], north),
        remote(near.at[1], near.at[0], s_m.at[3], v_m.at[3], south),
    ]
    for copy in mask_lat:
        copy.start()
    cot_copy.wait()
    for row in range(2):
        band = cots[row * 8 : row * 8 + 8].astype(FULL)
        for col in range(2):
            at = (row * 2 + col) * 64
            piece = band[:, col * 8 : col * 8 + 8, :].reshape(64, 512)
            flags = jnp.concatenate([oceans[row * 2 + col]] * 4, axis=1)
            gb[at : at + 64, :] = (piece * flags).astype(LOW)
    wo_copy.wait()
    dout[...] = dot_nt(gb[...], wo[...]).astype(LOW)
    for group in range(2):
        for row in range(4):
            gkv[group, row * 256 : row * 256 + 256, :] = jnp.zeros((256, 512), FULL)
    relayed = []
    for row, line, peer in ((0, 3, north), (1, 0, south)):
        for side, col in ((0, 3), (1, 0)):
            to_lon[row * 2 + side].wait()
            relayed.append(
                remote(
                    ext.at[1 + row, col], ext.at[line, col],
                    s_rel.at[row, side], v_rel.at[row, side], peer,
                )
            )
            relayed[-1].start()
    project(((1, 0), (2, 0), (1, 3), (2, 3)))
    for copy in mask_lat:
        copy.wait()
    place = ((0, 1), (1, 0), (1, 1), (2, 0))
    for tile_row in range(3):
        for tile_col in range(3):
            sides = centre if (tile_row, tile_col) == (1, 1) else mask_columns(tile_row, tile_col)
            for row in range(4):
                for col in range(4):
                    if place[row][0] != tile_row or place[col][0] != tile_col:
                        continue
                    at = (row * 4 + col) * 64
                    flags = sides[place[col][1]][place[row][1] * 64 : place[row][1] * 64 + 64]
                    if row == 0:
                        flags = flags * has_north
                    if row == 3:
                        flags = flags * has_south
                    bias[at : at + 64, :] = (flags - 1.0) * 1000000000.0
    for copy in to_lat:
        copy.wait()
    project(((0, 1), (0, 2), (3, 1), (3, 2)))
    for copy in relayed:
        copy.wait()
    project(((0, 0), (0, 3), (3, 0), (3, 3)))

    block_row = lax.broadcasted_iota(jnp.int32, (256, 256), 0) // 64
    block_col = lax.broadcasted_iota(jnp.int32, (256, 256), 1) // 64
    diag = jnp.where(block_row == block_col, 1.0, 0.0).astype(FULL)
    diag_low = diag.astype(LOW)

    def fold(square):
        kept = square * diag
        return (kept[:64] + kept[64:128]) + (kept[128:192] + kept[192:])

    def attend(index, group):
        row, col = index // 2, index % 2
        at = slice(index * 64, index * 64 + 64)
        lanes = slice(group * 256, group * 256 + 256)
        alive = jnp.max(oceans[index], axis=(0, 1), keepdims=True)
        slot = index % 2
        spare = 192 if col == 0 else 0
        for part in range(3):
            pscr[slot, part * 256 + spare : part * 256 + spare + 64, :] = jnp.zeros((64, 256), LOW)
            dscr[slot, part * 256 + spare : part * 256 + spare + 64, :] = jnp.zeros((64, 256), LOW)
        starts = [(row + part) * 256 + col * 64 for part in range(3)]
        spans = [slice(start, start + 192) for start in starts]
        inner = [slice(part * 256 + col * 64, part * 256 + col * 64 + 192) for part in range(3)]
        slab = slice(row * 256, row * 256 + 768)
        qbd = jnp.concatenate([qs[at, lanes]] * 4, axis=0) * diag_low
        dbd = jnp.concatenate([dout[at, lanes]] * 4, axis=0) * diag_low
        scores = [
            dot_nt(kv[group, span, :256], qbd) + jnp.concatenate([bias[span, :]] * 2, axis=1)
            for span in spans
        ]
        tops = [jnp.max(part, axis=0, keepdims=True) for part in scores]
        top = jnp.maximum(jnp.maximum(tops[0], tops[1]), tops[2])
        weights = [jnp.exp(part - top) for part in scores]
        sums = [jnp.sum(part, axis=0, keepdims=True) for part in weights]
        inverse = 1.0 / (sums[0] + sums[1] + sums[2])
        probs = [part * inverse for part in weights]
        for part in range(3):
            pscr[slot, inner[part], :] = probs[part].astype(LOW)
        out = fold(dot_tn(pscr[slot], kv[group, slab, 256:]))
        mixed[at, lanes] = (out * alive).astype(LOW)
        gprobs = [dot_nt(kv[group, span, 256:], dbd) for span in spans]
        deltas = [
            jnp.sum(probs[part] * gprobs[part], axis=0, keepdims=True) for part in range(3)
        ]
        delta = deltas[0] + deltas[1] + deltas[2]
        for part in range(3):
            dscr[slot, inner[part], :] = (probs[part] * (gprobs[part] - delta)).astype(LOW)
        gq[at, lanes] = (fold(dot_tn(dscr[slot], kv[group, slab, :256])) * 0.125).astype(LOW)
        for part in range(3):
            gkv[group, spans[part], :256] += dot_nn(dscr[slot, inner[part], :], qbd)
            gkv[group, spans[part], 256:] += dot_nn(pscr[slot, inner[part], :], dbd)

    wgs = (wg_a, wg_c, wg_b)
    r1s = (r1_a, r1_c, r1_b)
    a1s = (a1_a, a1_c, a1_b)
    r2s = (r2_a, r2_c, r2_b)
    a2s = (a2_a, a2_c, a2_b)
    r3s = (r3_a, r3_c, r3_b)
    totals = (sum_a, sum_c, sum_b)

    def pair_copies(chunk):
        return [
            remote(
                wgs[chunk].at[part * 2 + 1 - core], r1s[chunk].at[part],
                s_pair.at[chunk, part], v_pair.at[chunk, part], partner,
            )
            for part in range(2)
        ]

    def plane_copy(chunk):
        def one(step):
            peer_hi, peer_lon = plane_peer(step)
            return remote(
                a1s[chunk].at[peer_hi * 8 + peer_lon], r2s[chunk].at[step - 1],
                s_plane.at[chunk, step - 1], v_plane.at[chunk, step - 1],
                (peer_lon, lat, peer_hi * 2 + core),
            )

        return one

    def z_copy(chunk):
        def one(step):
            return remote(
                a2s[chunk], r3s[chunk].at[step - 1],
                s_z.at[chunk, step - 1], v_z.at[chunk, step - 1], (lon, (lat + step) % 8, lev),
            )

        return one

    def all_copy(chunk):
        def one(step):
            return remote(
                totals[chunk].at[lon], totals[chunk].at[lon],
                s_all.at[chunk, step - 1], v_all.at[chunk, step - 1],
                ((lon + step) % 8, lat, lev),
            )

        return one

    def start_pair(chunk):
        for copy in pair_copies(chunk):
            copy.start()

    def pair_to_plane(chunk):
        for part, copy in enumerate(pair_copies(chunk)):
            copy.wait()

            def add(piece, carry):
                span = pl.ds(pl.multiple_of(piece * 16, 16), 16)
                total = wgs[chunk][part * 2 + core, span, :].astype(FULL) + r1s[chunk][
                    part, span, :
                ].astype(FULL)
                a1s[chunk][part * 8 + piece] = total.astype(LOW)
                return carry

            lax.fori_loop(0, 8, add, 0)
        lax.fori_loop(1, 16, begin(plane_copy(chunk)), 0)

    def plane_to_z(chunk):
        lax.fori_loop(1, 16, finish(plane_copy(chunk)), 0)
        for first in range(0, WIDTHS[chunk], 256):
            cols = slice(first, first + 256)
            total = a1s[chunk][here, :, cols].astype(FULL)
            for step in range(15):
                total = total + r2s[chunk][step, :, cols].astype(FULL)
            a2s[chunk][:, cols] = total.astype(LOW)
        lax.fori_loop(1, 8, begin(z_copy(chunk)), 0)

    def z_to_all(chunk):
        lax.fori_loop(1, 8, finish(z_copy(chunk)), 0)
        for first in range(0, WIDTHS[chunk], 256):
            cols = slice(first, first + 256)
            total = a2s[chunk][:, cols].astype(FULL)
            for step in range(7):
                total = total + r3s[chunk][step, :, cols].astype(FULL)
            totals[chunk][lon, :, cols] = total.astype(LOW)
        lax.fori_loop(1, 8, begin(all_copy(chunk)), 0)

    def return_lat(group):
        corners = []
        edges = []
        for line, target, peer, side in ((0, from_south, north, 0), (3, from_north, south, 1)):
            for col in (0, 3):
                corners.append(
                    remote(
                        back.at[group, line, col], target.at[group, col],
                        s_gz.at[group, side, col], v_gz.at[group, side, col], peer,
                    )
                )
            edges.append(
                remote(
                    back.at[group, line, pl.ds(1, 2)], target.at[group, pl.ds(1, 2)],
                    s_gz.at[group, side, 1], v_gz.at[group, side, 1], peer,
                )
            )
        return corners, edges

    def return_lon(group):
        return [
            remote(
                to_west.at[group], from_east.at[group], s_gx.at[group, 0], v_gx.at[group, 0], west
            ),
            remote(
                to_east.at[group], from_west.at[group], s_gx.at[group, 1], v_gx.at[group, 1], east
            ),
        ]

    sources = (from_north, from_south)

    def start_return(group):
        corners, edges = return_lat(group)
        for copy in corners + edges:
            copy.start()

    def corner_to_lon(group):
        for copy in return_lat(group)[0]:
            copy.wait()
        for row in range(2):
            to_west[group, row] = (
                back[group, 1 + row, 0].astype(FULL) + sources[row][group, 0].astype(FULL)
            ).astype(LOW)
            to_east[group, row] = (
                back[group, 1 + row, 3].astype(FULL) + sources[row][group, 3].astype(FULL)
            ).astype(LOW)
        for copy in return_lon(group):
            copy.start()

    def finish_return(group):
        for copy in return_lat(group)[1] + return_lon(group):
            copy.wait()
        pieces = []
        for row in range(2):
            for col in range(2):
                at = ((1 + row) * 4 + 1 + col) * 64
                side = (from_west, from_east)[col]
                pieces.append(
                    (
                        gkv[group, at : at + 64, :]
                        + sources[row][group, 1 + col].astype(FULL)
                        + side[group, row].astype(FULL)
                    ).astype(LOW)
                )
        return jnp.concatenate(pieces, axis=0)

    def settle(group):
        for row in range(4):
            for col in range(4):
                at = (row * 4 + col) * 64
                back[group, row, col] = gkv[group, at : at + 64, :].astype(LOW)

    def own_rows(row):
        return slice(row * 256 + 320, row * 256 + 448)

    def weight_chunk(group, chunk):
        lanes = slice(group * 256, group * 256 + 256)
        query = dot_tn(hid[own_rows(0), :], gq[:128, lanes]) + dot_tn(
            hid[own_rows(1), :], gq[128:, lanes]
        )
        wgs[chunk][:, :, :256] = query.astype(LOW).reshape(4, 128, 256)
        both = dot_tn(hid[...], back[group].reshape(1024, 512))
        wgs[chunk][:, :, 256:] = both.astype(LOW).reshape(4, 128, 512)

    for index in range(4):
        attend(index, 0)
    settle(0)
    weight_chunk(0, 0)
    start_pair(0)
    start_return(0)
    attend(0, 1)
    pair_to_plane(0)
    attend(1, 1)
    attend(2, 1)
    corner_to_lon(0)
    attend(3, 1)
    wg_c[...] = dot_tn(mixed[...], gb[...]).astype(LOW).reshape(4, 128, 512)
    start_pair(1)
    settle(1)
    weight_chunk(1, 2)
    start_pair(2)
    pair_to_plane(1)
    pair_to_plane(2)
    start_return(1)
    plane_to_z(0)
    branch = dot_nn(mixed[...], wo[...])
    for row in range(2):
        pieces = []
        for col in range(2):
            index = row * 2 + col
            flags = jnp.concatenate([oceans[index]] * 4, axis=1)
            tokens = ext[1 + row, 1 + col].astype(FULL).reshape(64, 512)
            result = tokens + flags * branch[index * 64 : index * 64 + 64]
            pieces.append(result.reshape(8, 8, 512))
        layer_ref[0, row * 8 : row * 8 + 8] = jnp.concatenate(pieces, axis=1).astype(LOW)
    z_to_all(0)
    plane_to_z(1)
    corner_to_lon(1)
    plane_to_z(2)
    z_to_all(1)
    grad_hidden = dot_nt(gq[...], wq[:, :512])
    for group in range(2):
        both = finish_return(group)
        for part in range(2):
            first = 512 + part * 512 + group * 256
            grad_hidden = grad_hidden + dot_nt(
                both[:, part * 256 : part * 256 + 256], wq[:, first : first + 256]
            )
    for row in range(2):
        pieces = []
        cot = cots[row * 8 : row * 8 + 8].astype(FULL)
        for col in range(2):
            at = (row * 2 + col) * 64
            normed, scaling = norm_rows(ext[1 + row, 1 + col].astype(FULL).reshape(64, 512))
            scaled = grad_hidden[at : at + 64] * gain
            correction = (
                scaled
                - jnp.mean(scaled, axis=-1, keepdims=True)
                - normed * jnp.mean(scaled * normed, axis=-1, keepdims=True)
            )
            result = cot[:, col * 8 : col * 8 + 8, :].reshape(64, 512) + scaling * correction
            pieces.append(result.reshape(8, 8, 512))
        grad_ref[0, row * 8 : row * 8 + 8] = jnp.concatenate(pieces, axis=1).astype(LOW)
    z_to_all(2)
    for chunk in range(3):
        lax.fori_loop(1, 8, finish(all_copy(chunk)), 0)


def layer(tokens_in, cotangent, qkv_weight, out_weight, gain, ocean_mask):
    dma = pltpu.SemaphoreType.DMA
    vmem = pl.BlockSpec(memory_space=pltpu.VMEM)
    hbm = pl.BlockSpec(memory_space=pltpu.HBM)
    scratch = [
        pltpu.VMEM((4, 4, 8, 8, 512), LOW),
        pltpu.VMEM((3, 3, 16, 16), jnp.int32),
        pltpu.VMEM((16, 16, 512), LOW),
        pltpu.VMEM((512, 1536), LOW),
        pltpu.VMEM((512, 512), LOW),
        pltpu.VMEM((1024, 512), LOW),
        pltpu.VMEM((2, 1024, 512), LOW),
        pltpu.VMEM((2, 1024, 512), FULL),
        pltpu.VMEM((2, 4, 4, 64, 512), LOW),
    ]
    scratch += [pltpu.VMEM((256, 512), LOW)] * 5
    scratch += [pltpu.VMEM((2, 768, 256), LOW)] * 2
    scratch += [pltpu.VMEM((1024, 128), FULL)]
    scratch += [pltpu.VMEM((4, 128, width), LOW) for width in WIDTHS]
    scratch += [pltpu.VMEM((2, 128, width), LOW) for width in WIDTHS]
    scratch += [pltpu.VMEM((16, 16, width), LOW) for width in WIDTHS]
    scratch += [pltpu.VMEM((15, 16, width), LOW) for width in WIDTHS]
    scratch += [pltpu.VMEM((16, width), LOW) for width in WIDTHS]
    scratch += [pltpu.VMEM((7, 16, width), LOW) for width in WIDTHS]
    scratch += [pltpu.VMEM((2, 4, 64, 512), LOW)] * 2
    scratch += [pltpu.VMEM((2, 2, 64, 512), LOW)] * 4
    scratch += [dma((8,))] + [dma((2, 2))] * 6 + [dma((4,))] * 2
    scratch += [dma((3, 2))] * 2 + [dma((3, 15))] * 2 + [dma((3, 7))] * 4
    scratch += [dma((2, 2, 4))] * 2 + [dma((2, 2))] * 2
    return pl.pallas_call(
        layer_kernel,
        out_shape=(
            jax.ShapeDtypeStruct((1, 16, 16, 512), LOW),
            jax.ShapeDtypeStruct((1, 16, 16, 512), LOW),
        )
        + tuple(jax.ShapeDtypeStruct((8, 16, width), LOW) for width in WIDTHS),
        in_specs=[hbm, hbm, hbm, hbm, vmem, hbm],
        out_specs=(vmem,) * 5,
        scratch_shapes=scratch,
        compiler_params=pltpu.CompilerParams(
            collective_id=0, has_side_effects=True, vmem_limit_bytes=44 << 20
        ),
    )(tokens_in, cotangent, qkv_weight, out_weight, gain, ocean_mask)


def finish_kernel(
    layer_ref, grad_ref, sum_a, sum_c, sum_b, wqkv_ref, gain_ref,
    layer_out, grad_out, qkv_out, out_out, gain_out, rows, sem,
):
    lev = lax.axis_index("lev")
    first = pl.multiple_of(lev * 128, 128)
    fetch = pltpu.make_async_copy(wqkv_ref.at[pl.ds(first, 128)], rows, sem)
    fetch.start()
    layer_out[...] = layer_ref[...]
    grad_out[...] = grad_ref[...]
    out_out[...] = sum_c[...].reshape(128, 512).astype(FULL)
    for part in range(3):
        for group, source in enumerate((sum_a, sum_b)):
            at = part * 512 + group * 256
            qkv_out[:, at : at + 256] = (
                source[:, :, part * 256 : part * 256 + 256].reshape(128, 256).astype(FULL)
            )
    fetch.wait()
    total = jnp.sum(rows[...].astype(FULL) * qkv_out[...], axis=1, keepdims=True)
    line = jnp.transpose(jnp.broadcast_to(total, (128, 128)))[:1]
    gain_out[...] = line / gain_ref[:, pl.ds(first, 128)]


def finish_outputs(parts, qkv_weight, gain):
    vmem = pl.BlockSpec(memory_space=pltpu.VMEM)
    return pl.pallas_call(
        finish_kernel,
        out_shape=(
            jax.ShapeDtypeStruct((1, 16, 16, 512), LOW),
            jax.ShapeDtypeStruct((1, 16, 16, 512), LOW),
            jax.ShapeDtypeStruct((128, 1536), FULL),
            jax.ShapeDtypeStruct((128, 512), FULL),
            jax.ShapeDtypeStruct((1, 128), FULL),
        ),
        in_specs=[vmem] * 5 + [pl.BlockSpec(memory_space=pltpu.HBM), vmem],
        out_specs=(vmem,) * 5,
        scratch_shapes=[pltpu.VMEM((128, 1536), LOW), pltpu.SemaphoreType.DMA],
        compiler_params=pltpu.CompilerParams(vmem_limit_bytes=16 << 20),
    )(*parts, qkv_weight, gain)


def on_device(tokens_in, cotangent, qkv_weight, out_weight, norm_gain, ocean_mask):
    gain = norm_gain.reshape(1, 512)
    parts = layer(tokens_in, cotangent, qkv_weight, out_weight, gain, ocean_mask)
    layer_out, input_grad, qkv_grad, out_grad, gain_grad = finish_outputs(parts, qkv_weight, gain)
    return (layer_out, input_grad, qkv_grad, out_grad, gain_grad.reshape(128))


def solution(mesh):
    placed = (
        P("lev", "lat", "lon", None),
        P("lev", "lat", "lon", None),
        P(),
        P(),
        P(),
        P("lev", "lat", "lon"),
    )
    return jax.shard_map(
        on_device,
        mesh=mesh,
        in_specs=placed,
        out_specs=(
            P("lev", "lat", "lon", None),
            P("lev", "lat", "lon", None),
            P("lev", None),
            P("lev", None),
            P("lev"),
        ),
        check_vma=False,
    )
```

```python
import jax
import jax.numpy as jnp
from jax import lax
from jax.experimental import pallas as pl
from jax.experimental.pallas import tpu as pltpu
from jax.sharding import PartitionSpec as P

MESH = pl.DeviceIdType.MESH
LOW = jnp.bfloat16
FULL = jnp.float32
WIDTHS = (1024, 512, 512)
WHOLE_VMEM = 67043328


def dot_nn(left, right):
    return lax.dot_general(
        left, right, (((1,), (0,)), ((), ())), preferred_element_type=jnp.float32
    )


def dot_nt(left, right):
    return lax.dot_general(
        left, right, (((1,), (1,)), ((), ())), preferred_element_type=jnp.float32
    )


def dot_tn(left, right):
    return lax.dot_general(
        left, right, (((0,), (0,)), ((), ())), preferred_element_type=jnp.float32
    )


def norm_rows(values_in):
    center = values_in - jnp.mean(values_in, axis=-1, keepdims=True)
    spread = jnp.mean(center * center, axis=-1, keepdims=True)
    scaling = lax.rsqrt(spread + 1e-05)
    return (center * scaling, scaling)


def layer_kernel(
    tokens_ref, cot_ref, wqkv_ref, wout_ref, gain_ref, mask_ref,
    layer_ref, grad_ref, sum_0, sum_1, sum_2,
    ext, near, cots, wq, wo, gains, layer_buf, grad_buf,
    hid, keys, values, gkeys, gvalues, low_keys, low_values, ghidden, ghalo,
    qs, gb, dout, mixed, gq, probs_all, pscr, dscr, bias,
    wg_0, wg_1, wg_2, r1_0, r1_1, r1_2, a1_0, a1_1, a1_2, r2_0, r2_1, r2_2,
    a2_0, a2_1, a2_2, r3_0, r3_1, r3_2, g5_0, g5_1, g5_2,
    from_north, from_south, from_west, from_east, to_west, to_east,
    local_sem, out_sem, s_lon, v_lon, s_lat, v_lat, s_rel, v_rel, s_m, v_m,
    s_pair, v_pair, s_plane, v_plane, s_z, v_z, s_all, v_all, s_gz, v_gz, s_gx, v_gx,
):
    lon = lax.axis_index("lon")
    lat = lax.axis_index("lat")
    lev = lax.axis_index("lev")
    hi = lev // 2
    core = lev % 2
    here = hi * 8 + lon
    west = ((lon + 7) % 8, lat, lev)
    east = ((lon + 1) % 8, lat, lev)
    north = (lon, (lat + 7) % 8, lev)
    south = (lon, (lat + 1) % 8, lev)
    partner = (lon, lat, hi * 2 + 1 - core)

    def plane_peer(step):
        there = (here + step) % 16
        return there // 8, there % 8

    def window(row, col):
        return tokens_ref.at[0, row * 8 : row * 8 + 8, col * 8 : col * 8 + 8, :]

    def local(src, dst, slot):
        copy = pltpu.make_async_copy(src, dst, local_sem.at[slot])
        copy.start()
        return copy

    def remote(src, dst, send, recv, peer):
        return pltpu.make_async_remote_copy(
            src_ref=src, dst_ref=dst, send_sem=send, recv_sem=recv, device_id=peer,
            device_id_type=MESH,
        )

    def begin(copy):
        def one(step, carry):
            copy(step).start()
            return carry

        return one

    def finish(copy):
        def one(step, carry):
            copy(step).wait()
            return carry

        return one

    mask_copy = local(mask_ref.at[0], near.at[1, 1], 0)
    own = [
        local(window(row, col), ext.at[1 + row, 1 + col], 1 + row * 2 + col)
        for row in range(2)
        for col in range(2)
    ]
    wq_copy = local(wqkv_ref, wq, 5)
    cot_copy = local(cot_ref.at[0], cots, 6)
    wo_copy = local(wout_ref, wo, 7)
    gain_copy = local(gain_ref, gains, 8)

    barrier = pltpu.get_barrier_semaphore()

    def greet(peer):
        pl.semaphore_signal(barrier, inc=1, device_id=peer, device_id_type=MESH)

    def greet_plane(step, carry):
        peer_hi, peer_lon = plane_peer(step)
        greet((peer_lon, lat, peer_hi * 2 + core))
        return carry

    def greet_lat(step, carry):
        greet((lon, (lat + step) % 8, lev))
        return carry

    greet(partner)
    lax.fori_loop(1, 16, greet_plane, 0)
    lax.fori_loop(1, 8, greet_lat, 0)
    mask_copy.wait()
    pl.semaphore_wait(barrier, 23)

    mask_lon = [
        remote(near.at[1, 1], near.at[1, 2], s_m.at[0], v_m.at[0], west),
        remote(near.at[1, 1], near.at[1, 0], s_m.at[1], v_m.at[1], east),
    ]
    to_lon = []
    to_lat = []
    for row in range(2):
        to_lon.append(
            remote(window(row, 0), ext.at[1 + row, 3], s_lon.at[row, 0], v_lon.at[row, 0], west)
        )
        to_lon.append(
            remote(window(row, 1), ext.at[1 + row, 0], s_lon.at[row, 1], v_lon.at[row, 1], east)
        )
    for col in range(2):
        to_lat.append(
            remote(window(0, col), ext.at[3, 1 + col], s_lat.at[0, col], v_lat.at[0, col], north)
        )
        to_lat.append(
            remote(window(1, col), ext.at[0, 1 + col], s_lat.at[1, col], v_lat.at[1, col], south)
        )
    for copy in mask_lon + to_lon + to_lat:
        copy.start()

    gain_copy.wait()
    gain = gains[...]

    def normalise(row, col):
        normed, _ = norm_rows(ext[row, col].astype(FULL).reshape(64, 512))
        at = (row * 4 + col) * 64
        hid[at : at + 64, :] = (normed * gain).astype(LOW)

    def project(spots):
        for row, col in spots:
            normalise(row, col)
        rows = jnp.concatenate(
            [hid[(row * 4 + col) * 64 : (row * 4 + col) * 64 + 64, :] for row, col in spots], axis=0
        )
        for part, target in enumerate((keys, values)):
            first = 512 + part * 512
            result = dot_nn(rows, wq[:, first : first + 512]).astype(LOW)
            for index, (row, col) in enumerate(spots):
                at = (row * 4 + col) * 64
                target[at : at + 64, :] = result[index * 64 : index * 64 + 64]
        return rows

    token_of = lax.broadcasted_iota(jnp.int32, (128, 16), 0)
    lane_of = lax.broadcasted_iota(jnp.int32, (128, 16), 1)
    repeat_rows = jnp.where(token_of // 8 == lane_of, 1.0, 0.0).astype(LOW)
    picks = [jnp.where(lane_of == token_of % 8 + 8 * side, 1.0, 0.0) for side in range(2)]
    has_north = jnp.where(lat > 0, 1.0, 0.0).astype(FULL)
    has_south = jnp.where(lat < 7, 1.0, 0.0).astype(FULL)

    def mask_columns(tile_row, tile_col):
        tall = dot_nn(repeat_rows, near[tile_row, tile_col].astype(FULL).astype(LOW))
        return [
            jnp.broadcast_to(jnp.sum(tall * pick, axis=1, keepdims=True), (128, 128))
            for pick in picks
        ]

    for copy in own:
        copy.wait()
    oceans = [None] * 4
    centre = mask_columns(1, 1)
    for row in range(2):
        for col in range(2):
            oceans[row * 2 + col] = centre[col][row * 64 : row * 64 + 64]
    wq_copy.wait()
    rows = project(((1, 1), (1, 2), (2, 1), (2, 2)))
    qs[...] = (dot_nn(rows, wq[:, :512]) * 0.125).astype(LOW)
    for copy in mask_lon:
        copy.wait()
    mask_lat = [
        remote(near.at[1], near.at[2], s_m.at[2], v_m.at[2], north),
        remote(near.at[1], near.at[0], s_m.at[3], v_m.at[3], south),
    ]
    for copy in mask_lat:
        copy.start()
    cot_copy.wait()
    for row in range(2):
        band = cots[row * 8 : row * 8 + 8].astype(FULL)
        for col in range(2):
            at = (row * 2 + col) * 64
            piece = band[:, col * 8 : col * 8 + 8, :].reshape(64, 512)
            flags = jnp.concatenate([oceans[row * 2 + col]] * 4, axis=1)
            gb[at : at + 64, :] = (piece * flags).astype(LOW)
    wo_copy.wait()
    dout[...] = dot_nt(gb[...], wo[...]).astype(LOW)
    for row in range(4):
        gkeys[row * 256 : row * 256 + 256, :] = jnp.zeros((256, 512), FULL)
        gvalues[row * 256 : row * 256 + 256, :] = jnp.zeros((256, 512), FULL)
    relayed = []
    for row, line, peer in ((0, 3, north), (1, 0, south)):
        for side, col in ((0, 3), (1, 0)):
            to_lon[row * 2 + side].wait()
            relayed.append(
                remote(
                    ext.at[1 + row, col], ext.at[line, col],
                    s_rel.at[row, side], v_rel.at[row, side], peer,
                )
            )
            relayed[-1].start()
    project(((1, 0), (2, 0), (1, 3), (2, 3)))
    for copy in mask_lat:
        copy.wait()
    place = ((0, 1), (1, 0), (1, 1), (2, 0))
    for tile_row in range(3):
        for tile_col in range(3):
            sides = centre if (tile_row, tile_col) == (1, 1) else mask_columns(tile_row, tile_col)
            for row in range(4):
                for col in range(4):
                    if place[row][0] != tile_row or place[col][0] != tile_col:
                        continue
                    at = (row * 4 + col) * 64
                    flags = sides[place[col][1]][place[row][1] * 64 : place[row][1] * 64 + 64]
                    if row == 0:
                        flags = flags * has_north
                    if row == 3:
                        flags = flags * has_south
                    bias[at : at + 64, :] = (flags - 1.0) * 1000000000.0
    for copy in to_lat:
        copy.wait()
    project(((0, 1), (0, 2), (3, 1), (3, 2)))
    for copy in relayed:
        copy.wait()
    project(((0, 0), (0, 3), (3, 0), (3, 3)))

    block_row = lax.broadcasted_iota(jnp.int32, (256, 256), 0) // 64
    block_col = lax.broadcasted_iota(jnp.int32, (256, 256), 1) // 64
    diag = jnp.where(block_row == block_col, 1.0, 0.0).astype(FULL)
    diag_low = diag.astype(LOW)

    def fold(square):
        kept = square * diag
        return (kept[:64] + kept[64:128]) + (kept[128:192] + kept[192:])

    def shape_of(index, group):
        row, col = index // 2, index % 2
        at = slice(index * 64, index * 64 + 64)
        lanes = slice(group * 256, group * 256 + 256)
        starts = [(row + part) * 256 + col * 64 for part in range(3)]
        spans = [slice(start, start + 192) for start in starts]
        inner = [slice(part * 256 + col * 64, part * 256 + col * 64 + 192) for part in range(3)]
        slab = slice(row * 256, row * 256 + 768)
        spare = 192 if col == 0 else 0
        return at, lanes, spans, inner, slab, spare

    def spread_heads(rows):
        return jnp.concatenate([rows] * 4, axis=0) * diag_low

    def attend(index, group):
        at, lanes, spans, inner, slab, spare = shape_of(index, group)
        slot = index * 2 + group
        alive = jnp.max(oceans[index], axis=(0, 1), keepdims=True)
        for part in range(3):
            pscr[slot, part * 256 + spare : part * 256 + spare + 64, :] = jnp.zeros((64, 256), LOW)
        qbd = spread_heads(qs[at, lanes])
        dbd = spread_heads(dout[at, lanes])
        scores = [
            dot_nt(keys[span, lanes], qbd) + jnp.concatenate([bias[span, :]] * 2, axis=1)
            for span in spans
        ]
        tops = [jnp.max(part, axis=0, keepdims=True) for part in scores]
        top = jnp.maximum(jnp.maximum(tops[0], tops[1]), tops[2])
        weights = [jnp.exp(part - top) for part in scores]
        sums = [jnp.sum(part, axis=0, keepdims=True) for part in weights]
        inverse = 1.0 / (sums[0] + sums[1] + sums[2])
        for part in range(3):
            probs = weights[part] * inverse
            probs_all[slot, part] = probs
            pscr[slot, inner[part], :] = probs.astype(LOW)
        out = fold(dot_tn(pscr[slot], values[slab, lanes]))
        mixed[at, lanes] = (out * alive).astype(LOW)
        for part in range(3):
            gvalues[spans[part], lanes] += dot_nn(pscr[slot, inner[part], :], dbd)

    def retreat(index, group):
        at, lanes, spans, inner, slab, spare = shape_of(index, group)
        slot = index * 2 + group
        side = index % 2
        for part in range(3):
            dscr[side, part * 256 + spare : part * 256 + spare + 64, :] = jnp.zeros((64, 256), LOW)
        qbd = spread_heads(qs[at, lanes])
        dbd = spread_heads(dout[at, lanes])
        gprobs = [dot_nt(values[span, lanes], dbd) for span in spans]
        deltas = [
            jnp.sum(probs_all[slot, part] * gprobs[part], axis=0, keepdims=True)
            for part in range(3)
        ]
        delta = deltas[0] + deltas[1] + deltas[2]
        for part in range(3):
            dscr[side, inner[part], :] = (
                probs_all[slot, part] * (gprobs[part] - delta)
            ).astype(LOW)
        gq[at, lanes] = (fold(dot_tn(dscr[side], keys[slab, lanes])) * 0.125).astype(LOW)
        for part in range(3):
            gkeys[spans[part], lanes] += dot_nn(dscr[side, inner[part], :], qbd)

    wgs = (wg_0, wg_1, wg_2)
    r1s = (r1_0, r1_1, r1_2)
    a1s = (a1_0, a1_1, a1_2)
    r2s = (r2_0, r2_1, r2_2)
    a2s = (a2_0, a2_1, a2_2)
    r3s = (r3_0, r3_1, r3_2)
    totals = (g5_0, g5_1, g5_2)
    outputs = (sum_0, sum_1, sum_2)

    def pair_copies(chunk):
        return [
            remote(
                wgs[chunk].at[part * 2 + 1 - core], r1s[chunk].at[part],
                s_pair.at[chunk, part], v_pair.at[chunk, part], partner,
            )
            for part in range(2)
        ]

    def plane_copy(chunk):
        def one(step):
            peer_hi, peer_lon = plane_peer(step)
            return remote(
                a1s[chunk].at[peer_hi * 8 + peer_lon], r2s[chunk].at[step - 1],
                s_plane.at[chunk, step - 1], v_plane.at[chunk, step - 1],
                (peer_lon, lat, peer_hi * 2 + core),
            )

        return one

    def z_copy(chunk):
        def one(step):
            return remote(
                a2s[chunk], r3s[chunk].at[step - 1],
                s_z.at[chunk, step - 1], v_z.at[chunk, step - 1], (lon, (lat + step) % 8, lev),
            )

        return one

    def all_copy(chunk):
        def one(step):
            return remote(
                totals[chunk].at[lon], totals[chunk].at[lon],
                s_all.at[chunk, step - 1], v_all.at[chunk, step - 1],
                ((lon + step) % 8, lat, lev),
            )

        return one

    def start_pair(chunk):
        for copy in pair_copies(chunk):
            copy.start()

    def pair_to_plane(chunk):
        for part, copy in enumerate(pair_copies(chunk)):
            copy.wait()

            def add(piece, carry):
                span = pl.ds(pl.multiple_of(piece * 16, 16), 16)
                total = wgs[chunk][part * 2 + core, span, :] + r1s[chunk][part, span, :]
                a1s[chunk][part * 8 + piece] = total.astype(LOW)
                return carry

            lax.fori_loop(0, 8, add, 0)
        lax.fori_loop(1, 16, begin(plane_copy(chunk)), 0)

    def plane_to_z(chunk):
        lax.fori_loop(1, 16, finish(plane_copy(chunk)), 0)
        for first in range(0, WIDTHS[chunk], 256):
            cols = slice(first, first + 256)
            total = a1s[chunk][here, :, cols].astype(FULL)
            for step in range(15):
                total = total + r2s[chunk][step, :, cols].astype(FULL)
            a2s[chunk][:, cols] = total.astype(LOW)
        lax.fori_loop(1, 8, begin(z_copy(chunk)), 0)

    def z_to_all(chunk):
        lax.fori_loop(1, 8, finish(z_copy(chunk)), 0)
        for first in range(0, WIDTHS[chunk], 256):
            cols = slice(first, first + 256)
            total = a2s[chunk][:, cols].astype(FULL)
            for step in range(7):
                total = total + r3s[chunk][step, :, cols].astype(FULL)
            totals[chunk][lon, :, cols] = total.astype(LOW)
        lax.fori_loop(1, 8, begin(all_copy(chunk)), 0)

    corners = []
    edges = []
    for line, target, peer, side in ((0, from_south, north, 0), (3, from_north, south, 1)):
        for col in (0, 3):
            corners.append(
                remote(
                    ghalo.at[line, col], target.at[col],
                    s_gz.at[side, col], v_gz.at[side, col], peer,
                )
            )
        edges.append(
            remote(
                ghalo.at[line, pl.ds(1, 2)], target.at[pl.ds(1, 2)],
                s_gz.at[side, 1], v_gz.at[side, 1], peer,
            )
        )
    sideways = [
        remote(to_west, from_east, s_gx.at[0], v_gx.at[0], west),
        remote(to_east, from_west, s_gx.at[1], v_gx.at[1], east),
    ]
    sources = (from_north, from_south)

    def own_rows(row):
        return slice(row * 256 + 320, row * 256 + 448)

    def query_key_chunk(group):
        lanes = slice(group * 256, group * 256 + 256)
        for row in range(4):
            span = slice(row * 256, row * 256 + 256)
            low_keys[span, lanes] = gkeys[span, lanes].astype(LOW)
        query = dot_tn(hid[own_rows(0), :], gq[:128, lanes]) + dot_tn(
            hid[own_rows(1), :], gq[128:, lanes]
        )
        wgs[1 + group][:, :, :256] = query.reshape(4, 128, 256)
        wgs[1 + group][:, :, 256:] = dot_tn(hid[...], low_keys[:, lanes]).reshape(4, 128, 256)
        start_pair(1 + group)

    for group in range(2):
        for index in range(4):
            attend(index, group)
    wg_0[:, :, :512] = dot_tn(mixed[...], gb[...]).reshape(4, 128, 512)
    for row in range(4):
        span = slice(row * 256, row * 256 + 256)
        low_values[span, :] = gvalues[span, :].astype(LOW)
    wg_0[:, :, 512:] = dot_tn(hid[...], low_values[...]).reshape(4, 128, 512)
    start_pair(0)
    retreat(0, 0)
    pair_to_plane(0)
    for index in range(1, 4):
        retreat(index, 0)
    query_key_chunk(0)
    for row in range(4):
        span = slice(row * 256, row * 256 + 256)
        ghidden[span, :] = dot_nt(low_values[span, :], wq[:, 1024:])
    retreat(0, 1)
    pair_to_plane(1)
    for index in range(1, 4):
        retreat(index, 1)
    query_key_chunk(1)
    for row in (0, 3, 1, 2):
        span = slice(row * 256, row * 256 + 256)
        total = ghidden[span, :] + dot_nt(low_keys[span, :], wq[:, 512:1024])
        if row in (1, 2):
            ghidden[span, :] = total
        for col in range(4):
            if row in (0, 3) or col in (0, 3):
                ghalo[row, col] = total[col * 64 : col * 64 + 64].astype(LOW)
        if row == 3:
            for copy in corners + edges:
                copy.start()
    pair_to_plane(2)
    plane_to_z(0)
    branch = dot_nn(mixed[...], wo[...])
    for row in range(2):
        pieces = []
        for col in range(2):
            index = row * 2 + col
            flags = jnp.concatenate([oceans[index]] * 4, axis=1)
            tokens = ext[1 + row, 1 + col].astype(FULL).reshape(64, 512)
            result = tokens + flags * branch[index * 64 : index * 64 + 64]
            pieces.append(result.reshape(8, 8, 512))
        layer_buf[0, row * 8 : row * 8 + 8] = jnp.concatenate(pieces, axis=1).astype(LOW)
    layer_copy = pltpu.make_async_copy(layer_buf, layer_ref, out_sem.at[0])
    layer_copy.start()
    grad_query = dot_nt(gq[...], wq[:, :512])
    for copy in corners:
        copy.wait()
    for row in range(2):
        to_west[row] = (
            ghalo[1 + row, 0].astype(FULL) + sources[row][0].astype(FULL)
        ).astype(LOW)
        to_east[row] = (
            ghalo[1 + row, 3].astype(FULL) + sources[row][3].astype(FULL)
        ).astype(LOW)
    for copy in sideways:
        copy.start()
    plane_to_z(1)
    z_to_all(0)
    plane_to_z(2)
    z_to_all(1)
    for copy in edges + sideways:
        copy.wait()
    for row in range(2):
        pieces = []
        cot = cots[row * 8 : row * 8 + 8].astype(FULL)
        for col in range(2):
            index = row * 2 + col
            at = ((1 + row) * 4 + 1 + col) * 64
            side = (from_west, from_east)[col]
            grad_hidden = (
                grad_query[index * 64 : index * 64 + 64]
                + ghidden[at : at + 64, :]
                + sources[row][1 + col].astype(FULL)
                + side[row].astype(FULL)
            )
            normed, scaling = norm_rows(ext[1 + row, 1 + col].astype(FULL).reshape(64, 512))
            scaled = grad_hidden * gain
            correction = (
                scaled
                - jnp.mean(scaled, axis=-1, keepdims=True)
                - normed * jnp.mean(scaled * normed, axis=-1, keepdims=True)
            )
            result = cot[:, col * 8 : col * 8 + 8, :].reshape(64, 512) + scaling * correction
            pieces.append(result.reshape(8, 8, 512))
        grad_buf[0, row * 8 : row * 8 + 8] = jnp.concatenate(pieces, axis=1).astype(LOW)
    grad_copy = pltpu.make_async_copy(grad_buf, grad_ref, out_sem.at[1])
    grad_copy.start()
    z_to_all(2)
    sum_copies = [
        pltpu.make_async_copy(totals[chunk], outputs[chunk], out_sem.at[2 + chunk])
        for chunk in range(3)
    ]
    for chunk in range(3):
        lax.fori_loop(1, 8, finish(all_copy(chunk)), 0)
        sum_copies[chunk].start()
    for copy in [layer_copy, grad_copy] + sum_copies:
        copy.wait()


def layer(tokens_in, cotangent, qkv_weight, out_weight, gain, ocean_mask):
    dma = pltpu.SemaphoreType.DMA
    hbm = pl.BlockSpec(memory_space=pltpu.HBM)
    scratch = [
        pltpu.VMEM((4, 4, 8, 8, 512), LOW),
        pltpu.VMEM((3, 3, 16, 16), jnp.int32),
        pltpu.VMEM((16, 16, 512), LOW),
        pltpu.VMEM((512, 1536), LOW),
        pltpu.VMEM((512, 512), LOW),
        pltpu.VMEM((1, 512), FULL),
        pltpu.VMEM((1, 16, 16, 512), LOW),
        pltpu.VMEM((1, 16, 16, 512), LOW),
    ]
    scratch += [pltpu.VMEM((1024, 512), LOW)] * 3
    scratch += [pltpu.VMEM((1024, 512), FULL)] * 2
    scratch += [pltpu.VMEM((1024, 512), LOW)] * 2
    scratch += [pltpu.VMEM((1024, 512), FULL), pltpu.VMEM((4, 4, 64, 512), LOW)]
    scratch += [pltpu.VMEM((256, 512), LOW)] * 5
    scratch += [pltpu.VMEM((8, 3, 192, 256), FULL)]
    scratch += [pltpu.VMEM((8, 768, 256), LOW), pltpu.VMEM((2, 768, 256), LOW)]
    scratch += [pltpu.VMEM((1024, 128), FULL)]
    scratch += [pltpu.VMEM((4, 128, width), FULL) for width in WIDTHS]
    scratch += [pltpu.VMEM((2, 128, width), FULL) for width in WIDTHS]
    scratch += [pltpu.VMEM((16, 16, width), LOW) for width in WIDTHS]
    scratch += [pltpu.VMEM((15, 16, width), LOW) for width in WIDTHS]
    scratch += [pltpu.VMEM((16, width), LOW) for width in WIDTHS]
    scratch += [pltpu.VMEM((7, 16, width), LOW) for width in WIDTHS]
    scratch += [pltpu.VMEM((8, 16, width), LOW) for width in WIDTHS]
    scratch += [pltpu.VMEM((4, 64, 512), LOW)] * 2
    scratch += [pltpu.VMEM((2, 64, 512), LOW)] * 4
    scratch += [dma((9,)), dma((5,))] + [dma((2, 2))] * 6 + [dma((4,))] * 2
    scratch += [dma((3, 2))] * 2 + [dma((3, 15))] * 2 + [dma((3, 7))] * 4
    scratch += [dma((2, 4))] * 2 + [dma((2,))] * 2
    return pl.pallas_call(
        layer_kernel,
        out_shape=(
            jax.ShapeDtypeStruct((1, 16, 16, 512), LOW),
            jax.ShapeDtypeStruct((1, 16, 16, 512), LOW),
        )
        + tuple(jax.ShapeDtypeStruct((8, 16, width), LOW) for width in WIDTHS),
        in_specs=[hbm] * 6,
        out_specs=(hbm,) * 5,
        scratch_shapes=scratch,
        compiler_params=pltpu.CompilerParams(
            collective_id=0, has_side_effects=True, vmem_limit_bytes=WHOLE_VMEM
        ),
    )(tokens_in, cotangent, qkv_weight, out_weight, gain, ocean_mask)


def finish_kernel(
    layer_ref, grad_ref, sum_0, sum_1, sum_2, wqkv_ref, gain_ref,
    layer_out, grad_out, qkv_out, out_out, gain_out,
    layer_buf, grad_buf, buf_0, buf_1, buf_2, rows, gains, qkv, outs, line_buf, in_sem, out_sem,
):
    lev = lax.axis_index("lev")
    first = pl.multiple_of(lev * 128, 128)
    pairs = (
        (sum_1, buf_1), (sum_2, buf_2), (sum_0, buf_0), (wqkv_ref.at[pl.ds(first, 128)], rows),
        (gain_ref, gains), (layer_ref, layer_buf), (grad_ref, grad_buf),
    )
    fetches = [
        pltpu.make_async_copy(src, dst, in_sem.at[slot]) for slot, (src, dst) in enumerate(pairs)
    ]
    for copy in fetches:
        copy.start()
    stores = [
        pltpu.make_async_copy(src, dst, out_sem.at[slot])
        for slot, (src, dst) in enumerate(
            (
                (qkv, qkv_out), (outs, out_out), (layer_buf, layer_out), (grad_buf, grad_out),
                (line_buf, gain_out),
            )
        )
    ]
    for group, source in enumerate((buf_1, buf_2)):
        fetches[group].wait()
        for part in range(2):
            at = part * 512 + group * 256
            qkv[:, at : at + 256] = (
                source[:, :, part * 256 : part * 256 + 256].reshape(128, 256).astype(FULL)
            )
    fetches[2].wait()
    qkv[:, 1024:] = buf_0[:, :, 512:].reshape(128, 512).astype(FULL)
    stores[0].start()
    outs[...] = buf_0[:, :, :512].reshape(128, 512).astype(FULL)
    stores[1].start()
    fetches[5].wait()
    stores[2].start()
    fetches[6].wait()
    stores[3].start()
    fetches[3].wait()
    fetches[4].wait()
    total = jnp.sum(rows[...].astype(FULL) * qkv[...], axis=1, keepdims=True)
    line = jnp.transpose(jnp.broadcast_to(total, (128, 128)))[:1]
    line_buf[...] = line / gains[:, pl.ds(first, 128)]
    stores[4].start()
    for copy in stores:
        copy.wait()


def finish_outputs(parts, qkv_weight, gain):
    hbm = pl.BlockSpec(memory_space=pltpu.HBM)
    dma = pltpu.SemaphoreType.DMA
    return pl.pallas_call(
        finish_kernel,
        out_shape=(
            jax.ShapeDtypeStruct((1, 16, 16, 512), LOW),
            jax.ShapeDtypeStruct((1, 16, 16, 512), LOW),
            jax.ShapeDtypeStruct((128, 1536), FULL),
            jax.ShapeDtypeStruct((128, 512), FULL),
            jax.ShapeDtypeStruct((1, 128), FULL),
        ),
        in_specs=[hbm] * 7,
        out_specs=(hbm,) * 5,
        scratch_shapes=[pltpu.VMEM((1, 16, 16, 512), LOW)] * 2
        + [pltpu.VMEM((8, 16, width), LOW) for width in WIDTHS]
        + [
            pltpu.VMEM((128, 1536), LOW), pltpu.VMEM((1, 512), FULL),
            pltpu.VMEM((128, 1536), FULL), pltpu.VMEM((128, 512), FULL),
            pltpu.VMEM((1, 128), FULL), dma((7,)), dma((5,)),
        ],
        compiler_params=pltpu.CompilerParams(vmem_limit_bytes=WHOLE_VMEM),
    )(*parts, qkv_weight, gain)


def on_device(tokens_in, cotangent, qkv_weight, out_weight, norm_gain, ocean_mask):
    gain = norm_gain.reshape(1, 512)
    parts = layer(tokens_in, cotangent, qkv_weight, out_weight, gain, ocean_mask)
    layer_out, input_grad, qkv_grad, out_grad, gain_grad = finish_outputs(parts, qkv_weight, gain)
    return (layer_out, input_grad, qkv_grad, out_grad, gain_grad.reshape(128))


def solution(mesh):
    placed = (
        P("lev", "lat", "lon", None),
        P("lev", "lat", "lon", None),
        P(),
        P(),
        P(),
        P("lev", "lat", "lon"),
    )
    return jax.shard_map(
        on_device,
        mesh=mesh,
        in_specs=placed,
        out_specs=(
            P("lev", "lat", "lon", None),
            P("lev", "lat", "lon", None),
            P("lev", None),
            P("lev", None),
            P("lev"),
        ),
        check_vma=False,
    )
```

```python
import jax
import jax.numpy as jnp
from jax import lax
from jax.experimental import pallas as pl
from jax.experimental.pallas import tpu as pltpu
from jax.sharding import PartitionSpec as P

MESH = pl.DeviceIdType.MESH
LOW = jnp.bfloat16
FULL = jnp.float32
WIDTHS = (512, 512, 512, 512)
WHOLE_VMEM = 67043328


def dot_nn(left, right):
    return lax.dot_general(
        left, right, (((1,), (0,)), ((), ())), preferred_element_type=jnp.float32
    )


def dot_nt(left, right):
    return lax.dot_general(
        left, right, (((1,), (1,)), ((), ())), preferred_element_type=jnp.float32
    )


def dot_tn(left, right):
    return lax.dot_general(
        left, right, (((0,), (0,)), ((), ())), preferred_element_type=jnp.float32
    )


def norm_rows(values_in):
    center = values_in - jnp.mean(values_in, axis=-1, keepdims=True)
    spread = jnp.mean(center * center, axis=-1, keepdims=True)
    scaling = lax.rsqrt(spread + 1e-05)
    return (center * scaling, scaling)


def layer_kernel(
    tokens_ref, cot_ref, wqkv_ref, wout_ref, gain_ref, mask_ref,
    layer_ref, grad_ref, sum_0, sum_1, sum_2, sum_3,
    ext, near, cots, wq, wo, gains, layer_buf, grad_buf,
    hid, keys, values, gkeys, gvalues, low_keys, low_values, ghidden, ghalo,
    qs, gb, dout, mixed, gq, probs_all, pscr, dscr, bias,
    wg_0, wg_1, wg_2, wg_3, r1_0, r1_1, r1_2, r1_3, a1_0, a1_1, a1_2, a1_3, r2_0, r2_1, r2_2, r2_3,
    a2_0, a2_1, a2_2, a2_3, r3_0, r3_1, r3_2, r3_3, g5_0, g5_1, g5_2, g5_3,
    from_north, from_south, from_west, from_east, to_west, to_east,
    local_sem, out_sem, s_lon, v_lon, s_lat, v_lat, s_rel, v_rel, s_m, v_m,
    s_pair, v_pair, s_plane, v_plane, s_z, v_z, s_all, v_all, s_gz, v_gz, s_gx, v_gx,
):
    lon = lax.axis_index("lon")
    lat = lax.axis_index("lat")
    lev = lax.axis_index("lev")
    hi = lev // 2
    core = lev % 2
    here = hi * 8 + lon
    west = ((lon + 7) % 8, lat, lev)
    east = ((lon + 1) % 8, lat, lev)
    north = (lon, (lat + 7) % 8, lev)
    south = (lon, (lat + 1) % 8, lev)
    partner = (lon, lat, hi * 2 + 1 - core)

    def plane_peer(step):
        there = (here + step) & 15
        return there >> 3, there & 7

    def window(row, col):
        return tokens_ref.at[0, row * 8 : row * 8 + 8, col * 8 : col * 8 + 8, :]

    def local(src, dst, slot):
        copy = pltpu.make_async_copy(src, dst, local_sem.at[slot])
        copy.start()
        return copy

    def remote(src, dst, send, recv, peer):
        return pltpu.make_async_remote_copy(
            src_ref=src, dst_ref=dst, send_sem=send, recv_sem=recv, device_id=peer,
            device_id_type=MESH,
        )

    def begin(copy):
        def one(step, carry):
            copy(step).start()
            return carry

        return one

    def finish(copy):
        def one(step, carry):
            copy(step).wait()
            return carry

        return one

    mask_copy = local(mask_ref.at[0], near.at[1, 1], 0)
    own = [
        local(window(row, col), ext.at[1 + row, 1 + col], 1 + row * 2 + col)
        for row in range(2)
        for col in range(2)
    ]
    wq_copy = local(wqkv_ref, wq, 5)
    cot_copy = local(cot_ref.at[0], cots, 6)
    wo_copy = local(wout_ref, wo, 7)
    gain_copy = local(gain_ref, gains, 8)

    barrier = pltpu.get_barrier_semaphore()

    def greet(peer):
        pl.semaphore_signal(barrier, inc=1, device_id=peer, device_id_type=MESH)

    def greet_plane(step, carry):
        peer_hi, peer_lon = plane_peer(step)
        greet((peer_lon, lat, peer_hi * 2 + core))
        return carry

    def greet_lat(step, carry):
        greet((lon, (lat + step) % 8, lev))
        return carry

    greet(partner)
    lax.fori_loop(1, 16, greet_plane, 0)
    lax.fori_loop(1, 8, greet_lat, 0)
    mask_copy.wait()
    pl.semaphore_wait(barrier, 23)

    mask_lon = [
        remote(near.at[1, 1], near.at[1, 2], s_m.at[0], v_m.at[0], west),
        remote(near.at[1, 1], near.at[1, 0], s_m.at[1], v_m.at[1], east),
    ]
    to_lon = []
    to_lat = []
    for row in range(2):
        to_lon.append(
            remote(window(row, 0), ext.at[1 + row, 3], s_lon.at[row, 0], v_lon.at[row, 0], west)
        )
        to_lon.append(
            remote(window(row, 1), ext.at[1 + row, 0], s_lon.at[row, 1], v_lon.at[row, 1], east)
        )
    for col in range(2):
        to_lat.append(
            remote(window(0, col), ext.at[3, 1 + col], s_lat.at[0, col], v_lat.at[0, col], north)
        )
        to_lat.append(
            remote(window(1, col), ext.at[0, 1 + col], s_lat.at[1, col], v_lat.at[1, col], south)
        )
    for copy in mask_lon + to_lon + to_lat:
        copy.start()

    gain_copy.wait()
    gain = gains[...]

    def normalise(row, col):
        normed, _ = norm_rows(ext[row, col].astype(FULL).reshape(64, 512))
        at = (row * 4 + col) * 64
        hid[at : at + 64, :] = (normed * gain).astype(LOW)

    def project(spots):
        for row, col in spots:
            normalise(row, col)
        rows = jnp.concatenate(
            [hid[(row * 4 + col) * 64 : (row * 4 + col) * 64 + 64, :] for row, col in spots], axis=0
        )
        for part, target in enumerate((keys, values)):
            first = 512 + part * 512
            result = dot_nn(rows, wq[:, first : first + 512]).astype(LOW)
            for index, (row, col) in enumerate(spots):
                at = (row * 4 + col) * 64
                target[at : at + 64, :] = result[index * 64 : index * 64 + 64]
        return rows

    token_of = lax.broadcasted_iota(jnp.int32, (128, 16), 0)
    lane_of = lax.broadcasted_iota(jnp.int32, (128, 16), 1)
    repeat_rows = jnp.where(token_of // 8 == lane_of, 1.0, 0.0).astype(LOW)
    picks = [jnp.where(lane_of == token_of % 8 + 8 * side, 1.0, 0.0) for side in range(2)]
    has_north = jnp.where(lat > 0, 1.0, 0.0).astype(FULL)
    has_south = jnp.where(lat < 7, 1.0, 0.0).astype(FULL)

    def mask_columns(tile_row, tile_col):
        tall = dot_nn(repeat_rows, near[tile_row, tile_col].astype(FULL).astype(LOW))
        return [
            jnp.broadcast_to(jnp.sum(tall * pick, axis=1, keepdims=True), (128, 128))
            for pick in picks
        ]

    for copy in own:
        copy.wait()
    oceans = [None] * 4
    centre = mask_columns(1, 1)
    for row in range(2):
        for col in range(2):
            oceans[row * 2 + col] = centre[col][row * 64 : row * 64 + 64]
    wq_copy.wait()
    rows = project(((1, 1), (1, 2), (2, 1), (2, 2)))
    qs[...] = (dot_nn(rows, wq[:, :512]) * 0.125).astype(LOW)
    for copy in mask_lon:
        copy.wait()
    mask_lat = [
        remote(near.at[1], near.at[2], s_m.at[2], v_m.at[2], north),
        remote(near.at[1], near.at[0], s_m.at[3], v_m.at[3], south),
    ]
    for copy in mask_lat:
        copy.start()
    cot_copy.wait()
    for row in range(2):
        band = cots[row * 8 : row * 8 + 8].astype(FULL)
        for col in range(2):
            at = (row * 2 + col) * 64
            piece = band[:, col * 8 : col * 8 + 8, :].reshape(64, 512)
            flags = jnp.concatenate([oceans[row * 2 + col]] * 4, axis=1)
            gb[at : at + 64, :] = (piece * flags).astype(LOW)
    wo_copy.wait()
    dout[...] = dot_nt(gb[...], wo[...]).astype(LOW)
    for row in range(4):
        gkeys[row * 256 : row * 256 + 256, :] = jnp.zeros((256, 512), FULL)
        gvalues[row * 256 : row * 256 + 256, :] = jnp.zeros((256, 512), FULL)
    relayed = []
    for row, line, peer in ((0, 3, north), (1, 0, south)):
        for side, col in ((0, 3), (1, 0)):
            to_lon[row * 2 + side].wait()
            relayed.append(
                remote(
                    ext.at[1 + row, col], ext.at[line, col],
                    s_rel.at[row, side], v_rel.at[row, side], peer,
                )
            )
            relayed[-1].start()
    project(((1, 0), (2, 0), (1, 3), (2, 3)))
    for copy in mask_lat:
        copy.wait()
    place = ((0, 1), (1, 0), (1, 1), (2, 0))
    for tile_row in range(3):
        for tile_col in range(3):
            sides = centre if (tile_row, tile_col) == (1, 1) else mask_columns(tile_row, tile_col)
            for row in range(4):
                for col in range(4):
                    if place[row][0] != tile_row or place[col][0] != tile_col:
                        continue
                    at = (row * 4 + col) * 64
                    flags = sides[place[col][1]][place[row][1] * 64 : place[row][1] * 64 + 64]
                    if row == 0:
                        flags = flags * has_north
                    if row == 3:
                        flags = flags * has_south
                    bias[at : at + 64, :] = (flags - 1.0) * 1000000000.0
    for copy in to_lat:
        copy.wait()
    project(((0, 1), (0, 2), (3, 1), (3, 2)))
    for copy in relayed:
        copy.wait()
    project(((0, 0), (0, 3), (3, 0), (3, 3)))

    block_row = lax.broadcasted_iota(jnp.int32, (256, 256), 0) // 64
    block_col = lax.broadcasted_iota(jnp.int32, (256, 256), 1) // 64
    diag = jnp.where(block_row == block_col, 1.0, 0.0).astype(FULL)
    diag_low = diag.astype(LOW)

    def fold(square):
        kept = square * diag
        return (kept[:64] + kept[64:128]) + (kept[128:192] + kept[192:])

    def shape_of(index, group):
        row, col = index // 2, index % 2
        at = slice(index * 64, index * 64 + 64)
        lanes = slice(group * 256, group * 256 + 256)
        starts = [(row + part) * 256 + col * 64 for part in range(3)]
        spans = [slice(start, start + 192) for start in starts]
        inner = [slice(part * 256 + col * 64, part * 256 + col * 64 + 192) for part in range(3)]
        slab = slice(row * 256, row * 256 + 768)
        spare = 192 if col == 0 else 0
        return at, lanes, spans, inner, slab, spare

    def spread_heads(rows):
        return jnp.concatenate([rows] * 4, axis=0) * diag_low

    def attend(index, group):
        at, lanes, spans, inner, slab, spare = shape_of(index, group)
        slot = index * 2 + group
        alive = jnp.max(oceans[index], axis=(0, 1), keepdims=True)
        for part in range(3):
            pscr[slot, part * 256 + spare : part * 256 + spare + 64, :] = jnp.zeros((64, 256), LOW)
        qbd = spread_heads(qs[at, lanes])
        dbd = spread_heads(dout[at, lanes])
        scores = [
            dot_nt(keys[span, lanes], qbd) + jnp.concatenate([bias[span, :]] * 2, axis=1)
            for span in spans
        ]
        tops = [jnp.max(part, axis=0, keepdims=True) for part in scores]
        top = jnp.maximum(jnp.maximum(tops[0], tops[1]), tops[2])
        weights = [jnp.exp(part - top) for part in scores]
        sums = [jnp.sum(part, axis=0, keepdims=True) for part in weights]
        inverse = 1.0 / (sums[0] + sums[1] + sums[2])
        for part in range(3):
            probs = weights[part] * inverse
            probs_all[slot, part] = probs
            pscr[slot, inner[part], :] = probs.astype(LOW)
        out = fold(dot_tn(pscr[slot], values[slab, lanes]))
        mixed[at, lanes] = (out * alive).astype(LOW)
        for part in range(3):
            gvalues[spans[part], lanes] += dot_nn(pscr[slot, inner[part], :], dbd)

    def retreat(index, group):
        at, lanes, spans, inner, slab, spare = shape_of(index, group)
        slot = index * 2 + group
        side = index % 2
        for part in range(3):
            dscr[side, part * 256 + spare : part * 256 + spare + 64, :] = jnp.zeros((64, 256), LOW)
        qbd = spread_heads(qs[at, lanes])
        dbd = spread_heads(dout[at, lanes])
        gprobs = [dot_nt(values[span, lanes], dbd) for span in spans]
        deltas = [
            jnp.sum(probs_all[slot, part] * gprobs[part], axis=0, keepdims=True)
            for part in range(3)
        ]
        delta = deltas[0] + deltas[1] + deltas[2]
        for part in range(3):
            dscr[side, inner[part], :] = (
                probs_all[slot, part] * (gprobs[part] - delta)
            ).astype(LOW)
        gq[at, lanes] = (fold(dot_tn(dscr[side], keys[slab, lanes])) * 0.125).astype(LOW)
        for part in range(3):
            gkeys[spans[part], lanes] += dot_nn(dscr[side, inner[part], :], qbd)

    wgs = (wg_0, wg_1, wg_2, wg_3)
    r1s = (r1_0, r1_1, r1_2, r1_3)
    a1s = (a1_0, a1_1, a1_2, a1_3)
    r2s = (r2_0, r2_1, r2_2, r2_3)
    a2s = (a2_0, a2_1, a2_2, a2_3)
    r3s = (r3_0, r3_1, r3_2, r3_3)
    totals = (g5_0, g5_1, g5_2, g5_3)
    outputs = (sum_0, sum_1, sum_2, sum_3)

    def pair_copies(chunk):
        return [
            remote(
                wgs[chunk].at[part * 2 + 1 - core], r1s[chunk].at[part],
                s_pair.at[chunk, part], v_pair.at[chunk, part], partner,
            )
            for part in range(2)
        ]

    def plane_copy(chunk):
        def one(step):
            peer_hi, peer_lon = plane_peer(step)
            return remote(
                a1s[chunk].at[peer_hi * 8 + peer_lon], r2s[chunk].at[step - 1],
                s_plane.at[chunk, step - 1], v_plane.at[chunk, step - 1],
                (peer_lon, lat, peer_hi * 2 + core),
            )

        return one

    def z_copy(chunk):
        def one(step):
            return remote(
                a2s[chunk], r3s[chunk].at[step - 1],
                s_z.at[chunk, step - 1], v_z.at[chunk, step - 1], (lon, (lat + step) % 8, lev),
            )

        return one

    def all_copy(chunk):
        def one(step):
            return remote(
                totals[chunk].at[lon], totals[chunk].at[lon],
                s_all.at[chunk, step - 1], v_all.at[chunk, step - 1],
                ((lon + step) % 8, lat, lev),
            )

        return one

    def start_pair(chunk):
        for copy in pair_copies(chunk):
            copy.start()

    def pair_to_plane(chunk):
        for part, copy in enumerate(pair_copies(chunk)):
            copy.wait()

            def add(piece, carry):
                span = pl.ds(pl.multiple_of(piece * 16, 16), 16)
                total = wgs[chunk][part * 2 + core, span, :] + r1s[chunk][part, span, :]
                a1s[chunk][part * 8 + piece] = total.astype(LOW)
                return carry

            lax.fori_loop(0, 8, add, 0)
        lax.fori_loop(1, 16, begin(plane_copy(chunk)), 0)

    def plane_to_z(chunk):
        lax.fori_loop(1, 16, finish(plane_copy(chunk)), 0)
        for first in range(0, WIDTHS[chunk], 256):
            cols = slice(first, first + 256)
            total = a1s[chunk][here, :, cols].astype(FULL)
            for step in range(15):
                total = total + r2s[chunk][step, :, cols].astype(FULL)
            a2s[chunk][:, cols] = total.astype(LOW)
        lax.fori_loop(1, 8, begin(z_copy(chunk)), 0)

    def z_to_all(chunk):
        lax.fori_loop(1, 8, finish(z_copy(chunk)), 0)
        for first in range(0, WIDTHS[chunk], 256):
            cols = slice(first, first + 256)
            total = a2s[chunk][:, cols].astype(FULL)
            for step in range(7):
                total = total + r3s[chunk][step, :, cols].astype(FULL)
            totals[chunk][lon, :, cols] = total.astype(LOW)
        lax.fori_loop(1, 8, begin(all_copy(chunk)), 0)

    corners = []
    edges = []
    for line, target, peer, side in ((0, from_south, north, 0), (3, from_north, south, 1)):
        for col in (0, 3):
            corners.append(
                remote(
                    ghalo.at[line, col], target.at[col],
                    s_gz.at[side, col], v_gz.at[side, col], peer,
                )
            )
        edges.append(
            remote(
                ghalo.at[line, pl.ds(1, 2)], target.at[pl.ds(1, 2)],
                s_gz.at[side, 1], v_gz.at[side, 1], peer,
            )
        )
    sideways = [
        remote(to_west, from_east, s_gx.at[0], v_gx.at[0], west),
        remote(to_east, from_west, s_gx.at[1], v_gx.at[1], east),
    ]
    sources = (from_north, from_south)

    def own_rows(row):
        return slice(row * 256 + 320, row * 256 + 448)

    def query_key_chunk(group):
        lanes = slice(group * 256, group * 256 + 256)
        for row in range(4):
            span = slice(row * 256, row * 256 + 256)
            low_keys[span, lanes] = gkeys[span, lanes].astype(LOW)
        query = dot_tn(hid[own_rows(0), :], gq[:128, lanes]) + dot_tn(
            hid[own_rows(1), :], gq[128:, lanes]
        )
        wgs[2 + group][:, :, :256] = query.reshape(4, 128, 256)
        wgs[2 + group][:, :, 256:] = dot_tn(hid[...], low_keys[:, lanes]).reshape(4, 128, 256)
        start_pair(2 + group)

    for group in range(2):
        for index in range(4):
            attend(index, group)
    wg_0[...] = dot_tn(mixed[...], gb[...]).reshape(4, 128, 512)
    start_pair(0)
    for row in range(4):
        span = slice(row * 256, row * 256 + 256)
        low_values[span, :] = gvalues[span, :].astype(LOW)
    wg_1[...] = dot_tn(hid[...], low_values[...]).reshape(4, 128, 512)
    start_pair(1)
    retreat(0, 0)
    retreat(1, 0)
    pair_to_plane(0)
    retreat(2, 0)
    pair_to_plane(1)
    retreat(3, 0)
    query_key_chunk(0)
    for row in range(4):
        span = slice(row * 256, row * 256 + 256)
        ghidden[span, :] = dot_nt(low_values[span, :], wq[:, 1024:])
    retreat(0, 1)
    retreat(1, 1)
    pair_to_plane(2)
    retreat(2, 1)
    plane_to_z(0)
    retreat(3, 1)
    query_key_chunk(1)
    for row in (0, 3, 1, 2):
        span = slice(row * 256, row * 256 + 256)
        total = ghidden[span, :] + dot_nt(low_keys[span, :], wq[:, 512:1024])
        if row in (1, 2):
            ghidden[span, :] = total
        for col in range(4):
            if row in (0, 3) or col in (0, 3):
                ghalo[row, col] = total[col * 64 : col * 64 + 64].astype(LOW)
        if row == 3:
            for copy in corners + edges:
                copy.start()
    pair_to_plane(3)
    plane_to_z(1)
    branch = dot_nn(mixed[...], wo[...])
    for row in range(2):
        pieces = []
        for col in range(2):
            index = row * 2 + col
            flags = jnp.concatenate([oceans[index]] * 4, axis=1)
            tokens = ext[1 + row, 1 + col].astype(FULL).reshape(64, 512)
            result = tokens + flags * branch[index * 64 : index * 64 + 64]
            pieces.append(result.reshape(8, 8, 512))
        layer_buf[0, row * 8 : row * 8 + 8] = jnp.concatenate(pieces, axis=1).astype(LOW)
    layer_copy = pltpu.make_async_copy(layer_buf, layer_ref, out_sem.at[0])
    layer_copy.start()
    grad_query = dot_nt(gq[...], wq[:, :512])
    z_to_all(0)
    for copy in corners:
        copy.wait()
    for row in range(2):
        to_west[row] = (
            ghalo[1 + row, 0].astype(FULL) + sources[row][0].astype(FULL)
        ).astype(LOW)
        to_east[row] = (
            ghalo[1 + row, 3].astype(FULL) + sources[row][3].astype(FULL)
        ).astype(LOW)
    for copy in sideways:
        copy.start()
    plane_to_z(2)
    z_to_all(1)
    plane_to_z(3)
    z_to_all(2)
    for copy in edges + sideways:
        copy.wait()
    for row in range(2):
        pieces = []
        cot = cots[row * 8 : row * 8 + 8].astype(FULL)
        for col in range(2):
            index = row * 2 + col
            at = ((1 + row) * 4 + 1 + col) * 64
            side = (from_west, from_east)[col]
            grad_hidden = (
                grad_query[index * 64 : index * 64 + 64]
                + ghidden[at : at + 64, :]
                + sources[row][1 + col].astype(FULL)
                + side[row].astype(FULL)
            )
            normed, scaling = norm_rows(ext[1 + row, 1 + col].astype(FULL).reshape(64, 512))
            scaled = grad_hidden * gain
            correction = (
                scaled
                - jnp.mean(scaled, axis=-1, keepdims=True)
                - normed * jnp.mean(scaled * normed, axis=-1, keepdims=True)
            )
            result = cot[:, col * 8 : col * 8 + 8, :].reshape(64, 512) + scaling * correction
            pieces.append(result.reshape(8, 8, 512))
        grad_buf[0, row * 8 : row * 8 + 8] = jnp.concatenate(pieces, axis=1).astype(LOW)
    grad_copy = pltpu.make_async_copy(grad_buf, grad_ref, out_sem.at[1])
    grad_copy.start()
    z_to_all(3)
    sum_copies = [
        pltpu.make_async_copy(totals[chunk], outputs[chunk], out_sem.at[2 + chunk])
        for chunk in range(4)
    ]
    for chunk in range(4):
        lax.fori_loop(1, 8, finish(all_copy(chunk)), 0)
        sum_copies[chunk].start()
    for copy in [layer_copy, grad_copy] + sum_copies:
        copy.wait()


def layer(tokens_in, cotangent, qkv_weight, out_weight, gain, ocean_mask):
    dma = pltpu.SemaphoreType.DMA
    hbm = pl.BlockSpec(memory_space=pltpu.HBM)
    scratch = [
        pltpu.VMEM((4, 4, 8, 8, 512), LOW),
        pltpu.VMEM((3, 3, 16, 16), jnp.int32),
        pltpu.VMEM((16, 16, 512), LOW),
        pltpu.VMEM((512, 1536), LOW),
        pltpu.VMEM((512, 512), LOW),
        pltpu.VMEM((1, 512), FULL),
        pltpu.VMEM((1, 16, 16, 512), LOW),
        pltpu.VMEM((1, 16, 16, 512), LOW),
    ]
    scratch += [pltpu.VMEM((1024, 512), LOW)] * 3
    scratch += [pltpu.VMEM((1024, 512), FULL)] * 2
    scratch += [pltpu.VMEM((1024, 512), LOW)] * 2
    scratch += [pltpu.VMEM((1024, 512), FULL), pltpu.VMEM((4, 4, 64, 512), LOW)]
    scratch += [pltpu.VMEM((256, 512), LOW)] * 5
    scratch += [pltpu.VMEM((8, 3, 192, 256), FULL)]
    scratch += [pltpu.VMEM((8, 768, 256), LOW), pltpu.VMEM((2, 768, 256), LOW)]
    scratch += [pltpu.VMEM((1024, 128), FULL)]
    scratch += [pltpu.VMEM((4, 128, width), FULL) for width in WIDTHS]
    scratch += [pltpu.VMEM((2, 128, width), FULL) for width in WIDTHS]
    scratch += [pltpu.VMEM((16, 16, width), LOW) for width in WIDTHS]
    scratch += [pltpu.VMEM((15, 16, width), LOW) for width in WIDTHS]
    scratch += [pltpu.VMEM((16, width), LOW) for width in WIDTHS]
    scratch += [pltpu.VMEM((7, 16, width), LOW) for width in WIDTHS]
    scratch += [pltpu.VMEM((8, 16, width), LOW) for width in WIDTHS]
    scratch += [pltpu.VMEM((4, 64, 512), LOW)] * 2
    scratch += [pltpu.VMEM((2, 64, 512), LOW)] * 4
    scratch += [dma((9,)), dma((6,))] + [dma((2, 2))] * 6 + [dma((4,))] * 2
    scratch += [dma((4, 2))] * 2 + [dma((4, 15))] * 2 + [dma((4, 7))] * 4
    scratch += [dma((2, 4))] * 2 + [dma((2,))] * 2
    return pl.pallas_call(
        layer_kernel,
        out_shape=(
            jax.ShapeDtypeStruct((1, 16, 16, 512), LOW),
            jax.ShapeDtypeStruct((1, 16, 16, 512), LOW),
        )
        + tuple(jax.ShapeDtypeStruct((8, 16, width), LOW) for width in WIDTHS),
        in_specs=[hbm] * 6,
        out_specs=(hbm,) * 6,
        scratch_shapes=scratch,
        compiler_params=pltpu.CompilerParams(
            collective_id=0, has_side_effects=True, vmem_limit_bytes=WHOLE_VMEM
        ),
    )(tokens_in, cotangent, qkv_weight, out_weight, gain, ocean_mask)


def finish_kernel(
    layer_ref, grad_ref, sum_0, sum_1, sum_2, sum_3, wqkv_ref, gain_ref,
    layer_out, grad_out, qkv_out, out_out, gain_out,
    layer_buf, grad_buf, buf_0, buf_1, buf_2, buf_3, rows, gains, qkv, outs, line_buf, in_sem,
    out_sem,
):
    lev = lax.axis_index("lev")
    first = pl.multiple_of(lev * 128, 128)
    pairs = (
        (sum_2, buf_2), (sum_3, buf_3), (sum_1, buf_1), (sum_0, buf_0), (wqkv_ref.at[pl.ds(first, 128)], rows),
        (gain_ref, gains), (layer_ref, layer_buf), (grad_ref, grad_buf),
    )
    fetches = [
        pltpu.make_async_copy(src, dst, in_sem.at[slot]) for slot, (src, dst) in enumerate(pairs)
    ]
    for copy in fetches:
        copy.start()
    stores = [
        pltpu.make_async_copy(src, dst, out_sem.at[slot])
        for slot, (src, dst) in enumerate(
            (
                (qkv, qkv_out), (outs, out_out), (layer_buf, layer_out), (grad_buf, grad_out),
                (line_buf, gain_out),
            )
        )
    ]
    for group, source in enumerate((buf_2, buf_3)):
        fetches[group].wait()
        for part in range(2):
            at = part * 512 + group * 256
            qkv[:, at : at + 256] = (
                source[:, :, part * 256 : part * 256 + 256].reshape(128, 256).astype(FULL)
            )
    fetches[2].wait()
    qkv[:, 1024:] = buf_1[...].reshape(128, 512).astype(FULL)
    stores[0].start()
    fetches[3].wait()
    outs[...] = buf_0[...].reshape(128, 512).astype(FULL)
    stores[1].start()
    fetches[6].wait()
    stores[2].start()
    fetches[7].wait()
    stores[3].start()
    fetches[4].wait()
    fetches[5].wait()
    total = jnp.sum(rows[...].astype(FULL) * qkv[...], axis=1, keepdims=True)
    line = jnp.transpose(jnp.broadcast_to(total, (128, 128)))[:1]
    line_buf[...] = line / gains[:, pl.ds(first, 128)]
    stores[4].start()
    for copy in stores:
        copy.wait()


def finish_outputs(parts, qkv_weight, gain):
    hbm = pl.BlockSpec(memory_space=pltpu.HBM)
    dma = pltpu.SemaphoreType.DMA
    return pl.pallas_call(
        finish_kernel,
        out_shape=(
            jax.ShapeDtypeStruct((1, 16, 16, 512), LOW),
            jax.ShapeDtypeStruct((1, 16, 16, 512), LOW),
            jax.ShapeDtypeStruct((128, 1536), FULL),
            jax.ShapeDtypeStruct((128, 512), FULL),
            jax.ShapeDtypeStruct((1, 128), FULL),
        ),
        in_specs=[hbm] * 8,
        out_specs=(hbm,) * 5,
        scratch_shapes=[pltpu.VMEM((1, 16, 16, 512), LOW)] * 2
        + [pltpu.VMEM((8, 16, width), LOW) for width in WIDTHS]
        + [
            pltpu.VMEM((128, 1536), LOW), pltpu.VMEM((1, 512), FULL),
            pltpu.VMEM((128, 1536), FULL), pltpu.VMEM((128, 512), FULL),
            pltpu.VMEM((1, 128), FULL), dma((8,)), dma((5,)),
        ],
        compiler_params=pltpu.CompilerParams(vmem_limit_bytes=WHOLE_VMEM),
    )(*parts, qkv_weight, gain)


def on_device(tokens_in, cotangent, qkv_weight, out_weight, norm_gain, ocean_mask):
    gain = norm_gain.reshape(1, 512)
    parts = layer(tokens_in, cotangent, qkv_weight, out_weight, gain, ocean_mask)
    layer_out, input_grad, qkv_grad, out_grad, gain_grad = finish_outputs(parts, qkv_weight, gain)
    return (layer_out, input_grad, qkv_grad, out_grad, gain_grad.reshape(128))


def solution(mesh):
    placed = (
        P("lev", "lat", "lon", None),
        P("lev", "lat", "lon", None),
        P(),
        P(),
        P(),
        P("lev", "lat", "lon"),
    )
    return jax.shard_map(
        on_device,
        mesh=mesh,
        in_specs=placed,
        out_specs=(
            P("lev", "lat", "lon", None),
            P("lev", "lat", "lon", None),
            P("lev", None),
            P("lev", None),
            P("lev"),
        ),
        check_vma=False,
    )
```

```python
import jax
import jax.numpy as jnp
from jax import lax
from jax.experimental import pallas as pl
from jax.experimental.pallas import tpu as pltpu
from jax.sharding import PartitionSpec as P

MESH = pl.DeviceIdType.MESH
LOW = jnp.bfloat16
FULL = jnp.float32
WIDTHS = (512, 512, 512, 512)
WHOLE_VMEM = 67043328


def dot_nn(left, right):
    return lax.dot_general(
        left, right, (((1,), (0,)), ((), ())), preferred_element_type=jnp.float32
    )


def dot_nt(left, right):
    return lax.dot_general(
        left, right, (((1,), (1,)), ((), ())), preferred_element_type=jnp.float32
    )


def dot_tn(left, right):
    return lax.dot_general(
        left, right, (((0,), (0,)), ((), ())), preferred_element_type=jnp.float32
    )


def norm_rows(values_in):
    center = values_in - jnp.mean(values_in, axis=-1, keepdims=True)
    spread = jnp.mean(center * center, axis=-1, keepdims=True)
    scaling = lax.rsqrt(spread + 1e-05)
    return (center * scaling, scaling)


def layer_kernel(
    tokens_ref, cot_ref, wqkv_ref, wout_ref, gain_ref, mask_ref,
    layer_ref, grad_ref, sum_0, sum_1, sum_2, sum_3,
    ext, near, cots, wq, wo, gains, layer_buf, grad_buf,
    hid, keys, values, gkeys, gvalues, low_keys, low_values, ghidden, ghalo,
    qs, gb, dout, mixed, gq, probs_all, pscr, dscr, bias,
    wg_0, wg_1, wg_2, wg_3, r1_0, r1_1, r1_2, r1_3, a1_0, a1_1, a1_2, a1_3, r2_0, r2_1, r2_2, r2_3,
    a2_0, a2_1, a2_2, a2_3, r3_0, r3_1, r3_2, r3_3, g5_0, g5_1, g5_2, g5_3,
    from_north, from_south, from_west, from_east, to_west, to_east,
    ready, local_sem, out_sem, s_lon, v_lon, s_lat, v_lat, s_rel, v_rel, s_m, v_m,
    s_pair, v_pair, s_plane, v_plane, s_z, v_z, s_all, v_all, s_gz, v_gz, s_gx, v_gx,
):
    lon = lax.axis_index("lon")
    lat = lax.axis_index("lat")
    lev = lax.axis_index("lev")
    hi = lev // 2
    core = lev % 2
    here = hi * 8 + lon
    west = ((lon + 7) % 8, lat, lev)
    east = ((lon + 1) % 8, lat, lev)
    north = (lon, (lat + 7) % 8, lev)
    south = (lon, (lat + 1) % 8, lev)
    partner = (lon, lat, hi * 2 + 1 - core)

    def plane_peer(step):
        there = (here + step) & 15
        return there >> 3, there & 7

    def window(row, col):
        return tokens_ref.at[0, row * 8 : row * 8 + 8, col * 8 : col * 8 + 8, :]

    def local(src, dst, slot):
        copy = pltpu.make_async_copy(src, dst, local_sem.at[slot])
        copy.start()
        return copy

    def remote(src, dst, send, recv, peer):
        return pltpu.make_async_remote_copy(
            src_ref=src, dst_ref=dst, send_sem=send, recv_sem=recv, device_id=peer,
            device_id_type=MESH,
        )

    def begin(copy):
        def one(step, carry):
            copy(step).start()
            return carry

        return one

    def finish(copy):
        def one(step, carry):
            copy(step).wait()
            return carry

        return one

    mask_copy = local(mask_ref.at[0], near.at[1, 1], 0)
    own = [
        local(window(row, col), ext.at[1 + row, 1 + col], 1 + row * 2 + col)
        for row in range(2)
        for col in range(2)
    ]
    wq_copy = local(wqkv_ref, wq, 5)
    cot_copy = local(cot_ref.at[0], cots, 6)
    wo_copy = local(wout_ref, wo, 7)
    gain_copy = local(gain_ref, gains, 8)

    barrier = pltpu.get_barrier_semaphore()

    def greet(peer):
        pl.semaphore_signal(barrier, inc=1, device_id=peer, device_id_type=MESH)

    close = (west, east, north, south, partner, (lon, lat, (1 - hi) * 2 + core))
    for peer in close:
        greet(peer)

    def spread_word(turn):
        if turn:
            pl.semaphore_wait(ready.at[turn - 1], 6)
        if turn < 4:
            for peer in close:
                pl.semaphore_signal(
                    ready.at[turn], inc=1, device_id=peer, device_id_type=MESH
                )

    mask_copy.wait()
    pl.semaphore_wait(barrier, 6)

    mask_lon = [
        remote(near.at[1, 1], near.at[1, 2], s_m.at[0], v_m.at[0], west),
        remote(near.at[1, 1], near.at[1, 0], s_m.at[1], v_m.at[1], east),
    ]
    to_lon = []
    to_lat = []
    for row in range(2):
        to_lon.append(
            remote(window(row, 0), ext.at[1 + row, 3], s_lon.at[row, 0], v_lon.at[row, 0], west)
        )
        to_lon.append(
            remote(window(row, 1), ext.at[1 + row, 0], s_lon.at[row, 1], v_lon.at[row, 1], east)
        )
    for col in range(2):
        to_lat.append(
            remote(window(0, col), ext.at[3, 1 + col], s_lat.at[0, col], v_lat.at[0, col], north)
        )
        to_lat.append(
            remote(window(1, col), ext.at[0, 1 + col], s_lat.at[1, col], v_lat.at[1, col], south)
        )
    for copy in mask_lon + to_lon + to_lat:
        copy.start()
    spread_word(0)

    gain_copy.wait()
    gain = gains[...]

    def normalise(row, col):
        normed, _ = norm_rows(ext[row, col].astype(FULL).reshape(64, 512))
        at = (row * 4 + col) * 64
        hid[at : at + 64, :] = (normed * gain).astype(LOW)

    def project(spots):
        for row, col in spots:
            normalise(row, col)
        rows = jnp.concatenate(
            [hid[(row * 4 + col) * 64 : (row * 4 + col) * 64 + 64, :] for row, col in spots], axis=0
        )
        for part, target in enumerate((keys, values)):
            first = 512 + part * 512
            result = dot_nn(rows, wq[:, first : first + 512]).astype(LOW)
            for index, (row, col) in enumerate(spots):
                at = (row * 4 + col) * 64
                target[at : at + 64, :] = result[index * 64 : index * 64 + 64]
        return rows

    token_of = lax.broadcasted_iota(jnp.int32, (128, 16), 0)
    lane_of = lax.broadcasted_iota(jnp.int32, (128, 16), 1)
    repeat_rows = jnp.where(token_of // 8 == lane_of, 1.0, 0.0).astype(LOW)
    picks = [jnp.where(lane_of == token_of % 8 + 8 * side, 1.0, 0.0) for side in range(2)]
    has_north = jnp.where(lat > 0, 1.0, 0.0).astype(FULL)
    has_south = jnp.where(lat < 7, 1.0, 0.0).astype(FULL)

    def mask_columns(tile_row, tile_col):
        tall = dot_nn(repeat_rows, near[tile_row, tile_col].astype(FULL).astype(LOW))
        return [
            jnp.broadcast_to(jnp.sum(tall * pick, axis=1, keepdims=True), (128, 128))
            for pick in picks
        ]

    for copy in own:
        copy.wait()
    oceans = [None] * 4
    centre = mask_columns(1, 1)
    for row in range(2):
        for col in range(2):
            oceans[row * 2 + col] = centre[col][row * 64 : row * 64 + 64]
    wq_copy.wait()
    rows = project(((1, 1), (1, 2), (2, 1), (2, 2)))
    qs[...] = (dot_nn(rows, wq[:, :512]) * 0.125).astype(LOW)
    spread_word(1)
    for copy in mask_lon:
        copy.wait()
    mask_lat = [
        remote(near.at[1], near.at[2], s_m.at[2], v_m.at[2], north),
        remote(near.at[1], near.at[0], s_m.at[3], v_m.at[3], south),
    ]
    for copy in mask_lat:
        copy.start()
    cot_copy.wait()
    for row in range(2):
        band = cots[row * 8 : row * 8 + 8].astype(FULL)
        for col in range(2):
            at = (row * 2 + col) * 64
            piece = band[:, col * 8 : col * 8 + 8, :].reshape(64, 512)
            flags = jnp.concatenate([oceans[row * 2 + col]] * 4, axis=1)
            gb[at : at + 64, :] = (piece * flags).astype(LOW)
    wo_copy.wait()
    dout[...] = dot_nt(gb[...], wo[...]).astype(LOW)
    for row in range(4):
        gkeys[row * 256 : row * 256 + 256, :] = jnp.zeros((256, 512), FULL)
        gvalues[row * 256 : row * 256 + 256, :] = jnp.zeros((256, 512), FULL)
    spread_word(2)
    relayed = []
    for row, line, peer in ((0, 3, north), (1, 0, south)):
        for side, col in ((0, 3), (1, 0)):
            to_lon[row * 2 + side].wait()
            relayed.append(
                remote(
                    ext.at[1 + row, col], ext.at[line, col],
                    s_rel.at[row, side], v_rel.at[row, side], peer,
                )
            )
            relayed[-1].start()
    project(((1, 0), (2, 0), (1, 3), (2, 3)))
    for copy in mask_lat:
        copy.wait()
    place = ((0, 1), (1, 0), (1, 1), (2, 0))
    for tile_row in range(3):
        for tile_col in range(3):
            sides = centre if (tile_row, tile_col) == (1, 1) else mask_columns(tile_row, tile_col)
            for row in range(4):
                for col in range(4):
                    if place[row][0] != tile_row or place[col][0] != tile_col:
                        continue
                    at = (row * 4 + col) * 64
                    flags = sides[place[col][1]][place[row][1] * 64 : place[row][1] * 64 + 64]
                    if row == 0:
                        flags = flags * has_north
                    if row == 3:
                        flags = flags * has_south
                    bias[at : at + 64, :] = (flags - 1.0) * 1000000000.0
    spread_word(3)
    for copy in to_lat:
        copy.wait()
    project(((0, 1), (0, 2), (3, 1), (3, 2)))
    spread_word(4)
    for copy in relayed:
        copy.wait()
    project(((0, 0), (0, 3), (3, 0), (3, 3)))

    block_row = lax.broadcasted_iota(jnp.int32, (256, 256), 0) // 64
    block_col = lax.broadcasted_iota(jnp.int32, (256, 256), 1) // 64
    diag = jnp.where(block_row == block_col, 1.0, 0.0).astype(FULL)
    diag_low = diag.astype(LOW)

    def fold(square):
        kept = square * diag
        return (kept[:64] + kept[64:128]) + (kept[128:192] + kept[192:])

    def shape_of(index, group):
        row, col = index // 2, index % 2
        at = slice(index * 64, index * 64 + 64)
        lanes = slice(group * 256, group * 256 + 256)
        starts = [(row + part) * 256 + col * 64 for part in range(3)]
        spans = [slice(start, start + 192) for start in starts]
        inner = [slice(part * 256 + col * 64, part * 256 + col * 64 + 192) for part in range(3)]
        slab = slice(row * 256, row * 256 + 768)
        spare = 192 if col == 0 else 0
        return at, lanes, spans, inner, slab, spare

    def spread_heads(rows):
        return jnp.concatenate([rows] * 4, axis=0) * diag_low

    def attend(index, group):
        at, lanes, spans, inner, slab, spare = shape_of(index, group)
        slot = index * 2 + group
        alive = jnp.max(oceans[index], axis=(0, 1), keepdims=True)
        for part in range(3):
            pscr[slot, part * 256 + spare : part * 256 + spare + 64, :] = jnp.zeros((64, 256), LOW)
        qbd = spread_heads(qs[at, lanes])
        dbd = spread_heads(dout[at, lanes])
        scores = [
            dot_nt(keys[span, lanes], qbd) + jnp.concatenate([bias[span, :]] * 2, axis=1)
            for span in spans
        ]
        tops = [jnp.max(part, axis=0, keepdims=True) for part in scores]
        top = jnp.maximum(jnp.maximum(tops[0], tops[1]), tops[2])
        weights = [jnp.exp(part - top) for part in scores]
        sums = [jnp.sum(part, axis=0, keepdims=True) for part in weights]
        inverse = 1.0 / (sums[0] + sums[1] + sums[2])
        for part in range(3):
            probs = weights[part] * inverse
            probs_all[slot, part] = probs
            pscr[slot, inner[part], :] = probs.astype(LOW)
        out = fold(dot_tn(pscr[slot], values[slab, lanes]))
        mixed[at, lanes] = (out * alive).astype(LOW)
        for part in range(3):
            gvalues[spans[part], lanes] += dot_nn(pscr[slot, inner[part], :], dbd)

    def retreat(index, group):
        at, lanes, spans, inner, slab, spare = shape_of(index, group)
        slot = index * 2 + group
        side = index % 2
        for part in range(3):
            dscr[side, part * 256 + spare : part * 256 + spare + 64, :] = jnp.zeros((64, 256), LOW)
        qbd = spread_heads(qs[at, lanes])
        dbd = spread_heads(dout[at, lanes])
        gprobs = [dot_nt(values[span, lanes], dbd) for span in spans]
        deltas = [
            jnp.sum(probs_all[slot, part] * gprobs[part], axis=0, keepdims=True)
            for part in range(3)
        ]
        delta = deltas[0] + deltas[1] + deltas[2]
        for part in range(3):
            dscr[side, inner[part], :] = (
                probs_all[slot, part] * (gprobs[part] - delta)
            ).astype(LOW)
        gq[at, lanes] = (fold(dot_tn(dscr[side], keys[slab, lanes])) * 0.125).astype(LOW)
        for part in range(3):
            gkeys[spans[part], lanes] += dot_nn(dscr[side, inner[part], :], qbd)

    wgs = (wg_0, wg_1, wg_2, wg_3)
    r1s = (r1_0, r1_1, r1_2, r1_3)
    a1s = (a1_0, a1_1, a1_2, a1_3)
    r2s = (r2_0, r2_1, r2_2, r2_3)
    a2s = (a2_0, a2_1, a2_2, a2_3)
    r3s = (r3_0, r3_1, r3_2, r3_3)
    totals = (g5_0, g5_1, g5_2, g5_3)
    outputs = (sum_0, sum_1, sum_2, sum_3)

    def pair_copies(chunk):
        return [
            remote(
                wgs[chunk].at[part * 2 + 1 - core], r1s[chunk].at[part],
                s_pair.at[chunk, part], v_pair.at[chunk, part], partner,
            )
            for part in range(2)
        ]

    def plane_copy(chunk):
        def one(step):
            peer_hi, peer_lon = plane_peer(step)
            return remote(
                a1s[chunk].at[peer_hi * 8 + peer_lon], r2s[chunk].at[step - 1],
                s_plane.at[chunk, step - 1], v_plane.at[chunk, step - 1],
                (peer_lon, lat, peer_hi * 2 + core),
            )

        return one

    def z_copy(chunk):
        def one(step):
            return remote(
                a2s[chunk], r3s[chunk].at[step - 1],
                s_z.at[chunk, step - 1], v_z.at[chunk, step - 1], (lon, (lat + step) % 8, lev),
            )

        return one

    def all_copy(chunk):
        def one(step):
            return remote(
                totals[chunk].at[lon], totals[chunk].at[lon],
                s_all.at[chunk, step - 1], v_all.at[chunk, step - 1],
                ((lon + step) % 8, lat, lev),
            )

        return one

    def start_pair(chunk):
        for copy in pair_copies(chunk):
            copy.start()

    def pair_to_plane(chunk):
        for part, copy in enumerate(pair_copies(chunk)):
            copy.wait()

            def add(piece, carry):
                span = pl.ds(pl.multiple_of(piece * 16, 16), 16)
                total = wgs[chunk][part * 2 + core, span, :] + r1s[chunk][part, span, :]
                a1s[chunk][part * 8 + piece] = total.astype(LOW)
                return carry

            lax.fori_loop(0, 8, add, 0)
        lax.fori_loop(1, 16, begin(plane_copy(chunk)), 0)

    def plane_to_z(chunk):
        lax.fori_loop(1, 16, finish(plane_copy(chunk)), 0)
        for first in range(0, WIDTHS[chunk], 256):
            cols = slice(first, first + 256)
            total = a1s[chunk][here, :, cols].astype(FULL)
            for step in range(15):
                total = total + r2s[chunk][step, :, cols].astype(FULL)
            a2s[chunk][:, cols] = total.astype(LOW)
        lax.fori_loop(1, 8, begin(z_copy(chunk)), 0)

    def z_to_all(chunk):
        lax.fori_loop(1, 8, finish(z_copy(chunk)), 0)
        for first in range(0, WIDTHS[chunk], 256):
            cols = slice(first, first + 256)
            total = a2s[chunk][:, cols].astype(FULL)
            for step in range(7):
                total = total + r3s[chunk][step, :, cols].astype(FULL)
            totals[chunk][lon, :, cols] = total.astype(LOW)
        lax.fori_loop(1, 8, begin(all_copy(chunk)), 0)

    corners = []
    edges = []
    for line, target, peer, side in ((0, from_south, north, 0), (3, from_north, south, 1)):
        for col in (0, 3):
            corners.append(
                remote(
                    ghalo.at[line, col], target.at[col],
                    s_gz.at[side, col], v_gz.at[side, col], peer,
                )
            )
        edges.append(
            remote(
                ghalo.at[line, pl.ds(1, 2)], target.at[pl.ds(1, 2)],
                s_gz.at[side, 1], v_gz.at[side, 1], peer,
            )
        )
    sideways = [
        remote(to_west, from_east, s_gx.at[0], v_gx.at[0], west),
        remote(to_east, from_west, s_gx.at[1], v_gx.at[1], east),
    ]
    sources = (from_north, from_south)

    def own_rows(row):
        return slice(row * 256 + 320, row * 256 + 448)

    def query_key_chunk(group):
        lanes = slice(group * 256, group * 256 + 256)
        for row in range(4):
            span = slice(row * 256, row * 256 + 256)
            low_keys[span, lanes] = gkeys[span, lanes].astype(LOW)
        query = dot_tn(hid[own_rows(0), :], gq[:128, lanes]) + dot_tn(
            hid[own_rows(1), :], gq[128:, lanes]
        )
        wgs[2 + group][:, :, :256] = query.reshape(4, 128, 256)
        wgs[2 + group][:, :, 256:] = dot_tn(hid[...], low_keys[:, lanes]).reshape(4, 128, 256)
        start_pair(2 + group)

    for group in range(2):
        for index in range(4):
            attend(index, group)
    wg_0[...] = dot_tn(mixed[...], gb[...]).reshape(4, 128, 512)
    start_pair(0)
    for row in range(4):
        span = slice(row * 256, row * 256 + 256)
        low_values[span, :] = gvalues[span, :].astype(LOW)
    wg_1[...] = dot_tn(hid[...], low_values[...]).reshape(4, 128, 512)
    start_pair(1)
    retreat(0, 0)
    retreat(1, 0)
    pair_to_plane(0)
    retreat(2, 0)
    pair_to_plane(1)
    retreat(3, 0)
    query_key_chunk(0)
    for row in range(4):
        span = slice(row * 256, row * 256 + 256)
        ghidden[span, :] = dot_nt(low_values[span, :], wq[:, 1024:])
    retreat(0, 1)
    retreat(1, 1)
    retreat(2, 1)
    pair_to_plane(2)
    retreat(3, 1)
    query_key_chunk(1)
    plane_to_z(0)
    for row in (0, 3, 1, 2):
        span = slice(row * 256, row * 256 + 256)
        total = ghidden[span, :] + dot_nt(low_keys[span, :], wq[:, 512:1024])
        if row in (1, 2):
            ghidden[span, :] = total
        for col in range(4):
            if row in (0, 3) or col in (0, 3):
                ghalo[row, col] = total[col * 64 : col * 64 + 64].astype(LOW)
        if row == 3:
            for copy in corners:
                copy.start()
            pair_to_plane(3)
            plane_to_z(1)
    for copy in edges:
        copy.start()
    for copy in corners:
        copy.wait()
    for row in range(2):
        to_west[row] = (
            ghalo[1 + row, 0].astype(FULL) + sources[row][0].astype(FULL)
        ).astype(LOW)
        to_east[row] = (
            ghalo[1 + row, 3].astype(FULL) + sources[row][3].astype(FULL)
        ).astype(LOW)
    for copy in sideways:
        copy.start()
    z_to_all(0)
    plane_to_z(2)
    z_to_all(1)
    branch = dot_nn(mixed[...], wo[...])
    for row in range(2):
        pieces = []
        for col in range(2):
            index = row * 2 + col
            flags = jnp.concatenate([oceans[index]] * 4, axis=1)
            tokens = ext[1 + row, 1 + col].astype(FULL).reshape(64, 512)
            result = tokens + flags * branch[index * 64 : index * 64 + 64]
            pieces.append(result.reshape(8, 8, 512))
        layer_buf[0, row * 8 : row * 8 + 8] = jnp.concatenate(pieces, axis=1).astype(LOW)
    layer_copy = pltpu.make_async_copy(layer_buf, layer_ref, out_sem.at[0])
    layer_copy.start()
    grad_query = dot_nt(gq[...], wq[:, :512])
    plane_to_z(3)
    z_to_all(2)
    z_to_all(3)
    for copy in edges + sideways:
        copy.wait()
    for row in range(2):
        pieces = []
        cot = cots[row * 8 : row * 8 + 8].astype(FULL)
        for col in range(2):
            index = row * 2 + col
            at = ((1 + row) * 4 + 1 + col) * 64
            side = (from_west, from_east)[col]
            grad_hidden = (
                grad_query[index * 64 : index * 64 + 64]
                + ghidden[at : at + 64, :]
                + sources[row][1 + col].astype(FULL)
                + side[row].astype(FULL)
            )
            normed, scaling = norm_rows(ext[1 + row, 1 + col].astype(FULL).reshape(64, 512))
            scaled = grad_hidden * gain
            correction = (
                scaled
                - jnp.mean(scaled, axis=-1, keepdims=True)
                - normed * jnp.mean(scaled * normed, axis=-1, keepdims=True)
            )
            result = cot[:, col * 8 : col * 8 + 8, :].reshape(64, 512) + scaling * correction
            pieces.append(result.reshape(8, 8, 512))
        grad_buf[0, row * 8 : row * 8 + 8] = jnp.concatenate(pieces, axis=1).astype(LOW)
    grad_copy = pltpu.make_async_copy(grad_buf, grad_ref, out_sem.at[1])
    grad_copy.start()
    sum_copies = [
        pltpu.make_async_copy(totals[chunk], outputs[chunk], out_sem.at[2 + chunk])
        for chunk in range(4)
    ]
    for chunk in range(4):
        lax.fori_loop(1, 8, finish(all_copy(chunk)), 0)
        sum_copies[chunk].start()
    for copy in [layer_copy, grad_copy] + sum_copies:
        copy.wait()


def layer(tokens_in, cotangent, qkv_weight, out_weight, gain, ocean_mask):
    dma = pltpu.SemaphoreType.DMA
    hbm = pl.BlockSpec(memory_space=pltpu.HBM)
    scratch = [
        pltpu.VMEM((4, 4, 8, 8, 512), LOW),
        pltpu.VMEM((3, 3, 16, 16), jnp.int32),
        pltpu.VMEM((16, 16, 512), LOW),
        pltpu.VMEM((512, 1536), LOW),
        pltpu.VMEM((512, 512), LOW),
        pltpu.VMEM((1, 512), FULL),
        pltpu.VMEM((1, 16, 16, 512), LOW),
        pltpu.VMEM((1, 16, 16, 512), LOW),
    ]
    scratch += [pltpu.VMEM((1024, 512), LOW)] * 3
    scratch += [pltpu.VMEM((1024, 512), FULL)] * 2
    scratch += [pltpu.VMEM((1024, 512), LOW)] * 2
    scratch += [pltpu.VMEM((1024, 512), FULL), pltpu.VMEM((4, 4, 64, 512), LOW)]
    scratch += [pltpu.VMEM((256, 512), LOW)] * 5
    scratch += [pltpu.VMEM((8, 3, 192, 256), FULL)]
    scratch += [pltpu.VMEM((8, 768, 256), LOW), pltpu.VMEM((2, 768, 256), LOW)]
    scratch += [pltpu.VMEM((1024, 128), FULL)]
    scratch += [pltpu.VMEM((4, 128, width), FULL) for width in WIDTHS]
    scratch += [pltpu.VMEM((2, 128, width), FULL) for width in WIDTHS]
    scratch += [pltpu.VMEM((16, 16, width), LOW) for width in WIDTHS]
    scratch += [pltpu.VMEM((15, 16, width), LOW) for width in WIDTHS]
    scratch += [pltpu.VMEM((16, width), LOW) for width in WIDTHS]
    scratch += [pltpu.VMEM((7, 16, width), LOW) for width in WIDTHS]
    scratch += [pltpu.VMEM((8, 16, width), LOW) for width in WIDTHS]
    scratch += [pltpu.VMEM((4, 64, 512), LOW)] * 2
    scratch += [pltpu.VMEM((2, 64, 512), LOW)] * 4
    scratch += [pltpu.SemaphoreType.REGULAR((4,))]
    scratch += [dma((9,)), dma((6,))] + [dma((2, 2))] * 6 + [dma((4,))] * 2
    scratch += [dma((4, 2))] * 2 + [dma((4, 15))] * 2 + [dma((4, 7))] * 4
    scratch += [dma((2, 4))] * 2 + [dma((2,))] * 2
    return pl.pallas_call(
        layer_kernel,
        out_shape=(
            jax.ShapeDtypeStruct((1, 16, 16, 512), LOW),
            jax.ShapeDtypeStruct((1, 16, 16, 512), LOW),
        )
        + tuple(jax.ShapeDtypeStruct((8, 16, width), LOW) for width in WIDTHS),
        in_specs=[hbm] * 6,
        out_specs=(hbm,) * 6,
        scratch_shapes=scratch,
        compiler_params=pltpu.CompilerParams(
            collective_id=0, has_side_effects=True, vmem_limit_bytes=WHOLE_VMEM
        ),
    )(tokens_in, cotangent, qkv_weight, out_weight, gain, ocean_mask)


def finish_kernel(
    layer_ref, grad_ref, sum_0, sum_1, sum_2, sum_3, wqkv_ref, gain_ref,
    layer_out, grad_out, qkv_out, out_out, gain_out,
    layer_buf, grad_buf, buf_0, buf_1, buf_2, buf_3, rows, gains, qkv, outs, line_buf, in_sem,
    out_sem,
):
    lev = lax.axis_index("lev")
    first = pl.multiple_of(lev * 128, 128)
    pairs = (
        (sum_2, buf_2), (sum_3, buf_3), (sum_1, buf_1), (sum_0, buf_0), (wqkv_ref.at[pl.ds(first, 128)], rows),
        (gain_ref, gains), (layer_ref, layer_buf), (grad_ref, grad_buf),
    )
    fetches = [
        pltpu.make_async_copy(src, dst, in_sem.at[slot]) for slot, (src, dst) in enumerate(pairs)
    ]
    for copy in fetches:
        copy.start()
    stores = [
        pltpu.make_async_copy(src, dst, out_sem.at[slot])
        for slot, (src, dst) in enumerate(
            (
                (qkv, qkv_out), (outs, out_out), (layer_buf, layer_out), (grad_buf, grad_out),
                (line_buf, gain_out),
            )
        )
    ]
    for group, source in enumerate((buf_2, buf_3)):
        fetches[group].wait()
        for part in range(2):
            at = part * 512 + group * 256
            qkv[:, at : at + 256] = (
                source[:, :, part * 256 : part * 256 + 256].reshape(128, 256).astype(FULL)
            )
    fetches[2].wait()
    qkv[:, 1024:] = buf_1[...].reshape(128, 512).astype(FULL)
    stores[0].start()
    fetches[3].wait()
    outs[...] = buf_0[...].reshape(128, 512).astype(FULL)
    stores[1].start()
    fetches[6].wait()
    stores[2].start()
    fetches[7].wait()
    stores[3].start()
    fetches[4].wait()
    fetches[5].wait()
    total = jnp.sum(rows[...].astype(FULL) * qkv[...], axis=1, keepdims=True)
    line = jnp.transpose(jnp.broadcast_to(total, (128, 128)))[:1]
    line_buf[...] = line / gains[:, pl.ds(first, 128)]
    stores[4].start()
    for copy in stores:
        copy.wait()


def finish_outputs(parts, qkv_weight, gain):
    hbm = pl.BlockSpec(memory_space=pltpu.HBM)
    dma = pltpu.SemaphoreType.DMA
    return pl.pallas_call(
        finish_kernel,
        out_shape=(
            jax.ShapeDtypeStruct((1, 16, 16, 512), LOW),
            jax.ShapeDtypeStruct((1, 16, 16, 512), LOW),
            jax.ShapeDtypeStruct((128, 1536), FULL),
            jax.ShapeDtypeStruct((128, 512), FULL),
            jax.ShapeDtypeStruct((1, 128), FULL),
        ),
        in_specs=[hbm] * 8,
        out_specs=(hbm,) * 5,
        scratch_shapes=[pltpu.VMEM((1, 16, 16, 512), LOW)] * 2
        + [pltpu.VMEM((8, 16, width), LOW) for width in WIDTHS]
        + [
            pltpu.VMEM((128, 1536), LOW), pltpu.VMEM((1, 512), FULL),
            pltpu.VMEM((128, 1536), FULL), pltpu.VMEM((128, 512), FULL),
            pltpu.VMEM((1, 128), FULL), dma((8,)), dma((5,)),
        ],
        compiler_params=pltpu.CompilerParams(vmem_limit_bytes=WHOLE_VMEM),
    )(*parts, qkv_weight, gain)


def on_device(tokens_in, cotangent, qkv_weight, out_weight, norm_gain, ocean_mask):
    gain = norm_gain.reshape(1, 512)
    parts = layer(tokens_in, cotangent, qkv_weight, out_weight, gain, ocean_mask)
    layer_out, input_grad, qkv_grad, out_grad, gain_grad = finish_outputs(parts, qkv_weight, gain)
    return (layer_out, input_grad, qkv_grad, out_grad, gain_grad.reshape(128))


def solution(mesh):
    placed = (
        P("lev", "lat", "lon", None),
        P("lev", "lat", "lon", None),
        P(),
        P(),
        P(),
        P("lev", "lat", "lon"),
    )
    return jax.shard_map(
        on_device,
        mesh=mesh,
        in_specs=placed,
        out_specs=(
            P("lev", "lat", "lon", None),
            P("lev", "lat", "lon", None),
            P("lev", None),
            P("lev", None),
            P("lev"),
        ),
        check_vma=False,
    )
```

```python
import jax
import jax.numpy as jnp
from jax import lax
from jax.experimental import pallas as pl
from jax.experimental.pallas import tpu as pltpu
from jax.sharding import PartitionSpec as P

MESH = pl.DeviceIdType.MESH
LOW = jnp.bfloat16
FULL = jnp.float32
WIDTHS = (512, 512, 512, 512)
WHOLE_VMEM = 67043328


def dot_nn(left, right):
    return lax.dot_general(
        left, right, (((1,), (0,)), ((), ())), preferred_element_type=jnp.float32
    )


def dot_nt(left, right):
    return lax.dot_general(
        left, right, (((1,), (1,)), ((), ())), preferred_element_type=jnp.float32
    )


def dot_tn(left, right):
    return lax.dot_general(
        left, right, (((0,), (0,)), ((), ())), preferred_element_type=jnp.float32
    )


def norm_rows(values_in):
    center = values_in - jnp.mean(values_in, axis=-1, keepdims=True)
    spread = jnp.mean(center * center, axis=-1, keepdims=True)
    scaling = lax.rsqrt(spread + 1e-05)
    return (center * scaling, scaling)


def layer_kernel(
    tokens_ref, cot_ref, wqkv_ref, wout_ref, gain_ref, mask_ref,
    layer_ref, grad_ref, sum_0, sum_1, sum_2, sum_3,
    ext, near, cots, wq, wo, gains, layer_buf, grad_buf,
    stats, hid, keys, values, gkeys, gvalues, low_keys, low_values, ghidden, ghalo,
    qs, gb, dout, mixed, gq, probs_all, pscr, dscr, bias,
    wg_0, wg_1, wg_2, wg_3, r1_0, r1_1, r1_2, r1_3, a1_0, a1_1, a1_2, a1_3, r2_0, r2_1, r2_2, r2_3,
    a2_0, a2_1, a2_2, a2_3, r3_0, r3_1, r3_2, r3_3, g5_0, g5_1, g5_2, g5_3,
    from_north, from_south, from_west, from_east, to_west, to_east,
    ready, local_sem, out_sem, s_lon, v_lon, s_lat, v_lat, s_rel, v_rel, s_m, v_m,
    s_pair, v_pair, s_plane, v_plane, s_z, v_z, s_all, v_all, s_gz, v_gz, s_gx, v_gx,
):
    lon = lax.axis_index("lon")
    lat = lax.axis_index("lat")
    lev = lax.axis_index("lev")
    hi = lev // 2
    core = lev % 2
    here = hi * 8 + lon
    west = ((lon + 7) % 8, lat, lev)
    east = ((lon + 1) % 8, lat, lev)
    north = (lon, (lat + 7) % 8, lev)
    south = (lon, (lat + 1) % 8, lev)
    partner = (lon, lat, hi * 2 + 1 - core)

    def plane_peer(step):
        there = (here + step) & 15
        return there >> 3, there & 7

    def window(row, col):
        return tokens_ref.at[0, row * 8 : row * 8 + 8, col * 8 : col * 8 + 8, :]

    def local(src, dst, slot):
        copy = pltpu.make_async_copy(src, dst, local_sem.at[slot])
        copy.start()
        return copy

    def remote(src, dst, send, recv, peer):
        return pltpu.make_async_remote_copy(
            src_ref=src, dst_ref=dst, send_sem=send, recv_sem=recv, device_id=peer,
            device_id_type=MESH,
        )

    mask_copy = local(mask_ref.at[0], near.at[1, 1], 0)
    own = [
        local(window(row, col), ext.at[1 + row, 1 + col], 1 + row * 2 + col)
        for row in range(2)
        for col in range(2)
    ]
    wq_copy = local(wqkv_ref, wq, 5)
    cot_copy = local(cot_ref.at[0], cots, 6)
    wo_copy = local(wout_ref, wo, 7)
    gain_copy = local(gain_ref, gains, 8)

    barrier = pltpu.get_barrier_semaphore()

    def greet(peer):
        pl.semaphore_signal(barrier, inc=1, device_id=peer, device_id_type=MESH)

    close = (west, east, north, south, partner, (lon, lat, (1 - hi) * 2 + core))
    for peer in close:
        greet(peer)

    def spread_word(turn):
        if turn:
            pl.semaphore_wait(ready.at[turn - 1], 6)
        if turn < 4:
            for peer in close:
                pl.semaphore_signal(
                    ready.at[turn], inc=1, device_id=peer, device_id_type=MESH
                )

    mask_copy.wait()
    pl.semaphore_wait(barrier, 6)

    mask_lon = [
        remote(near.at[1, 1], near.at[1, 2], s_m.at[0], v_m.at[0], west),
        remote(near.at[1, 1], near.at[1, 0], s_m.at[1], v_m.at[1], east),
    ]
    to_lon = []
    to_lat = []
    for row in range(2):
        to_lon.append(
            remote(window(row, 0), ext.at[1 + row, 3], s_lon.at[row, 0], v_lon.at[row, 0], west)
        )
        to_lon.append(
            remote(window(row, 1), ext.at[1 + row, 0], s_lon.at[row, 1], v_lon.at[row, 1], east)
        )
    for col in range(2):
        to_lat.append(
            remote(window(0, col), ext.at[3, 1 + col], s_lat.at[0, col], v_lat.at[0, col], north)
        )
        to_lat.append(
            remote(window(1, col), ext.at[0, 1 + col], s_lat.at[1, col], v_lat.at[1, col], south)
        )
    for copy in mask_lon + to_lon + to_lat:
        copy.start()
    spread_word(0)

    gain_copy.wait()
    gain = gains[...]

    def normalise(row, col):
        normed, _ = norm_rows(ext[row, col].astype(FULL).reshape(64, 512))
        at = (row * 4 + col) * 64
        hid[at : at + 64, :] = (normed * gain).astype(LOW)

    def project(spots):
        for row, col in spots:
            normalise(row, col)
        rows = jnp.concatenate(
            [hid[(row * 4 + col) * 64 : (row * 4 + col) * 64 + 64, :] for row, col in spots], axis=0
        )
        for part, target in enumerate((keys, values)):
            first = 512 + part * 512
            result = dot_nn(rows, wq[:, first : first + 512]).astype(LOW)
            for index, (row, col) in enumerate(spots):
                at = (row * 4 + col) * 64
                target[at : at + 64, :] = result[index * 64 : index * 64 + 64]
        return rows

    block_row = lax.broadcasted_iota(jnp.int32, (256, 256), 0) // 64
    block_col = lax.broadcasted_iota(jnp.int32, (256, 256), 1) // 64
    diag = jnp.where(block_row == block_col, 1.0, 0.0).astype(FULL)
    diag_low = diag.astype(LOW)

    def fold(square):
        kept = square * diag
        return (kept[:64] + kept[64:128]) + (kept[128:192] + kept[192:])

    def shape_of(index, group):
        row, col = index // 2, index % 2
        at = slice(index * 64, index * 64 + 64)
        lanes = slice(group * 256, group * 256 + 256)
        starts = [(row + part) * 256 + col * 64 for part in range(3)]
        spans = [slice(start, start + 192) for start in starts]
        inner = [slice(part * 256 + col * 64, part * 256 + col * 64 + 192) for part in range(3)]
        slab = slice(row * 256, row * 256 + 768)
        spare = 192 if col == 0 else 0
        return at, lanes, spans, inner, slab, spare

    def spread_heads(rows):
        return jnp.concatenate([rows] * 4, axis=0) * diag_low

    def middle_parts(index):
        return (1, 2) if index < 2 else (0, 1)

    def score(index, group, part, qbd):
        at, lanes, spans, inner, slab, spare = shape_of(index, group)
        span = spans[part]
        return dot_nt(keys[span, lanes], qbd) + jnp.concatenate([bias[span, :]] * 2, axis=1)

    def attend_early(index, group):
        at, lanes, spans, inner, slab, spare = shape_of(index, group)
        slot = index * 2 + group
        qbd = spread_heads(qs[at, lanes])
        first, second = middle_parts(index)
        score_a = score(index, group, first, qbd)
        score_b = score(index, group, second, qbd)
        top = jnp.maximum(
            jnp.max(score_a, axis=0, keepdims=True), jnp.max(score_b, axis=0, keepdims=True)
        )
        weights_a = jnp.exp(score_a - top)
        weights_b = jnp.exp(score_b - top)
        probs_all[slot, first] = weights_a
        probs_all[slot, second] = weights_b
        stats[slot, 0:1, :] = top
        stats[slot, 1:2, :] = jnp.sum(weights_a, axis=0, keepdims=True) + jnp.sum(
            weights_b, axis=0, keepdims=True
        )

    token_of = lax.broadcasted_iota(jnp.int32, (128, 16), 0)
    lane_of = lax.broadcasted_iota(jnp.int32, (128, 16), 1)
    repeat_rows = jnp.where(token_of // 8 == lane_of, 1.0, 0.0).astype(LOW)
    picks = [jnp.where(lane_of == token_of % 8 + 8 * side, 1.0, 0.0) for side in range(2)]
    has_north = jnp.where(lat > 0, 1.0, 0.0).astype(FULL)
    has_south = jnp.where(lat < 7, 1.0, 0.0).astype(FULL)

    def mask_columns(tile_row, tile_col):
        tall = dot_nn(repeat_rows, near[tile_row, tile_col].astype(FULL).astype(LOW))
        return [
            jnp.broadcast_to(jnp.sum(tall * pick, axis=1, keepdims=True), (128, 128))
            for pick in picks
        ]

    for copy in own:
        copy.wait()
    oceans = [None] * 4
    centre = mask_columns(1, 1)
    for row in range(2):
        for col in range(2):
            oceans[row * 2 + col] = centre[col][row * 64 : row * 64 + 64]
    wq_copy.wait()
    rows = project(((1, 1), (1, 2), (2, 1), (2, 2)))
    qs[...] = (dot_nn(rows, wq[:, :512]) * 0.125).astype(LOW)
    spread_word(1)
    for copy in mask_lon:
        copy.wait()
    mask_lat = [
        remote(near.at[1], near.at[2], s_m.at[2], v_m.at[2], north),
        remote(near.at[1], near.at[0], s_m.at[3], v_m.at[3], south),
    ]
    for copy in mask_lat:
        copy.start()
    cot_copy.wait()
    for row in range(2):
        band = cots[row * 8 : row * 8 + 8].astype(FULL)
        for col in range(2):
            at = (row * 2 + col) * 64
            piece = band[:, col * 8 : col * 8 + 8, :].reshape(64, 512)
            flags = jnp.concatenate([oceans[row * 2 + col]] * 4, axis=1)
            gb[at : at + 64, :] = (piece * flags).astype(LOW)
    wo_copy.wait()
    dout[...] = dot_nt(gb[...], wo[...]).astype(LOW)
    for row in range(4):
        gkeys[row * 256 : row * 256 + 256, :] = jnp.zeros((256, 512), FULL)
        gvalues[row * 256 : row * 256 + 256, :] = jnp.zeros((256, 512), FULL)
    spread_word(2)
    relayed = []
    for row, line, peer in ((0, 3, north), (1, 0, south)):
        for side, col in ((0, 3), (1, 0)):
            to_lon[row * 2 + side].wait()
            relayed.append(
                remote(
                    ext.at[1 + row, col], ext.at[line, col],
                    s_rel.at[row, side], v_rel.at[row, side], peer,
                )
            )
            relayed[-1].start()
    project(((1, 0), (2, 0), (1, 3), (2, 3)))
    place = ((0, 1), (1, 0), (1, 1), (2, 0))

    def write_bias(tile_rows):
        for tile_row in tile_rows:
            for tile_col in range(3):
                if (tile_row, tile_col) == (1, 1):
                    sides = centre
                else:
                    sides = mask_columns(tile_row, tile_col)
                for row in range(4):
                    for col in range(4):
                        if place[row][0] != tile_row or place[col][0] != tile_col:
                            continue
                        at = (row * 4 + col) * 64
                        flags = sides[place[col][1]][place[row][1] * 64 : place[row][1] * 64 + 64]
                        if row == 0:
                            flags = flags * has_north
                        if row == 3:
                            flags = flags * has_south
                        bias[at : at + 64, :] = (flags - 1.0) * 1000000000.0

    write_bias((1,))
    for index in range(4):
        for group in range(2):
            attend_early(index, group)
    for copy in mask_lat:
        copy.wait()
    write_bias((0, 2))
    spread_word(3)
    for copy in to_lat:
        copy.wait()
    project(((0, 1), (0, 2), (3, 1), (3, 2)))
    spread_word(4)
    for copy in relayed:
        copy.wait()
    project(((0, 0), (0, 3), (3, 0), (3, 3)))

    def attend(index, group):
        at, lanes, spans, inner, slab, spare = shape_of(index, group)
        slot = index * 2 + group
        alive = jnp.max(oceans[index], axis=(0, 1), keepdims=True)
        for part in range(3):
            pscr[slot, part * 256 + spare : part * 256 + spare + 64, :] = jnp.zeros((64, 256), LOW)
        qbd = spread_heads(qs[at, lanes])
        dbd = spread_heads(dout[at, lanes])
        first, second = middle_parts(index)
        last = 3 - first - second
        scores = score(index, group, last, qbd)
        early_top = stats[slot, 0:1, :]
        top = jnp.maximum(jnp.max(scores, axis=0, keepdims=True), early_top)
        weights = jnp.exp(scores - top)
        shrink = jnp.exp(early_top - top)
        total = jnp.sum(weights, axis=0, keepdims=True) + shrink * stats[slot, 1:2, :]
        inverse = 1.0 / total
        for part in range(3):
            if part == last:
                probs = weights * inverse
            else:
                probs = probs_all[slot, part] * (shrink * inverse)
            probs_all[slot, part] = probs
            pscr[slot, inner[part], :] = probs.astype(LOW)
        out = fold(dot_tn(pscr[slot], values[slab, lanes]))
        mixed[at, lanes] = (out * alive).astype(LOW)
        for part in range(3):
            gvalues[spans[part], lanes] += dot_nn(pscr[slot, inner[part], :], dbd)

    def retreat(index, group):
        at, lanes, spans, inner, slab, spare = shape_of(index, group)
        slot = index * 2 + group
        side = index % 2
        for part in range(3):
            dscr[side, part * 256 + spare : part * 256 + spare + 64, :] = jnp.zeros((64, 256), LOW)
        qbd = spread_heads(qs[at, lanes])
        dbd = spread_heads(dout[at, lanes])
        gprobs = [dot_nt(values[span, lanes], dbd) for span in spans]
        deltas = [
            jnp.sum(probs_all[slot, part] * gprobs[part], axis=0, keepdims=True)
            for part in range(3)
        ]
        delta = deltas[0] + deltas[1] + deltas[2]
        for part in range(3):
            dscr[side, inner[part], :] = (
                probs_all[slot, part] * (gprobs[part] - delta)
            ).astype(LOW)
        gq[at, lanes] = (fold(dot_tn(dscr[side], keys[slab, lanes])) * 0.125).astype(LOW)
        for part in range(3):
            gkeys[spans[part], lanes] += dot_nn(dscr[side, inner[part], :], qbd)

    wgs = (wg_0, wg_1, wg_2, wg_3)
    r1s = (r1_0, r1_1, r1_2, r1_3)
    a1s = (a1_0, a1_1, a1_2, a1_3)
    r2s = (r2_0, r2_1, r2_2, r2_3)
    a2s = (a2_0, a2_1, a2_2, a2_3)
    r3s = (r3_0, r3_1, r3_2, r3_3)
    totals = (g5_0, g5_1, g5_2, g5_3)
    outputs = (sum_0, sum_1, sum_2, sum_3)

    def pair_copies(chunk):
        return [
            remote(
                wgs[chunk].at[part * 2 + 1 - core], r1s[chunk].at[part],
                s_pair.at[chunk, part], v_pair.at[chunk, part], partner,
            )
            for part in range(2)
        ]

    def plane_copy(chunk):
        def one(step):
            peer_hi, peer_lon = plane_peer(step)
            return remote(
                a1s[chunk].at[peer_hi * 8 + peer_lon], r2s[chunk].at[step - 1],
                s_plane.at[chunk, step - 1], v_plane.at[chunk, step - 1],
                (peer_lon, lat, peer_hi * 2 + core),
            )

        return one

    def z_copy(chunk):
        def one(step):
            return remote(
                a2s[chunk], r3s[chunk].at[step - 1],
                s_z.at[chunk, step - 1], v_z.at[chunk, step - 1], (lon, (lat + step) % 8, lev),
            )

        return one

    def all_copy(chunk):
        def one(step):
            return remote(
                totals[chunk].at[lon], totals[chunk].at[lon],
                s_all.at[chunk, step - 1], v_all.at[chunk, step - 1],
                ((lon + step) % 8, lat, lev),
            )

        return one

    def start_pair(chunk):
        for copy in pair_copies(chunk):
            copy.start()

    def pair_to_plane(chunk):
        for part, copy in enumerate(pair_copies(chunk)):
            copy.wait()

            def add(piece, carry):
                span = pl.ds(pl.multiple_of(piece * 16, 16), 16)
                total = wgs[chunk][part * 2 + core, span, :] + r1s[chunk][part, span, :]
                a1s[chunk][part * 8 + piece] = total.astype(LOW)
                return carry

            lax.fori_loop(0, 8, add, 0)
        for step in range(1, 16):
            plane_copy(chunk)(step).start()

    def plane_to_z(chunk):
        for step in range(1, 16):
            plane_copy(chunk)(step).wait()
        for first in range(0, WIDTHS[chunk], 256):
            cols = slice(first, first + 256)
            total = a1s[chunk][here, :, cols].astype(FULL)
            for step in range(15):
                total = total + r2s[chunk][step, :, cols].astype(FULL)
            a2s[chunk][:, cols] = total.astype(LOW)
        for step in range(1, 8):
            z_copy(chunk)(step).start()

    def z_to_all(chunk):
        for step in range(1, 8):
            z_copy(chunk)(step).wait()
        for first in range(0, WIDTHS[chunk], 256):
            cols = slice(first, first + 256)
            total = a2s[chunk][:, cols].astype(FULL)
            for step in range(7):
                total = total + r3s[chunk][step, :, cols].astype(FULL)
            totals[chunk][lon, :, cols] = total.astype(LOW)
        for step in range(1, 8):
            all_copy(chunk)(step).start()

    corners = []
    edges = []
    for line, target, peer, side in ((0, from_south, north, 0), (3, from_north, south, 1)):
        for col in (0, 3):
            corners.append(
                remote(
                    ghalo.at[line, col], target.at[col],
                    s_gz.at[side, col], v_gz.at[side, col], peer,
                )
            )
        edges.append(
            remote(
                ghalo.at[line, pl.ds(1, 2)], target.at[pl.ds(1, 2)],
                s_gz.at[side, 1], v_gz.at[side, 1], peer,
            )
        )
    sideways = [
        remote(to_west, from_east, s_gx.at[0], v_gx.at[0], west),
        remote(to_east, from_west, s_gx.at[1], v_gx.at[1], east),
    ]
    sources = (from_north, from_south)

    def own_rows(row):
        return slice(row * 256 + 320, row * 256 + 448)

    def query_key_chunk(group):
        lanes = slice(group * 256, group * 256 + 256)
        for row in range(4):
            span = slice(row * 256, row * 256 + 256)
            low_keys[span, lanes] = gkeys[span, lanes].astype(LOW)
        query = dot_tn(hid[own_rows(0), :], gq[:128, lanes]) + dot_tn(
            hid[own_rows(1), :], gq[128:, lanes]
        )
        wgs[2 + group][:, :, :256] = query.reshape(4, 128, 256)
        wgs[2 + group][:, :, 256:] = dot_tn(hid[...], low_keys[:, lanes]).reshape(4, 128, 256)
        start_pair(2 + group)

    for group in range(2):
        for index in range(4):
            attend(index, group)
    wg_0[...] = dot_tn(mixed[...], gb[...]).reshape(4, 128, 512)
    start_pair(0)
    for row in range(4):
        span = slice(row * 256, row * 256 + 256)
        low_values[span, :] = gvalues[span, :].astype(LOW)
    wg_1[...] = dot_tn(hid[...], low_values[...]).reshape(4, 128, 512)
    start_pair(1)
    retreat(0, 0)
    retreat(1, 0)
    pair_to_plane(0)
    retreat(2, 0)
    pair_to_plane(1)
    retreat(3, 0)
    query_key_chunk(0)
    for row in range(4):
        span = slice(row * 256, row * 256 + 256)
        ghidden[span, :] = dot_nt(low_values[span, :], wq[:, 1024:])
    retreat(0, 1)
    retreat(1, 1)
    retreat(2, 1)
    pair_to_plane(2)
    retreat(3, 1)
    query_key_chunk(1)
    plane_to_z(0)
    for row in (0, 3, 1, 2):
        span = slice(row * 256, row * 256 + 256)
        total = ghidden[span, :] + dot_nt(low_keys[span, :], wq[:, 512:1024])
        if row in (1, 2):
            ghidden[span, :] = total
        for col in range(4):
            if row in (0, 3) or col in (0, 3):
                ghalo[row, col] = total[col * 64 : col * 64 + 64].astype(LOW)
        if row == 3:
            for copy in corners:
                copy.start()
            pair_to_plane(3)
            plane_to_z(1)
    for copy in edges:
        copy.start()
    for copy in corners:
        copy.wait()
    for row in range(2):
        to_west[row] = (
            ghalo[1 + row, 0].astype(FULL) + sources[row][0].astype(FULL)
        ).astype(LOW)
        to_east[row] = (
            ghalo[1 + row, 3].astype(FULL) + sources[row][3].astype(FULL)
        ).astype(LOW)
    for copy in sideways:
        copy.start()
    z_to_all(0)
    plane_to_z(2)
    z_to_all(1)
    branch = dot_nn(mixed[...], wo[...])
    for row in range(2):
        pieces = []
        for col in range(2):
            index = row * 2 + col
            flags = jnp.concatenate([oceans[index]] * 4, axis=1)
            tokens = ext[1 + row, 1 + col].astype(FULL).reshape(64, 512)
            result = tokens + flags * branch[index * 64 : index * 64 + 64]
            pieces.append(result.reshape(8, 8, 512))
        layer_buf[0, row * 8 : row * 8 + 8] = jnp.concatenate(pieces, axis=1).astype(LOW)
    layer_copy = pltpu.make_async_copy(layer_buf, layer_ref, out_sem.at[0])
    layer_copy.start()
    grad_query = dot_nt(gq[...], wq[:, :512])
    plane_to_z(3)
    z_to_all(2)
    z_to_all(3)
    for copy in edges + sideways:
        copy.wait()
    for row in range(2):
        pieces = []
        cot = cots[row * 8 : row * 8 + 8].astype(FULL)
        for col in range(2):
            index = row * 2 + col
            at = ((1 + row) * 4 + 1 + col) * 64
            side = (from_west, from_east)[col]
            grad_hidden = (
                grad_query[index * 64 : index * 64 + 64]
                + ghidden[at : at + 64, :]
                + sources[row][1 + col].astype(FULL)
                + side[row].astype(FULL)
            )
            normed, scaling = norm_rows(ext[1 + row, 1 + col].astype(FULL).reshape(64, 512))
            scaled = grad_hidden * gain
            correction = (
                scaled
                - jnp.mean(scaled, axis=-1, keepdims=True)
                - normed * jnp.mean(scaled * normed, axis=-1, keepdims=True)
            )
            result = cot[:, col * 8 : col * 8 + 8, :].reshape(64, 512) + scaling * correction
            pieces.append(result.reshape(8, 8, 512))
        grad_buf[0, row * 8 : row * 8 + 8] = jnp.concatenate(pieces, axis=1).astype(LOW)
    grad_copy = pltpu.make_async_copy(grad_buf, grad_ref, out_sem.at[1])
    grad_copy.start()
    sum_copies = [
        pltpu.make_async_copy(totals[chunk], outputs[chunk], out_sem.at[2 + chunk])
        for chunk in range(4)
    ]
    for chunk in range(4):
        for step in range(1, 8):
            all_copy(chunk)(step).wait()
        sum_copies[chunk].start()
    for copy in [layer_copy, grad_copy] + sum_copies:
        copy.wait()


def layer(tokens_in, cotangent, qkv_weight, out_weight, gain, ocean_mask):
    dma = pltpu.SemaphoreType.DMA
    hbm = pl.BlockSpec(memory_space=pltpu.HBM)
    scratch = [
        pltpu.VMEM((4, 4, 8, 8, 512), LOW),
        pltpu.VMEM((3, 3, 16, 16), jnp.int32),
        pltpu.VMEM((16, 16, 512), LOW),
        pltpu.VMEM((512, 1536), LOW),
        pltpu.VMEM((512, 512), LOW),
        pltpu.VMEM((1, 512), FULL),
        pltpu.VMEM((1, 16, 16, 512), LOW),
        pltpu.VMEM((1, 16, 16, 512), LOW),
        pltpu.VMEM((8, 8, 256), FULL),
    ]
    scratch += [pltpu.VMEM((1024, 512), LOW)] * 3
    scratch += [pltpu.VMEM((1024, 512), FULL)] * 2
    scratch += [pltpu.VMEM((1024, 512), LOW)] * 2
    scratch += [pltpu.VMEM((1024, 512), FULL), pltpu.VMEM((4, 4, 64, 512), LOW)]
    scratch += [pltpu.VMEM((256, 512), LOW)] * 5
    scratch += [pltpu.VMEM((8, 3, 192, 256), FULL)]
    scratch += [pltpu.VMEM((8, 768, 256), LOW), pltpu.VMEM((2, 768, 256), LOW)]
    scratch += [pltpu.VMEM((1024, 128), FULL)]
    scratch += [pltpu.VMEM((4, 128, width), FULL) for width in WIDTHS]
    scratch += [pltpu.VMEM((2, 128, width), FULL) for width in WIDTHS]
    scratch += [pltpu.VMEM((16, 16, width), LOW) for width in WIDTHS]
    scratch += [pltpu.VMEM((15, 16, width), LOW) for width in WIDTHS]
    scratch += [pltpu.VMEM((16, width), LOW) for width in WIDTHS]
    scratch += [pltpu.VMEM((7, 16, width), LOW) for width in WIDTHS]
    scratch += [pltpu.VMEM((8, 16, width), LOW) for width in WIDTHS]
    scratch += [pltpu.VMEM((4, 64, 512), LOW)] * 2
    scratch += [pltpu.VMEM((2, 64, 512), LOW)] * 4
    scratch += [pltpu.SemaphoreType.REGULAR((4,))]
    scratch += [dma((9,)), dma((6,))] + [dma((2, 2))] * 6 + [dma((4,))] * 2
    scratch += [dma((4, 2))] * 2 + [dma((4, 15))] * 2 + [dma((4, 7))] * 4
    scratch += [dma((2, 4))] * 2 + [dma((2,))] * 2
    return pl.pallas_call(
        layer_kernel,
        out_shape=(
            jax.ShapeDtypeStruct((1, 16, 16, 512), LOW),
            jax.ShapeDtypeStruct((1, 16, 16, 512), LOW),
        )
        + tuple(jax.ShapeDtypeStruct((8, 16, width), LOW) for width in WIDTHS),
        in_specs=[hbm] * 6,
        out_specs=(hbm,) * 6,
        scratch_shapes=scratch,
        compiler_params=pltpu.CompilerParams(
            collective_id=0, has_side_effects=True, vmem_limit_bytes=WHOLE_VMEM
        ),
    )(tokens_in, cotangent, qkv_weight, out_weight, gain, ocean_mask)


def finish_kernel(
    layer_ref, grad_ref, sum_0, sum_1, sum_2, sum_3, wqkv_ref, gain_ref,
    layer_out, grad_out, qkv_out, out_out, gain_out,
    layer_buf, grad_buf, buf_0, buf_1, buf_2, buf_3, rows, gains, qkv, outs, line_buf, in_sem,
    out_sem,
):
    lev = lax.axis_index("lev")
    first = pl.multiple_of(lev * 128, 128)
    pairs = (
        (sum_2, buf_2), (sum_3, buf_3), (sum_1, buf_1), (sum_0, buf_0), (wqkv_ref.at[pl.ds(first, 128)], rows),
        (gain_ref, gains), (layer_ref, layer_buf), (grad_ref, grad_buf),
    )
    fetches = [
        pltpu.make_async_copy(src, dst, in_sem.at[slot]) for slot, (src, dst) in enumerate(pairs)
    ]
    for copy in fetches:
        copy.start()
    stores = [
        pltpu.make_async_copy(src, dst, out_sem.at[slot])
        for slot, (src, dst) in enumerate(
            (
                (qkv, qkv_out), (outs, out_out), (layer_buf, layer_out), (grad_buf, grad_out),
                (line_buf, gain_out),
            )
        )
    ]
    for group, source in enumerate((buf_2, buf_3)):
        fetches[group].wait()
        for part in range(2):
            at = part * 512 + group * 256
            qkv[:, at : at + 256] = (
                source[:, :, part * 256 : part * 256 + 256].reshape(128, 256).astype(FULL)
            )
    fetches[2].wait()
    qkv[:, 1024:] = buf_1[...].reshape(128, 512).astype(FULL)
    stores[0].start()
    fetches[3].wait()
    outs[...] = buf_0[...].reshape(128, 512).astype(FULL)
    stores[1].start()
    fetches[6].wait()
    stores[2].start()
    fetches[7].wait()
    stores[3].start()
    fetches[4].wait()
    fetches[5].wait()
    total = jnp.sum(rows[...].astype(FULL) * qkv[...], axis=1, keepdims=True)
    line = jnp.transpose(jnp.broadcast_to(total, (128, 128)))[:1]
    line_buf[...] = line / gains[:, pl.ds(first, 128)]
    stores[4].start()
    for copy in stores:
        copy.wait()


def finish_outputs(parts, qkv_weight, gain):
    hbm = pl.BlockSpec(memory_space=pltpu.HBM)
    dma = pltpu.SemaphoreType.DMA
    return pl.pallas_call(
        finish_kernel,
        out_shape=(
            jax.ShapeDtypeStruct((1, 16, 16, 512), LOW),
            jax.ShapeDtypeStruct((1, 16, 16, 512), LOW),
            jax.ShapeDtypeStruct((128, 1536), FULL),
            jax.ShapeDtypeStruct((128, 512), FULL),
            jax.ShapeDtypeStruct((1, 128), FULL),
        ),
        in_specs=[hbm] * 8,
        out_specs=(hbm,) * 5,
        scratch_shapes=[pltpu.VMEM((1, 16, 16, 512), LOW)] * 2
        + [pltpu.VMEM((8, 16, width), LOW) for width in WIDTHS]
        + [
            pltpu.VMEM((128, 1536), LOW), pltpu.VMEM((1, 512), FULL),
            pltpu.VMEM((128, 1536), FULL), pltpu.VMEM((128, 512), FULL),
            pltpu.VMEM((1, 128), FULL), dma((8,)), dma((5,)),
        ],
        compiler_params=pltpu.CompilerParams(vmem_limit_bytes=WHOLE_VMEM),
    )(*parts, qkv_weight, gain)


def on_device(tokens_in, cotangent, qkv_weight, out_weight, norm_gain, ocean_mask):
    gain = norm_gain.reshape(1, 512)
    parts = layer(tokens_in, cotangent, qkv_weight, out_weight, gain, ocean_mask)
    layer_out, input_grad, qkv_grad, out_grad, gain_grad = finish_outputs(parts, qkv_weight, gain)
    return (layer_out, input_grad, qkv_grad, out_grad, gain_grad.reshape(128))


def solution(mesh):
    placed = (
        P("lev", "lat", "lon", None),
        P("lev", "lat", "lon", None),
        P(),
        P(),
        P(),
        P("lev", "lat", "lon"),
    )
    return jax.shard_map(
        on_device,
        mesh=mesh,
        in_specs=placed,
        out_specs=(
            P("lev", "lat", "lon", None),
            P("lev", "lat", "lon", None),
            P("lev", None),
            P("lev", None),
            P("lev"),
        ),
        check_vma=False,
    )
```

```python
import jax
import jax.numpy as jnp
from jax import lax
from jax.experimental import pallas as pl
from jax.experimental.pallas import tpu as pltpu
from jax.sharding import PartitionSpec as P

MESH = pl.DeviceIdType.MESH
LOW = jnp.bfloat16
FULL = jnp.float32
WIDTHS = (512, 512, 512, 512)
WHOLE_VMEM = 67043328


def dot_nn(left, right):
    return lax.dot_general(
        left, right, (((1,), (0,)), ((), ())), preferred_element_type=jnp.float32
    )


def dot_nt(left, right):
    return lax.dot_general(
        left, right, (((1,), (1,)), ((), ())), preferred_element_type=jnp.float32
    )


def dot_tn(left, right):
    return lax.dot_general(
        left, right, (((0,), (0,)), ((), ())), preferred_element_type=jnp.float32
    )


def norm_rows(values_in):
    center = values_in - jnp.mean(values_in, axis=-1, keepdims=True)
    spread = jnp.mean(center * center, axis=-1, keepdims=True)
    scaling = lax.rsqrt(spread + 1e-05)
    return (center * scaling, scaling)


def layer_kernel(
    tokens_ref, cot_ref, wqkv_ref, wout_ref, gain_ref, mask_ref,
    layer_ref, grad_ref, sum_0, sum_1, sum_2, sum_3,
    ext, near, cots, wq, wo, gains, layer_buf, grad_buf,
    stats, hid, keys, values, gkeys, gvalues, low_keys, low_values, ghidden, ghalo,
    qs, gb, dout, mixed, gq, probs_all, pscr, dscr, bias,
    wg_0, wg_1, wg_2, wg_3, r1_0, r1_1, r1_2, r1_3, a1_0, a1_1, a1_2, a1_3, r2_0, r2_1, r2_2, r2_3,
    a2_0, a2_1, a2_2, a2_3, r3_0, r3_1, r3_2, r3_3, g5_0, g5_1, g5_2, g5_3,
    from_north, from_south, from_west, from_east, to_west, to_east,
    ready, local_sem, out_sem, s_lon, v_lon, s_lat, v_lat, s_rel, v_rel, s_m, v_m,
    s_pair, v_pair, s_plane, v_plane, s_z, v_z, s_all, v_all, s_gz, v_gz, s_gx, v_gx,
):
    lon = lax.axis_index("lon")
    lat = lax.axis_index("lat")
    lev = lax.axis_index("lev")
    hi = lev // 2
    core = lev % 2
    here = hi * 8 + lon
    west = ((lon + 7) % 8, lat, lev)
    east = ((lon + 1) % 8, lat, lev)
    north = (lon, (lat + 7) % 8, lev)
    south = (lon, (lat + 1) % 8, lev)
    partner = (lon, lat, hi * 2 + 1 - core)

    def plane_peer(step):
        there = (here + step) & 15
        return there >> 3, there & 7

    def window(row, col):
        return tokens_ref.at[0, row * 8 : row * 8 + 8, col * 8 : col * 8 + 8, :]

    def local(src, dst, slot):
        copy = pltpu.make_async_copy(src, dst, local_sem.at[slot])
        copy.start()
        return copy

    def remote(src, dst, send, recv, peer):
        return pltpu.make_async_remote_copy(
            src_ref=src, dst_ref=dst, send_sem=send, recv_sem=recv, device_id=peer,
            device_id_type=MESH,
        )

    mask_copy = local(mask_ref.at[0], near.at[1, 1], 0)
    own = [
        local(window(row, col), ext.at[1 + row, 1 + col], 1 + row * 2 + col)
        for row in range(2)
        for col in range(2)
    ]
    wq_copy = local(wqkv_ref, wq, 5)
    cot_copy = local(cot_ref.at[0], cots, 6)
    wo_copy = local(wout_ref, wo, 7)
    gain_copy = local(gain_ref, gains, 8)

    barrier = pltpu.get_barrier_semaphore()

    def greet(peer):
        pl.semaphore_signal(barrier, inc=1, device_id=peer, device_id_type=MESH)

    close = (west, east, north, south, partner, (lon, lat, (1 - hi) * 2 + core))
    for peer in close:
        greet(peer)

    def spread_word(turn):
        if turn:
            pl.semaphore_wait(ready.at[turn - 1], 6)
        if turn < 4:
            for peer in close:
                pl.semaphore_signal(
                    ready.at[turn], inc=1, device_id=peer, device_id_type=MESH
                )

    mask_copy.wait()
    pl.semaphore_wait(barrier, 6)

    mask_lon = [
        remote(near.at[1, 1], near.at[1, 2], s_m.at[0], v_m.at[0], west),
        remote(near.at[1, 1], near.at[1, 0], s_m.at[1], v_m.at[1], east),
    ]
    to_lon = []
    to_lat = []
    for row in range(2):
        to_lon.append(
            remote(window(row, 0), ext.at[1 + row, 3], s_lon.at[row, 0], v_lon.at[row, 0], west)
        )
        to_lon.append(
            remote(window(row, 1), ext.at[1 + row, 0], s_lon.at[row, 1], v_lon.at[row, 1], east)
        )
    for col in range(2):
        to_lat.append(
            remote(window(0, col), ext.at[3, 1 + col], s_lat.at[0, col], v_lat.at[0, col], north)
        )
        to_lat.append(
            remote(window(1, col), ext.at[0, 1 + col], s_lat.at[1, col], v_lat.at[1, col], south)
        )
    for copy in mask_lon + to_lon + to_lat:
        copy.start()
    spread_word(0)

    gain_copy.wait()
    gain = gains[...]

    def normalise(row, col):
        normed, _ = norm_rows(ext[row, col].astype(FULL).reshape(64, 512))
        at = (row * 4 + col) * 64
        hid[at : at + 64, :] = (normed * gain).astype(LOW)

    def project(spots):
        for row, col in spots:
            normalise(row, col)
        rows = jnp.concatenate(
            [hid[(row * 4 + col) * 64 : (row * 4 + col) * 64 + 64, :] for row, col in spots], axis=0
        )
        for part, target in enumerate((keys, values)):
            first = 512 + part * 512
            result = dot_nn(rows, wq[:, first : first + 512]).astype(LOW)
            for index, (row, col) in enumerate(spots):
                at = (row * 4 + col) * 64
                target[at : at + 64, :] = result[index * 64 : index * 64 + 64]
        return rows

    block_row = lax.broadcasted_iota(jnp.int32, (256, 256), 0) // 64
    block_col = lax.broadcasted_iota(jnp.int32, (256, 256), 1) // 64
    diag = jnp.where(block_row == block_col, 1.0, 0.0).astype(FULL)
    diag_low = diag.astype(LOW)

    def fold(square):
        kept = square * diag
        return (kept[:64] + kept[64:128]) + (kept[128:192] + kept[192:])

    def shape_of(index, group):
        row, col = index // 2, index % 2
        at = slice(index * 64, index * 64 + 64)
        lanes = slice(group * 256, group * 256 + 256)
        starts = [(row + part) * 256 + col * 64 for part in range(3)]
        spans = [slice(start, start + 192) for start in starts]
        inner = [slice(part * 256 + col * 64, part * 256 + col * 64 + 192) for part in range(3)]
        slab = slice(row * 256, row * 256 + 768)
        spare = 192 if col == 0 else 0
        return at, lanes, spans, inner, slab, spare

    def spread_heads(rows):
        return jnp.concatenate([rows] * 4, axis=0) * diag_low

    def middle_parts(index):
        return (1, 2) if index < 2 else (0, 1)

    def score(index, group, part, qbd):
        at, lanes, spans, inner, slab, spare = shape_of(index, group)
        span = spans[part]
        return dot_nt(keys[span, lanes], qbd) + jnp.concatenate([bias[span, :]] * 2, axis=1)

    def attend_early(index, group):
        at, lanes, spans, inner, slab, spare = shape_of(index, group)
        slot = index * 2 + group
        qbd = spread_heads(qs[at, lanes])
        first, second = middle_parts(index)
        score_a = score(index, group, first, qbd)
        score_b = score(index, group, second, qbd)
        top = jnp.maximum(
            jnp.max(score_a, axis=0, keepdims=True), jnp.max(score_b, axis=0, keepdims=True)
        )
        weights_a = jnp.exp(score_a - top)
        weights_b = jnp.exp(score_b - top)
        probs_all[slot, first] = weights_a
        probs_all[slot, second] = weights_b
        stats[slot, 0:1, :] = top
        stats[slot, 1:2, :] = jnp.sum(weights_a, axis=0, keepdims=True) + jnp.sum(
            weights_b, axis=0, keepdims=True
        )

    token_of = lax.broadcasted_iota(jnp.int32, (128, 16), 0)
    lane_of = lax.broadcasted_iota(jnp.int32, (128, 16), 1)
    repeat_rows = jnp.where(token_of // 8 == lane_of, 1.0, 0.0).astype(LOW)
    picks = [jnp.where(lane_of == token_of % 8 + 8 * side, 1.0, 0.0) for side in range(2)]
    has_north = jnp.where(lat > 0, 1.0, 0.0).astype(FULL)
    has_south = jnp.where(lat < 7, 1.0, 0.0).astype(FULL)

    def mask_columns(tile_row, tile_col):
        tall = dot_nn(repeat_rows, near[tile_row, tile_col].astype(FULL).astype(LOW))
        return [
            jnp.broadcast_to(jnp.sum(tall * pick, axis=1, keepdims=True), (128, 128))
            for pick in picks
        ]

    for copy in own:
        copy.wait()
    oceans = [None] * 4
    centre = mask_columns(1, 1)
    for row in range(2):
        for col in range(2):
            oceans[row * 2 + col] = centre[col][row * 64 : row * 64 + 64]
    wq_copy.wait()
    rows = project(((1, 1), (1, 2), (2, 1), (2, 2)))
    qs[...] = (dot_nn(rows, wq[:, :512]) * 0.125).astype(LOW)
    spread_word(1)
    for copy in mask_lon:
        copy.wait_recv()
    mask_lat = [
        remote(near.at[1], near.at[2], s_m.at[2], v_m.at[2], north),
        remote(near.at[1], near.at[0], s_m.at[3], v_m.at[3], south),
    ]
    for copy in mask_lat:
        copy.start()
    cot_copy.wait()
    for row in range(2):
        band = cots[row * 8 : row * 8 + 8].astype(FULL)
        for col in range(2):
            at = (row * 2 + col) * 64
            piece = band[:, col * 8 : col * 8 + 8, :].reshape(64, 512)
            flags = jnp.concatenate([oceans[row * 2 + col]] * 4, axis=1)
            gb[at : at + 64, :] = (piece * flags).astype(LOW)
    wo_copy.wait()
    dout[...] = dot_nt(gb[...], wo[...]).astype(LOW)
    for row in range(4):
        gkeys[row * 256 : row * 256 + 256, :] = jnp.zeros((256, 512), FULL)
        gvalues[row * 256 : row * 256 + 256, :] = jnp.zeros((256, 512), FULL)
    spread_word(2)
    relayed = []
    for row, line, peer in ((0, 3, north), (1, 0, south)):
        for side, col in ((0, 3), (1, 0)):
            to_lon[row * 2 + side].wait_recv()
            relayed.append(
                remote(
                    ext.at[1 + row, col], ext.at[line, col],
                    s_rel.at[row, side], v_rel.at[row, side], peer,
                )
            )
            relayed[-1].start()
    project(((1, 0), (2, 0), (1, 3), (2, 3)))
    place = ((0, 1), (1, 0), (1, 1), (2, 0))

    def write_bias(tile_rows):
        for tile_row in tile_rows:
            for tile_col in range(3):
                if (tile_row, tile_col) == (1, 1):
                    sides = centre
                else:
                    sides = mask_columns(tile_row, tile_col)
                for row in range(4):
                    for col in range(4):
                        if place[row][0] != tile_row or place[col][0] != tile_col:
                            continue
                        at = (row * 4 + col) * 64
                        flags = sides[place[col][1]][place[row][1] * 64 : place[row][1] * 64 + 64]
                        if row == 0:
                            flags = flags * has_north
                        if row == 3:
                            flags = flags * has_south
                        bias[at : at + 64, :] = (flags - 1.0) * 1000000000.0

    write_bias((1,))
    for index in range(4):
        for group in range(2):
            attend_early(index, group)
    for copy in mask_lat:
        copy.wait_recv()
    write_bias((0, 2))
    spread_word(3)
    for copy in to_lat:
        copy.wait_recv()
    project(((0, 1), (0, 2), (3, 1), (3, 2)))
    spread_word(4)
    for copy in relayed:
        copy.wait_recv()
    project(((0, 0), (0, 3), (3, 0), (3, 3)))

    def attend(index, group):
        at, lanes, spans, inner, slab, spare = shape_of(index, group)
        slot = index * 2 + group
        alive = jnp.max(oceans[index], axis=(0, 1), keepdims=True)
        for part in range(3):
            pscr[slot, part * 256 + spare : part * 256 + spare + 64, :] = jnp.zeros((64, 256), LOW)
        qbd = spread_heads(qs[at, lanes])
        dbd = spread_heads(dout[at, lanes])
        first, second = middle_parts(index)
        last = 3 - first - second
        scores = score(index, group, last, qbd)
        early_top = stats[slot, 0:1, :]
        top = jnp.maximum(jnp.max(scores, axis=0, keepdims=True), early_top)
        weights = jnp.exp(scores - top)
        shrink = jnp.exp(early_top - top)
        total = jnp.sum(weights, axis=0, keepdims=True) + shrink * stats[slot, 1:2, :]
        inverse = 1.0 / total
        for part in range(3):
            if part == last:
                probs = weights * inverse
            else:
                probs = probs_all[slot, part] * (shrink * inverse)
            probs_all[slot, part] = probs
            pscr[slot, inner[part], :] = probs.astype(LOW)
        out = fold(dot_tn(pscr[slot], values[slab, lanes]))
        mixed[at, lanes] = (out * alive).astype(LOW)
        for part in range(3):
            gvalues[spans[part], lanes] += dot_nn(pscr[slot, inner[part], :], dbd)

    def retreat(index, group):
        at, lanes, spans, inner, slab, spare = shape_of(index, group)
        slot = index * 2 + group
        side = index % 2
        for part in range(3):
            dscr[side, part * 256 + spare : part * 256 + spare + 64, :] = jnp.zeros((64, 256), LOW)
        qbd = spread_heads(qs[at, lanes])
        dbd = spread_heads(dout[at, lanes])
        gprobs = [dot_nt(values[span, lanes], dbd) for span in spans]
        deltas = [
            jnp.sum(probs_all[slot, part] * gprobs[part], axis=0, keepdims=True)
            for part in range(3)
        ]
        delta = deltas[0] + deltas[1] + deltas[2]
        for part in range(3):
            dscr[side, inner[part], :] = (
                probs_all[slot, part] * (gprobs[part] - delta)
            ).astype(LOW)
        gq[at, lanes] = (fold(dot_tn(dscr[side], keys[slab, lanes])) * 0.125).astype(LOW)
        for part in range(3):
            gkeys[spans[part], lanes] += dot_nn(dscr[side, inner[part], :], qbd)

    wgs = (wg_0, wg_1, wg_2, wg_3)
    r1s = (r1_0, r1_1, r1_2, r1_3)
    a1s = (a1_0, a1_1, a1_2, a1_3)
    r2s = (r2_0, r2_1, r2_2, r2_3)
    a2s = (a2_0, a2_1, a2_2, a2_3)
    r3s = (r3_0, r3_1, r3_2, r3_3)
    totals = (g5_0, g5_1, g5_2, g5_3)
    outputs = (sum_0, sum_1, sum_2, sum_3)

    def pair_copies(chunk):
        return [
            remote(
                wgs[chunk].at[part * 2 + 1 - core], r1s[chunk].at[part],
                s_pair.at[chunk, part], v_pair.at[chunk, part], partner,
            )
            for part in range(2)
        ]

    def plane_copy(chunk):
        def one(step):
            peer_hi, peer_lon = plane_peer(step)
            return remote(
                a1s[chunk].at[peer_hi * 8 + peer_lon], r2s[chunk].at[step - 1],
                s_plane.at[chunk, step - 1], v_plane.at[chunk, step - 1],
                (peer_lon, lat, peer_hi * 2 + core),
            )

        return one

    def z_copy(chunk):
        def one(step):
            return remote(
                a2s[chunk], r3s[chunk].at[step - 1],
                s_z.at[chunk, step - 1], v_z.at[chunk, step - 1], (lon, (lat + step) % 8, lev),
            )

        return one

    def all_copy(chunk):
        def one(step):
            return remote(
                totals[chunk].at[lon], totals[chunk].at[lon],
                s_all.at[chunk, step - 1], v_all.at[chunk, step - 1],
                ((lon + step) % 8, lat, lev),
            )

        return one

    def start_pair(chunk):
        for copy in pair_copies(chunk):
            copy.start()

    def pair_to_plane(chunk):
        for part, copy in enumerate(pair_copies(chunk)):
            copy.wait_recv()

            def add(piece, carry):
                span = pl.ds(pl.multiple_of(piece * 16, 16), 16)
                total = wgs[chunk][part * 2 + core, span, :] + r1s[chunk][part, span, :]
                a1s[chunk][part * 8 + piece] = total.astype(LOW)
                return carry

            lax.fori_loop(0, 8, add, 0)
        for step in range(1, 16):
            plane_copy(chunk)(step).start()

    def plane_to_z(chunk):
        for step in range(1, 16):
            plane_copy(chunk)(step).wait_recv()
        for first in range(0, WIDTHS[chunk], 256):
            cols = slice(first, first + 256)
            total = a1s[chunk][here, :, cols].astype(FULL)
            for step in range(15):
                total = total + r2s[chunk][step, :, cols].astype(FULL)
            a2s[chunk][:, cols] = total.astype(LOW)
        for step in range(1, 8):
            z_copy(chunk)(step).start()

    def z_to_all(chunk):
        for step in range(1, 8):
            z_copy(chunk)(step).wait_recv()
        for first in range(0, WIDTHS[chunk], 256):
            cols = slice(first, first + 256)
            total = a2s[chunk][:, cols].astype(FULL)
            for step in range(7):
                total = total + r3s[chunk][step, :, cols].astype(FULL)
            totals[chunk][lon, :, cols] = total.astype(LOW)
        for step in range(1, 8):
            all_copy(chunk)(step).start()

    corners = []
    edges = []
    for line, target, peer, side in ((0, from_south, north, 0), (3, from_north, south, 1)):
        for col in (0, 3):
            corners.append(
                remote(
                    ghalo.at[line, col], target.at[col],
                    s_gz.at[side, col], v_gz.at[side, col], peer,
                )
            )
        edges.append(
            remote(
                ghalo.at[line, pl.ds(1, 2)], target.at[pl.ds(1, 2)],
                s_gz.at[side, 1], v_gz.at[side, 1], peer,
            )
        )
    sideways = [
        remote(to_west, from_east, s_gx.at[0], v_gx.at[0], west),
        remote(to_east, from_west, s_gx.at[1], v_gx.at[1], east),
    ]
    sources = (from_north, from_south)

    def own_rows(row):
        return slice(row * 256 + 320, row * 256 + 448)

    def query_key_chunk(group):
        lanes = slice(group * 256, group * 256 + 256)
        for row in range(4):
            span = slice(row * 256, row * 256 + 256)
            low_keys[span, lanes] = gkeys[span, lanes].astype(LOW)
        query = dot_tn(hid[own_rows(0), :], gq[:128, lanes]) + dot_tn(
            hid[own_rows(1), :], gq[128:, lanes]
        )
        wgs[2 + group][:, :, :256] = query.reshape(4, 128, 256)
        wgs[2 + group][:, :, 256:] = dot_tn(hid[...], low_keys[:, lanes]).reshape(4, 128, 256)
        start_pair(2 + group)

    for group in range(2):
        for index in range(4):
            attend(index, group)
    wg_0[...] = dot_tn(mixed[...], gb[...]).reshape(4, 128, 512)
    start_pair(0)
    for row in range(4):
        span = slice(row * 256, row * 256 + 256)
        low_values[span, :] = gvalues[span, :].astype(LOW)
    wg_1[...] = dot_tn(hid[...], low_values[...]).reshape(4, 128, 512)
    start_pair(1)
    retreat(0, 0)
    retreat(1, 0)
    pair_to_plane(0)
    retreat(2, 0)
    pair_to_plane(1)
    retreat(3, 0)
    query_key_chunk(0)
    for row in range(4):
        span = slice(row * 256, row * 256 + 256)
        ghidden[span, :] = dot_nt(low_values[span, :], wq[:, 1024:])
    retreat(0, 1)
    retreat(1, 1)
    retreat(2, 1)
    pair_to_plane(2)
    retreat(3, 1)
    query_key_chunk(1)
    plane_to_z(0)
    for row in (0, 3, 1, 2):
        span = slice(row * 256, row * 256 + 256)
        total = ghidden[span, :] + dot_nt(low_keys[span, :], wq[:, 512:1024])
        if row in (1, 2):
            ghidden[span, :] = total
        for col in range(4):
            if row in (0, 3) or col in (0, 3):
                ghalo[row, col] = total[col * 64 : col * 64 + 64].astype(LOW)
        if row == 3:
            for copy in corners:
                copy.start()
            pair_to_plane(3)
            plane_to_z(1)
    for copy in edges:
        copy.start()
    for copy in corners:
        copy.wait_recv()
    for row in range(2):
        to_west[row] = (
            ghalo[1 + row, 0].astype(FULL) + sources[row][0].astype(FULL)
        ).astype(LOW)
        to_east[row] = (
            ghalo[1 + row, 3].astype(FULL) + sources[row][3].astype(FULL)
        ).astype(LOW)
    for copy in sideways:
        copy.start()
    z_to_all(0)
    plane_to_z(2)
    z_to_all(1)
    branch = dot_nn(mixed[...], wo[...])
    for row in range(2):
        pieces = []
        for col in range(2):
            index = row * 2 + col
            flags = jnp.concatenate([oceans[index]] * 4, axis=1)
            tokens = ext[1 + row, 1 + col].astype(FULL).reshape(64, 512)
            result = tokens + flags * branch[index * 64 : index * 64 + 64]
            pieces.append(result.reshape(8, 8, 512))
        layer_buf[0, row * 8 : row * 8 + 8] = jnp.concatenate(pieces, axis=1).astype(LOW)
    layer_copy = pltpu.make_async_copy(layer_buf, layer_ref, out_sem.at[0])
    layer_copy.start()
    grad_query = dot_nt(gq[...], wq[:, :512])
    plane_to_z(3)
    z_to_all(2)
    z_to_all(3)
    for copy in edges + sideways:
        copy.wait_recv()
    for row in range(2):
        pieces = []
        cot = cots[row * 8 : row * 8 + 8].astype(FULL)
        for col in range(2):
            index = row * 2 + col
            at = ((1 + row) * 4 + 1 + col) * 64
            side = (from_west, from_east)[col]
            grad_hidden = (
                grad_query[index * 64 : index * 64 + 64]
                + ghidden[at : at + 64, :]
                + sources[row][1 + col].astype(FULL)
                + side[row].astype(FULL)
            )
            normed, scaling = norm_rows(ext[1 + row, 1 + col].astype(FULL).reshape(64, 512))
            scaled = grad_hidden * gain
            correction = (
                scaled
                - jnp.mean(scaled, axis=-1, keepdims=True)
                - normed * jnp.mean(scaled * normed, axis=-1, keepdims=True)
            )
            result = cot[:, col * 8 : col * 8 + 8, :].reshape(64, 512) + scaling * correction
            pieces.append(result.reshape(8, 8, 512))
        grad_buf[0, row * 8 : row * 8 + 8] = jnp.concatenate(pieces, axis=1).astype(LOW)
    grad_copy = pltpu.make_async_copy(grad_buf, grad_ref, out_sem.at[1])
    grad_copy.start()
    sum_copies = [
        pltpu.make_async_copy(totals[chunk], outputs[chunk], out_sem.at[2 + chunk])
        for chunk in range(4)
    ]
    for chunk in range(4):
        for step in range(1, 8):
            all_copy(chunk)(step).wait_recv()
        sum_copies[chunk].start()
    sent = mask_lon + to_lon + to_lat + mask_lat + relayed + corners + edges + sideways
    for chunk in range(4):
        sent += pair_copies(chunk)
        sent += [plane_copy(chunk)(step) for step in range(1, 16)]
        sent += [z_copy(chunk)(step) for step in range(1, 8)]
        sent += [all_copy(chunk)(step) for step in range(1, 8)]
    for copy in sent:
        copy.wait_send()
    for copy in [layer_copy, grad_copy] + sum_copies:
        copy.wait()


def layer(tokens_in, cotangent, qkv_weight, out_weight, gain, ocean_mask):
    dma = pltpu.SemaphoreType.DMA
    hbm = pl.BlockSpec(memory_space=pltpu.HBM)
    scratch = [
        pltpu.VMEM((4, 4, 8, 8, 512), LOW),
        pltpu.VMEM((3, 3, 16, 16), jnp.int32),
        pltpu.VMEM((16, 16, 512), LOW),
        pltpu.VMEM((512, 1536), LOW),
        pltpu.VMEM((512, 512), LOW),
        pltpu.VMEM((1, 512), FULL),
        pltpu.VMEM((1, 16, 16, 512), LOW),
        pltpu.VMEM((1, 16, 16, 512), LOW),
        pltpu.VMEM((8, 8, 256), FULL),
    ]
    scratch += [pltpu.VMEM((1024, 512), LOW)] * 3
    scratch += [pltpu.VMEM((1024, 512), FULL)] * 2
    scratch += [pltpu.VMEM((1024, 512), LOW)] * 2
    scratch += [pltpu.VMEM((1024, 512), FULL), pltpu.VMEM((4, 4, 64, 512), LOW)]
    scratch += [pltpu.VMEM((256, 512), LOW)] * 5
    scratch += [pltpu.VMEM((8, 3, 192, 256), FULL)]
    scratch += [pltpu.VMEM((8, 768, 256), LOW), pltpu.VMEM((2, 768, 256), LOW)]
    scratch += [pltpu.VMEM((1024, 128), FULL)]
    scratch += [pltpu.VMEM((4, 128, width), FULL) for width in WIDTHS]
    scratch += [pltpu.VMEM((2, 128, width), FULL) for width in WIDTHS]
    scratch += [pltpu.VMEM((16, 16, width), LOW) for width in WIDTHS]
    scratch += [pltpu.VMEM((15, 16, width), LOW) for width in WIDTHS]
    scratch += [pltpu.VMEM((16, width), LOW) for width in WIDTHS]
    scratch += [pltpu.VMEM((7, 16, width), LOW) for width in WIDTHS]
    scratch += [pltpu.VMEM((8, 16, width), LOW) for width in WIDTHS]
    scratch += [pltpu.VMEM((4, 64, 512), LOW)] * 2
    scratch += [pltpu.VMEM((2, 64, 512), LOW)] * 4
    scratch += [pltpu.SemaphoreType.REGULAR((4,))]
    scratch += [dma((9,)), dma((6,))] + [dma((2, 2))] * 6 + [dma((4,))] * 2
    scratch += [dma((4, 2))] * 2 + [dma((4, 15))] * 2 + [dma((4, 7))] * 4
    scratch += [dma((2, 4))] * 2 + [dma((2,))] * 2
    return pl.pallas_call(
        layer_kernel,
        out_shape=(
            jax.ShapeDtypeStruct((1, 16, 16, 512), LOW),
            jax.ShapeDtypeStruct((1, 16, 16, 512), LOW),
        )
        + tuple(jax.ShapeDtypeStruct((8, 16, width), LOW) for width in WIDTHS),
        in_specs=[hbm] * 6,
        out_specs=(hbm,) * 6,
        scratch_shapes=scratch,
        compiler_params=pltpu.CompilerParams(
            collective_id=0, has_side_effects=True, vmem_limit_bytes=WHOLE_VMEM
        ),
    )(tokens_in, cotangent, qkv_weight, out_weight, gain, ocean_mask)


def finish_kernel(
    layer_ref, grad_ref, sum_0, sum_1, sum_2, sum_3, wqkv_ref, gain_ref,
    layer_out, grad_out, qkv_out, out_out, gain_out,
    layer_buf, grad_buf, buf_0, buf_1, buf_2, buf_3, rows, gains, qkv, outs, line_buf, in_sem,
    out_sem,
):
    lev = lax.axis_index("lev")
    first = pl.multiple_of(lev * 128, 128)
    pairs = (
        (sum_2, buf_2), (sum_3, buf_3), (sum_1, buf_1), (sum_0, buf_0), (wqkv_ref.at[pl.ds(first, 128)], rows),
        (gain_ref, gains), (layer_ref, layer_buf), (grad_ref, grad_buf),
    )
    fetches = [
        pltpu.make_async_copy(src, dst, in_sem.at[slot]) for slot, (src, dst) in enumerate(pairs)
    ]
    for copy in fetches:
        copy.start()
    stores = [
        pltpu.make_async_copy(src, dst, out_sem.at[slot])
        for slot, (src, dst) in enumerate(
            (
                (qkv, qkv_out), (outs, out_out), (layer_buf, layer_out), (grad_buf, grad_out),
                (line_buf, gain_out),
            )
        )
    ]
    for group, source in enumerate((buf_2, buf_3)):
        fetches[group].wait()
        for part in range(2):
            at = part * 512 + group * 256
            qkv[:, at : at + 256] = (
                source[:, :, part * 256 : part * 256 + 256].reshape(128, 256).astype(FULL)
            )
    fetches[2].wait()
    qkv[:, 1024:] = buf_1[...].reshape(128, 512).astype(FULL)
    stores[0].start()
    fetches[3].wait()
    outs[...] = buf_0[...].reshape(128, 512).astype(FULL)
    stores[1].start()
    fetches[6].wait()
    stores[2].start()
    fetches[7].wait()
    stores[3].start()
    fetches[4].wait()
    fetches[5].wait()
    total = jnp.sum(rows[...].astype(FULL) * qkv[...], axis=1, keepdims=True)
    line = jnp.transpose(jnp.broadcast_to(total, (128, 128)))[:1]
    line_buf[...] = line / gains[:, pl.ds(first, 128)]
    stores[4].start()
    for copy in stores:
        copy.wait()


def finish_outputs(parts, qkv_weight, gain):
    hbm = pl.BlockSpec(memory_space=pltpu.HBM)
    dma = pltpu.SemaphoreType.DMA
    return pl.pallas_call(
        finish_kernel,
        out_shape=(
            jax.ShapeDtypeStruct((1, 16, 16, 512), LOW),
            jax.ShapeDtypeStruct((1, 16, 16, 512), LOW),
            jax.ShapeDtypeStruct((128, 1536), FULL),
            jax.ShapeDtypeStruct((128, 512), FULL),
            jax.ShapeDtypeStruct((1, 128), FULL),
        ),
        in_specs=[hbm] * 8,
        out_specs=(hbm,) * 5,
        scratch_shapes=[pltpu.VMEM((1, 16, 16, 512), LOW)] * 2
        + [pltpu.VMEM((8, 16, width), LOW) for width in WIDTHS]
        + [
            pltpu.VMEM((128, 1536), LOW), pltpu.VMEM((1, 512), FULL),
            pltpu.VMEM((128, 1536), FULL), pltpu.VMEM((128, 512), FULL),
            pltpu.VMEM((1, 128), FULL), dma((8,)), dma((5,)),
        ],
        compiler_params=pltpu.CompilerParams(vmem_limit_bytes=WHOLE_VMEM),
    )(*parts, qkv_weight, gain)


def on_device(tokens_in, cotangent, qkv_weight, out_weight, norm_gain, ocean_mask):
    gain = norm_gain.reshape(1, 512)
    parts = layer(tokens_in, cotangent, qkv_weight, out_weight, gain, ocean_mask)
    layer_out, input_grad, qkv_grad, out_grad, gain_grad = finish_outputs(parts, qkv_weight, gain)
    return (layer_out, input_grad, qkv_grad, out_grad, gain_grad.reshape(128))


def solution(mesh):
    placed = (
        P("lev", "lat", "lon", None),
        P("lev", "lat", "lon", None),
        P(),
        P(),
        P(),
        P("lev", "lat", "lon"),
    )
    return jax.shard_map(
        on_device,
        mesh=mesh,
        in_specs=placed,
        out_specs=(
            P("lev", "lat", "lon", None),
            P("lev", "lat", "lon", None),
            P("lev", None),
            P("lev", None),
            P("lev"),
        ),
        check_vma=False,
    )
```
